32 devices in a mesh: lat: 4 (over x, core), lev: 8 (over z, y).
Axes of the slice: x: 2, y: 2, z: 4, core: 2. Of those that a mesh axis runs over, the one named last changes fastest.
Arguments:
- prognostic_arrays: float32 [16, 3, 32, 2688], P(None, None, ('lat', 'lev')), may hold values from -6 to 6
- coriolis: float32 [32], P(('lat', 'lev')), may hold values from -1.5 to 1.5
- weights: float32 [32], P(('lat', 'lev')), may hold values from 0.5 to 2
- row_points: int32 [32], P(('lat', 'lev')), may hold values from 196 to 2688, as said below
- owner_pairs: int32 [8, 6], replicated, may hold values from 0 to 47, as said below
- legendre: bfloat16 [8, 6, 97, 32], P('lev', None, None, 'lat'), may hold values from -2 to 2
- depths: float32 [16], replicated, may hold values from 0.5 to 8
- diffusion: float32 [16], replicated, may hold values from 0.5 to 8
Outputs:
- updated: float32 [16, 3, 32, 2688], P(None, None, ('lat', 'lev'))
The draws below stay inside these ranges and needn't reach their ends.
Inputs may be any that keep to these rules, and one draw needn't show every extreme that they name: `owner_pairs`: a permutation of the pair indices 0 .. 47, 6 to each owner; pair s stands for the wavenumbers s and 95 - s. `row_points`: multiples of 4; some row has exactly 2688 points and some exactly 196.
All inputs are finite; a program needn't handle non-finite values.
Results may differ from the reference program's by a relative error of at most 0.0058.
Values may be sent and summed in bfloat16 or wider, within the bound.
No kernel may reach another device: no remote copies, remote signals or barrier semaphores. Data moves between devices by JAX's collectives and lax.ppermute only.
A program may use at most 64 MiB of HBM per device.

```python
import math
import jax
import jax.numpy as jnp
from jax import lax

L = 16
PG = 6
NLON = 2688
M = 96
NLAT = 32
N_LEV = 8


def draw_owner_pairs(key, part):
    shuffled = jax.random.permutation(jax.random.fold_in(key, 17), M // 2)
    return shuffled.reshape(-1, PG).astype(jnp.int32)


def draw_row_points(key, part):
    first_key, second_key = jax.random.split(jax.random.fold_in(key, 29))
    lowered = jax.random.randint(first_key, (NLAT,), 0, (NLON - 2 * M) // 4)
    points = NLON - 4 * lowered
    chosen = jax.random.permutation(second_key, NLAT)[:2]
    points = points.at[chosen[0]].set(NLON).at[chosen[1]].set(2 * M + 4)
    return points.astype(jnp.int32)


def level_of(own_key, extent, cuts, least, high):
    factor_of = 1.0
    for axis_at, blocks in cuts:
        heights = jax.random.uniform(jax.random.fold_in(jax.random.fold_in(own_key, 6), axis_at), (blocks,), jnp.float32, least / len(cuts), high / len(cuts))
        factor_of = factor_of * jnp.repeat(jnp.exp(heights), extent[axis_at] // blocks).reshape((-1,) + (1,) * (len(extent) - 1 - axis_at))
    return factor_of


def gaussian(key, dims, scale, most, cuts=(), held_as=jnp.bfloat16):
    factor_of = level_of(key, dims, cuts, -0.22, 0.18) if cuts else 1.0
    entries = jax.random.normal(key, dims, jnp.float32) * scale * factor_of
    return jnp.minimum(jnp.maximum(entries, -most), most).astype(held_as)


def setup_inputs(seed: int = 0) -> dict:
    key_of = jax.random.split(jax.random.key(seed), 9)
    prognostic_arrays = gaussian(key_of[0], (L, 3, NLAT, NLON), 1.0, 6.0, ((2, 32),), jnp.float32)
    coriolis = jnp.clip(jax.random.uniform(key_of[1], (NLAT,), jnp.float32, -1.5, 1.5) * level_of(key_of[1], (NLAT,), ((0, 32),), -0.4, 0.0), -1.5, 1.5)
    weights = jnp.clip(jnp.exp(math.log(2.0) - 1.3862944 * jax.random.uniform(key_of[2], (NLAT,), jnp.float32) ** level_of(key_of[2], (NLAT,), ((0, 32),), -0.2, 0.2)), 0.5, 2.0)
    row_points = draw_row_points(jax.random.fold_in(key_of[8], 71), 0)
    owner_pairs = draw_owner_pairs(jax.random.fold_in(key_of[8], 71), 0)
    legendre = gaussian(key_of[5], (N_LEV, PG, M + 1, NLAT), (M * (NLAT * NLON ** -1) ** 0.5) ** -0.5, 2.0, ((0, 8), (3, 4)))
    depths = jnp.clip(jnp.exp(jax.random.uniform(key_of[6], (L,), jnp.float32, math.log(0.5), math.log(8.0))), 0.5, 8.0)
    diffusion = jnp.clip(jnp.exp(jax.random.uniform(key_of[7], (L,), jnp.float32, math.log(0.5), math.log(8.0))), 0.5, 8.0)
    return dict(prognostic_arrays=prognostic_arrays, coriolis=coriolis, weights=weights, row_points=row_points, owner_pairs=owner_pairs, legendre=legendre, depths=depths, diffusion=diffusion)


stepsize_delta = 0.5


def tendencies(prognostic_arrays, coriolis):
    vorticity = prognostic_arrays[:, 0]
    spreading_rate_grid = prognostic_arrays[:, 1]
    thermal_state_grid = prognostic_arrays[:, 2]
    rotation = coriolis[None, :, None]
    advanced_curl_rate = vorticity - stepsize_delta * (rotation + vorticity) * spreading_rate_grid
    advanced_spreading_rate = spreading_rate_grid + stepsize_delta * (rotation * vorticity - spreading_rate_grid * spreading_rate_grid)
    advanced_thermal_state = thermal_state_grid - stepsize_delta * thermal_state_grid * spreading_rate_grid
    return jnp.stack([advanced_curl_rate, advanced_spreading_rate, advanced_thermal_state], axis=1).astype(jnp.bfloat16)


def owner_waves(owner_pairs, highest):
    return jnp.stack([owner_pairs, highest - 1 - owner_pairs], axis=1)


def phase_table(points, wavenumbers, lon_count):
    positions = jnp.arange(lon_count, dtype=jnp.int32)
    product = (positions[None, :, None] * wavenumbers[None, None, :]) % points[:, None, None]
    angle = product.astype(jnp.float32) * (2.0 * math.pi / points.astype(jnp.float32))[:, None, None]
    return jnp.stack([jnp.cos(angle), -jnp.sin(angle)], axis=2).astype(jnp.bfloat16)


def valid_points(points, lon_count):
    positions = jnp.arange(lon_count, dtype=jnp.int32)
    return positions[None, :] < points[:, None]


def half_mask(my_pairs, slot_total):
    positions = jnp.arange(slot_total, dtype=jnp.int32)
    return positions[None, :] < (slot_total - 1 - my_pairs)[:, None]


def implicit(summed, my_pairs, depth_part, diff_part):
    slot_total = summed.shape[3]
    slot_count = summed.shape[2]
    highest = slot_total - 1
    positions = jnp.arange(slot_total, dtype=jnp.int32)[None, :]
    first_half = positions < (highest - my_pairs)[:, None]
    total = jnp.where(first_half, my_pairs[:, None] + positions, positions - 1).astype(jnp.float32)
    harmonic_operator_spectrum = total * (total + 1.0) / float(highest * highest)
    bundled_prognostics = summed.reshape(-1, 3, 2, slot_count, slot_total)
    vorticity = bundled_prognostics[:, 0]
    spreading_rate_grid = bundled_prognostics[:, 1]
    thermal_state_grid = bundled_prognostics[:, 2]
    layer_stack_count = depth_part[:, None, None, None]
    diff_cols = diff_part[:, None, None, None]
    advanced_curl_rate = vorticity / (1.0 + diff_cols * harmonic_operator_spectrum * harmonic_operator_spectrum)
    advanced_spreading_rate = (spreading_rate_grid + harmonic_operator_spectrum * thermal_state_grid) / (1.0 + layer_stack_count * harmonic_operator_spectrum)
    advanced_thermal_state = thermal_state_grid - layer_stack_count * advanced_spreading_rate
    piled_prognostics = jnp.stack([advanced_curl_rate, advanced_spreading_rate, advanced_thermal_state], axis=1)
    return piled_prognostics.reshape(summed.shape).astype(jnp.bfloat16)


def direct_ref(band_block, legendre_block, my_pairs):
    both_halves = jnp.einsum('lkqht,tpl->kqhtp', band_block.astype(jnp.float32), legendre_block.astype(jnp.float32))
    first_half = half_mask(my_pairs, legendre_block.shape[1])
    return jnp.where(first_half, both_halves[:, :, 0], both_halves[:, :, 1])


def inverse_ref(solved, legendre_block, my_pairs):
    slot_total = legendre_block.shape[1]
    first_half = half_mask(my_pairs, slot_total)
    half_masks = jnp.stack([first_half, jnp.logical_not(first_half)], axis=0)
    masked_spec = jnp.where(half_masks[None, None], solved[:, :, None], jnp.zeros((), solved.dtype))
    inverted = jnp.einsum('kqhtp,tpl->lkqht', masked_spec.astype(jnp.float32), legendre_block.astype(jnp.float32))
    doubling = jnp.where(owner_waves(my_pairs[None], slot_total - 1)[0] == 0, 1.0, 2.0).astype(jnp.float32)
    return (inverted * doubling[None, None, None]).astype(jnp.bfloat16)


def reference(prognostic_arrays, coriolis, weights, row_points, owner_pairs, legendre, depths, diffusion):
    levels = prognostic_arrays.shape[0]
    row_total = prognostic_arrays.shape[2]
    lon_count = prognostic_arrays.shape[3]
    group_count = owner_pairs.shape[0]
    slot_count = owner_pairs.shape[1]
    highest = legendre.shape[2] - 1
    channels = levels * 3
    wavenumbers = owner_waves(owner_pairs, highest).reshape(-1)
    valid = valid_points(row_points, lon_count)
    gridded = tendencies(prognostic_arrays, coriolis).reshape(channels, row_total, lon_count)
    gridded = jnp.where(valid[None], gridded, jnp.zeros((), gridded.dtype))
    row_scale = weights / row_points.astype(jnp.float32)

    def forward_row(inputs):
        row_data, points, factor = inputs
        phases = phase_table(points[None], wavenumbers, lon_count)[0]
        out = jnp.einsum('cx,xqk->cqk', row_data.astype(jnp.float32), phases.astype(jnp.float32))
        return (out * factor).astype(jnp.bfloat16)

    fourier = lax.map(forward_row, (jnp.moveaxis(gridded, 1, 0), row_points, row_scale))
    fourier = fourier.reshape(row_total, channels, 2, group_count, 2, slot_count)

    def per_owner(owner):
        band_block = lax.dynamic_index_in_dim(fourier, owner, 3, keepdims=False)
        legendre_block = lax.dynamic_index_in_dim(legendre, owner, 0, keepdims=False)
        my_pairs = lax.dynamic_index_in_dim(owner_pairs, owner, 0, keepdims=False)
        summed = direct_ref(band_block, legendre_block, my_pairs)
        solved = implicit(summed, my_pairs, depths, diffusion)
        return inverse_ref(solved, legendre_block, my_pairs)

    inverted = lax.map(per_owner, jnp.arange(group_count, dtype=jnp.int32))
    inverted = jnp.transpose(inverted, (1, 2, 3, 0, 4, 5)).reshape(row_total, channels, 2, -1)

    def inverse_row(inputs):
        coeff_row, points = inputs
        phases = phase_table(points[None], wavenumbers, lon_count)[0]
        return jnp.einsum('cqk,xqk->cx', coeff_row.astype(jnp.float32), phases.astype(jnp.float32))

    outgrid = jnp.moveaxis(lax.map(inverse_row, (inverted, row_points)), 0, 1)
    outgrid = jnp.where(valid[None], outgrid, jnp.zeros((), outgrid.dtype))
    return outgrid.reshape(levels, 3, row_total, lon_count)
```

```python
import functools
import math

import jax
import jax.numpy as jnp
from jax import lax
from jax.experimental import pallas as pl
from jax.experimental.pallas import tpu as pltpu
from jax.sharding import PartitionSpec as P

stepsize_delta = 0.5


def tendencies(prognostic_arrays, coriolis):
    vorticity = prognostic_arrays[:, 0]
    spreading_rate_grid = prognostic_arrays[:, 1]
    thermal_state_grid = prognostic_arrays[:, 2]
    rotation = coriolis[None, :, None]
    advanced_curl_rate = vorticity - stepsize_delta * (rotation + vorticity) * spreading_rate_grid
    advanced_spreading_rate = spreading_rate_grid + stepsize_delta * (
        rotation * vorticity - spreading_rate_grid * spreading_rate_grid
    )
    advanced_thermal_state = (
        thermal_state_grid - stepsize_delta * thermal_state_grid * spreading_rate_grid
    )
    return jnp.stack(
        [advanced_curl_rate, advanced_spreading_rate, advanced_thermal_state], axis=1
    ).astype(jnp.bfloat16)


def owner_waves(owner_pairs, highest):
    return jnp.stack([owner_pairs, highest - 1 - owner_pairs], axis=1)


def phase_table(points, wavenumbers, lon_count):
    positions = jnp.arange(lon_count, dtype=jnp.int32)
    product = positions[None, :, None] * wavenumbers[None, None, :] % points[:, None, None]
    angle = (
        product.astype(jnp.float32) * (2.0 * math.pi / points.astype(jnp.float32))[:, None, None]
    )
    return jnp.stack([jnp.cos(angle), -jnp.sin(angle)], axis=2).astype(jnp.bfloat16)


def valid_points(points, lon_count):
    positions = jnp.arange(lon_count, dtype=jnp.int32)
    return positions[None, :] < points[:, None]


def half_mask(my_pairs, slot_total):
    positions = jnp.arange(slot_total, dtype=jnp.int32)
    return positions[None, :] < (slot_total - 1 - my_pairs)[:, None]


def implicit(summed, my_pairs, depth_part, diff_part):
    slot_total = summed.shape[3]
    slot_count = summed.shape[2]
    highest = slot_total - 1
    positions = jnp.arange(slot_total, dtype=jnp.int32)[None, :]
    first_half = positions < (highest - my_pairs)[:, None]
    total = jnp.where(first_half, my_pairs[:, None] + positions, positions - 1).astype(jnp.float32)
    harmonic_operator_spectrum = total * (total + 1.0) / float(highest * highest)
    bundled_prognostics = summed.reshape(-1, 3, 2, slot_count, slot_total)
    vorticity = bundled_prognostics[:, 0]
    spreading_rate_grid = bundled_prognostics[:, 1]
    thermal_state_grid = bundled_prognostics[:, 2]
    layer_stack_count = depth_part[:, None, None, None]
    diff_cols = diff_part[:, None, None, None]
    advanced_curl_rate = vorticity / (
        1.0 + diff_cols * harmonic_operator_spectrum * harmonic_operator_spectrum
    )
    advanced_spreading_rate = (
        spreading_rate_grid + harmonic_operator_spectrum * thermal_state_grid
    ) / (1.0 + layer_stack_count * harmonic_operator_spectrum)
    advanced_thermal_state = thermal_state_grid - layer_stack_count * advanced_spreading_rate
    piled_prognostics = jnp.stack(
        [advanced_curl_rate, advanced_spreading_rate, advanced_thermal_state], axis=1
    )
    return piled_prognostics.reshape(summed.shape).astype(jnp.bfloat16)


def general_body(
    prognostic_arrays, coriolis, weights, row_points, owner_pairs, legendre, depths, diffusion
):
    levels = prognostic_arrays.shape[0]
    row_count = prognostic_arrays.shape[2]
    lon_count = prognostic_arrays.shape[3]
    group_count = owner_pairs.shape[0]
    slot_count = owner_pairs.shape[1]
    local_basis = legendre[0]
    slot_total = local_basis.shape[1]
    highest = slot_total - 1
    channels = levels * 3
    packed = channels * 4 * slot_count
    wavenumbers = owner_waves(owner_pairs, highest).reshape(-1)
    valid = valid_points(row_points, lon_count)
    gridded = tendencies(prognostic_arrays, coriolis).reshape(channels, row_count, lon_count)
    gridded = jnp.where(valid[None], gridded, jnp.zeros((), gridded.dtype))
    phases = phase_table(row_points, wavenumbers, lon_count).reshape(
        row_count, lon_count, 2, group_count, 2, slot_count
    )
    row_scale = weights / row_points.astype(jnp.float32)
    fourier = jnp.einsum("crx,rxqght->grcqht", gridded, phases, preferred_element_type=jnp.float32)
    fourier = (fourier * row_scale[None, :, None, None, None, None]).astype(jnp.bfloat16)
    band_data = lax.all_to_all(
        fourier.reshape(group_count, row_count, packed),
        "lev",
        split_axis=0,
        concat_axis=0,
        tiled=True,
    )
    band_block = band_data.reshape(group_count * row_count, channels, 2, 2, slot_count)
    owner_index = lax.axis_index("lev")
    my_pairs = lax.dynamic_index_in_dim(owner_pairs, owner_index, 0, keepdims=False)
    first_half = half_mask(my_pairs, slot_total)
    half_masks = jnp.stack([first_half, jnp.logical_not(first_half)], axis=0)
    doubling = jnp.where(owner_waves(my_pairs[None], highest)[0] == 0, 1.0, 2.0).astype(jnp.float32)
    both_halves = jnp.einsum(
        "lkqht,tpl->kqhtp", band_block, local_basis, preferred_element_type=jnp.float32
    )
    summed = lax.psum(jnp.where(first_half, both_halves[:, :, 0], both_halves[:, :, 1]), "lat")
    solved = implicit(summed, my_pairs, depths, diffusion)
    masked_spec = jnp.where(half_masks[None, None], solved[:, :, None], jnp.zeros((), solved.dtype))
    inverted = jnp.einsum(
        "kqhtp,tpl->lkqht", masked_spec, local_basis, preferred_element_type=jnp.float32
    )
    inverted = (inverted * doubling[None, None, None]).astype(jnp.bfloat16)
    returned = lax.all_to_all(
        inverted.reshape(group_count, row_count, packed),
        "lev",
        split_axis=0,
        concat_axis=0,
        tiled=True,
    )
    returned = returned.reshape(group_count, row_count, channels, 2, 2, slot_count)
    outgrid = jnp.einsum("grcqht,rxqght->crx", returned, phases, preferred_element_type=jnp.float32)
    outgrid = jnp.where(valid[None], outgrid, jnp.zeros((), outgrid.dtype))
    return outgrid.reshape(levels, 3, row_count, lon_count)


lane_count = 128
piece_rows = 8


def turn_cos_sin(turns, quarter):
    scaled = turns * 4.0
    nearest = jnp.floor(scaled + 0.5)
    arc = (scaled - nearest) * (0.5 * math.pi)
    square = arc * arc
    sine = arc + arc * square * (
        -1.6666654611e-1 + square * (8.3321608736e-3 + square * -1.9515295891e-4)
    )
    cosine = (
        1.0
        - 0.5 * square
        + square
        * square
        * (4.166664568298827e-2 + square * (-1.388731625493765e-3 + square * 2.443315711809948e-5))
    )
    turn = nearest + quarter
    turn = turn - 4.0 * jnp.floor(turn * 0.25)
    swapped = jnp.logical_or(turn == 1.0, turn == 3.0)
    cos_part = jnp.where(swapped, sine, cosine)
    sin_part = jnp.where(swapped, cosine, sine)
    cos_part = jnp.where(jnp.logical_or(turn == 1.0, turn == 2.0), -cos_part, cos_part)
    sin_part = jnp.where(turn >= 2.0, -sin_part, sin_part)
    return cos_part, sin_part


def turns_of(product, points, inverse):
    rest = product - jnp.floor(product * inverse) * points
    rest = jnp.where(rest < 0.0, rest + points, rest)
    rest = jnp.where(rest >= points, rest - points, rest)
    return rest * inverse


def analysis_kernel(
    dims,
    grid_hbm,
    coriolis_ref,
    weights_ref,
    points_ref,
    pairs_ref,
    legendre_ref,
    sent_ref,
    table_ref,
    grid_ref,
    rhs_ref,
    wave_ref,
    sem,
):
    levels, lon_count, group_count, slot_count, parts, per_part, highest = dims
    channels = 3 * levels
    blocks = lon_count // lane_count
    active = slot_count // per_part
    copy = pltpu.make_async_copy(grid_hbm, grid_ref, sem)
    copy.start()

    tile = (piece_rows, lane_count)
    points = points_ref[0]
    points_vec = jnp.full(tile, points, jnp.int32).astype(jnp.float32)
    inverse = 1.0 / points_vec
    row = lax.broadcasted_iota(jnp.int32, tile, 0)
    lane = lax.broadcasted_iota(jnp.int32, tile, 1)
    lane_float = lane.astype(jnp.float32)
    quarter = (row // (2 * per_part)).astype(jnp.float32)
    second_half = (row // per_part) % 2 == 1
    slot = row % per_part
    for part in range(active):
        for group in range(group_count):
            pair = jnp.full(tile, pairs_ref[group, part * per_part], jnp.int32)
            for other in range(1, per_part):
                pair = jnp.where(slot == other, pairs_ref[group, part * per_part + other], pair)
            wave = jnp.where(second_half, highest - 1 - pair, pair).astype(jnp.float32)
            near_cos, near_sin = turn_cos_sin(
                turns_of(wave * lane_float, points_vec, inverse), quarter
            )
            far_cos, far_sin = turn_cos_sin(
                turns_of(wave * (lane_float * float(lane_count)), points_vec, inverse),
                jnp.zeros(tile, jnp.float32),
            )
            at = (part * group_count + group) * piece_rows
            for block in range(blocks):
                turned = (
                    near_cos * far_cos[:, block : block + 1]
                    - near_sin * far_sin[:, block : block + 1]
                )
                table_ref[at : at + piece_rows, block * lane_count : (block + 1) * lane_count] = (
                    turned.astype(jnp.bfloat16)
                )

    copy.wait()
    rotation = coriolis_ref[0]
    lane_wide = lax.broadcasted_iota(jnp.int32, (levels, lane_count), 1)
    for block in range(blocks):
        vorticity, spreading, thermal = (
            grid_ref[pl.ds(field * blocks + block, levels, stride=3 * blocks), :]
            for field in range(3)
        )
        inside = lane_wide < points - block * lane_count
        advanced = (
            vorticity - stepsize_delta * (rotation + vorticity) * spreading,
            spreading + stepsize_delta * (rotation * vorticity - spreading * spreading),
            thermal - stepsize_delta * thermal * spreading,
        )
        for field in range(3):
            rhs_ref[
                field * levels : (field + 1) * levels,
                block * lane_count : (block + 1) * lane_count,
            ] = jnp.where(inside, advanced[field], 0.0).astype(jnp.bfloat16)

    summed = lax.dot_general(
        table_ref[...],
        rhs_ref[...],
        (((1,), (1,)), ((), ())),
        preferred_element_type=jnp.float32,
    )
    wave_ref[:, :channels] = summed
    scale = jnp.full(tile, weights_ref[0], jnp.float32) / points_vec
    slot_total = highest + 1
    left = lane_count - channels
    for part in range(active):
        first = jnp.pad(
            legendre_ref[0, part * per_part].astype(jnp.float32),
            ((0, 0), (0, lane_count - slot_total)),
        )
        second = jnp.pad(
            legendre_ref[0, part * per_part + 1].astype(jnp.float32),
            ((0, 0), (0, lane_count - slot_total)),
        )
        upper_basis = pltpu.roll(first, channels, 1)
        lower = jnp.where(
            lane < slot_total, second, pltpu.roll(first, (slot_total - left) % lane_count, 1)
        )
        for group in range(group_count):
            at = part * group_count + group
            upper = jnp.where(
                lane < channels,
                wave_ref[at * piece_rows : (at + 1) * piece_rows, :] * scale,
                upper_basis,
            )
            sent_ref[at] = jnp.concatenate([upper, lower], axis=0).astype(jnp.bfloat16)
    for at in range(active * group_count, parts * group_count):
        sent_ref[at] = jnp.zeros((2 * piece_rows, lane_count), jnp.bfloat16)


def spectral_kernel(
    dims,
    received_ref,
    position_ref,
    pairs_ref,
    depths_ref,
    diffusion_ref,
    sent_ref,
    wave_ref,
):
    levels, lon_count, group_count, slot_count, parts, per_part, highest = dims
    channels = 3 * levels
    slot_total = highest + 1
    left = lane_count - channels
    sources = parts * group_count
    part, group = position_ref[0], position_ref[1]
    tile = (piece_rows, lane_count)
    lane = lax.broadcasted_iota(jnp.int32, tile, 1)
    for source in range(sources):
        wave_ref[source * piece_rows : (source + 1) * piece_rows, :] = received_ref[
            source, :piece_rows, :
        ].astype(jnp.float32)
    first, second = [], []
    for band in range(parts):
        piece = received_ref[band * group_count + group].astype(jnp.float32)
        upper, lower = piece[:piece_rows], piece[piece_rows:]
        start = pltpu.roll(upper, left, 1)
        rest = pltpu.roll(lower, (lane_count - (slot_total - left)) % lane_count, 1)
        first.append(jnp.where(lane < left, start, jnp.where(lane < slot_total, rest, 0.0)))
        second.append(jnp.where(lane < slot_total, lower, 0.0))
    bases = [
        jnp.concatenate(first, axis=0).astype(jnp.bfloat16),
        jnp.concatenate(second, axis=0).astype(jnp.bfloat16),
    ]
    row_tile = (1, lane_count)
    lane_row = lax.broadcasted_iota(jnp.int32, row_tile, 1)
    depth_row = jnp.zeros(row_tile, jnp.float32)
    damp_row = jnp.zeros(row_tile, jnp.float32)
    for level in range(levels):
        depth_row = jnp.where(lane_row % levels == level, depths_ref[level], depth_row)
        damp_row = jnp.where(lane_row == level, diffusion_ref[level], damp_row)
    is_first = lane_row < levels
    is_last = lane_row >= 2 * levels
    coeff_row = jnp.where(is_first, damp_row, depth_row)
    column_tile = (lane_count, 1)
    position = lax.broadcasted_iota(jnp.int32, column_tile, 0)
    for index in range(per_part):
        pair = pairs_ref[group, jnp.minimum(part * per_part + index, slot_count - 1)]
        lower_half = position < highest - pair
        total = jnp.where(lower_half, pair + position, position - 1).astype(jnp.float32)
        operator = total * (total + 1.0) / float(highest * highest)
        factor = jnp.where(is_first, operator * operator, operator)
        divisor = 1.0 + coeff_row * factor
        basis = bases[index]
        basis_turned = basis.astype(jnp.float32).T.astype(jnp.bfloat16)
        solved = []
        for phase in range(2):
            halves = []
            for half in range(2):
                at = (phase * 2 + half) * per_part + index
                waves = wave_ref[pl.ds(at, sources, stride=piece_rows), :].astype(jnp.bfloat16)
                halves.append(
                    jnp.dot(basis_turned, waves, preferred_element_type=jnp.float32)
                )
            spec = jnp.where(lower_half, halves[0], halves[1])
            thermal = pltpu.roll(spec, lane_count - levels, 1)
            top = jnp.where(is_first, spec, spec + operator * thermal)
            quotient = top / divisor
            moved = pltpu.roll(quotient, levels, 1)
            solved.append(jnp.where(is_last, spec - depth_row * moved, quotient))
        for phase in range(2):
            for half in range(2):
                at = (phase * 2 + half) * per_part + index
                kept = jnp.where(
                    lower_half if half == 0 else jnp.logical_not(lower_half), solved[phase], 0.0
                )
                back = jnp.dot(
                    basis, kept.astype(jnp.bfloat16), preferred_element_type=jnp.float32
                )
                wavenumber = pair if half == 0 else highest - 1 - pair
                doubling = jnp.where(wavenumber == 0, 1.0, 2.0)
                wave_ref[pl.ds(at, sources, stride=piece_rows), :] = back * doubling
    for source in range(sources):
        sent_ref[source] = wave_ref[
            source * piece_rows : (source + 1) * piece_rows, :
        ].astype(jnp.bfloat16)


def synthesis_kernel(dims, received_ref, table_ref, points_ref, out_ref):
    levels, lon_count, group_count, slot_count, parts, per_part, highest = dims
    blocks = lon_count // lane_count
    sources = parts * group_count
    columns = (slot_count // per_part) * group_count * piece_rows
    pieces = [received_ref[source].astype(jnp.float32) for source in range(sources)]
    turned = jnp.concatenate(pieces, axis=0).T
    waves = turned[: 3 * levels, :columns].astype(jnp.bfloat16)
    points = points_ref[0]
    lane_wide = lax.broadcasted_iota(jnp.int32, (levels, lane_count), 1)
    result = jnp.dot(waves, table_ref[...], preferred_element_type=jnp.float32)
    for block in range(blocks):
        inside = lane_wide < points - block * lane_count
        for field in range(3):
            value = result[
                field * levels : (field + 1) * levels,
                block * lane_count : (block + 1) * lane_count,
            ]
            out_ref[pl.ds(field * blocks + block, levels, stride=3 * blocks), :] = jnp.where(
                inside, value, 0.0
            )


def packed_body(
    dims,
    prognostic_arrays,
    coriolis,
    weights,
    row_points,
    owner_pairs,
    legendre,
    depths,
    diffusion,
):
    levels, lon_count, group_count, slot_count, parts, per_part, highest = dims
    channels = 3 * levels
    blocks = lon_count // lane_count
    sources = parts * group_count
    columns = (slot_count // per_part) * group_count * piece_rows
    in_vmem = pl.BlockSpec(memory_space=pltpu.VMEM)
    in_smem = pl.BlockSpec(memory_space=pltpu.SMEM)
    in_hbm = pl.BlockSpec(memory_space=pl.ANY)
    params = pltpu.CompilerParams(vmem_limit_bytes=16 << 20)
    grid = prognostic_arrays.reshape(channels * blocks, lane_count)
    position = jnp.stack([lax.axis_index("lat"), lax.axis_index("lev")]).astype(jnp.int32)
    sent, table = pl.pallas_call(
        functools.partial(analysis_kernel, dims),
        name="analysis",
        out_shape=(
            jax.ShapeDtypeStruct((sources, 2 * piece_rows, lane_count), jnp.bfloat16),
            jax.ShapeDtypeStruct((columns, lon_count), jnp.bfloat16),
        ),
        in_specs=[in_hbm, in_smem, in_smem, in_smem, in_smem, in_vmem],
        out_specs=(in_vmem, in_vmem),
        scratch_shapes=[
            pltpu.VMEM((channels * blocks, lane_count), jnp.float32),
            pltpu.VMEM((channels, lon_count), jnp.bfloat16),
            pltpu.VMEM((columns, lane_count), jnp.float32),
            pltpu.SemaphoreType.DMA(()),
        ],
        compiler_params=params,
    )(grid, coriolis, weights, row_points, owner_pairs, jnp.swapaxes(legendre, 2, 3))
    received = lax.all_to_all(sent, ("lat", "lev"), split_axis=0, concat_axis=0, tiled=True)
    solved = pl.pallas_call(
        functools.partial(spectral_kernel, dims),
        name="spectral",
        out_shape=jax.ShapeDtypeStruct((sources, piece_rows, lane_count), jnp.bfloat16),
        in_specs=[in_vmem, in_smem, in_smem, in_smem, in_smem],
        out_specs=in_vmem,
        scratch_shapes=[pltpu.VMEM((sources * piece_rows, lane_count), jnp.float32)],
        compiler_params=params,
    )(received, position, owner_pairs, depths, diffusion)
    returned = lax.all_to_all(solved, ("lat", "lev"), split_axis=0, concat_axis=0, tiled=True)
    updated = pl.pallas_call(
        functools.partial(synthesis_kernel, dims),
        name="synthesis",
        out_shape=jax.ShapeDtypeStruct((channels * blocks, lane_count), jnp.float32),
        in_specs=[in_vmem, in_vmem, in_smem],
        out_specs=in_vmem,
        compiler_params=params,
    )(returned, table, row_points)
    return updated.reshape(prognostic_arrays.shape)


def body(prognostic_arrays, coriolis, weights, row_points, owner_pairs, legendre, depths, diffusion):
    levels, _, row_count, lon_count = prognostic_arrays.shape
    group_count, slot_count = owner_pairs.shape
    slot_total, band_rows = legendre.shape[2:]
    parts = lax.axis_size("lat")
    per_part = -(-slot_count // parts)
    channels = 3 * levels
    fits = (
        row_count == 1
        and band_rows == piece_rows == group_count
        and 4 * per_part == piece_rows
        and slot_count % per_part == 0
        and lon_count % lane_count == 0
        and lon_count // lane_count <= lane_count
        and levels % 16 == 0
        and channels < slot_total <= lane_count
        and 2 * slot_total + channels <= 2 * lane_count
        and lon_count * slot_total < 2**24
        and (parts * group_count * piece_rows) % lane_count == 0
    )
    arguments = (
        prognostic_arrays, coriolis, weights, row_points, owner_pairs, legendre, depths, diffusion
    )
    if not fits:
        return general_body(*arguments)
    dims = (levels, lon_count, group_count, slot_count, parts, per_part, slot_total - 1)
    return packed_body(dims, *arguments)


def solution(mesh):
    in_specs = (
        P(None, None, ("lat", "lev"), None),
        P(("lat", "lev")),
        P(("lat", "lev")),
        P(("lat", "lev")),
        P(),
        P("lev", None, None, "lat"),
        P(),
        P(),
    )
    out_specs = P(None, None, ("lat", "lev"), None)
    return jax.shard_map(body, mesh=mesh, in_specs=in_specs, out_specs=out_specs, check_vma=False)
```

```python
import functools
import math

import jax
import jax.numpy as jnp
from jax import lax
from jax.experimental import pallas as pl
from jax.experimental.pallas import tpu as pltpu
from jax.sharding import PartitionSpec as P

stepsize_delta = 0.5


def tendencies(prognostic_arrays, coriolis):
    vorticity = prognostic_arrays[:, 0]
    spreading_rate_grid = prognostic_arrays[:, 1]
    thermal_state_grid = prognostic_arrays[:, 2]
    rotation = coriolis[None, :, None]
    advanced_curl_rate = vorticity - stepsize_delta * (rotation + vorticity) * spreading_rate_grid
    advanced_spreading_rate = spreading_rate_grid + stepsize_delta * (
        rotation * vorticity - spreading_rate_grid * spreading_rate_grid
    )
    advanced_thermal_state = (
        thermal_state_grid - stepsize_delta * thermal_state_grid * spreading_rate_grid
    )
    return jnp.stack(
        [advanced_curl_rate, advanced_spreading_rate, advanced_thermal_state], axis=1
    ).astype(jnp.bfloat16)


def owner_waves(owner_pairs, highest):
    return jnp.stack([owner_pairs, highest - 1 - owner_pairs], axis=1)


def phase_table(points, wavenumbers, lon_count):
    positions = jnp.arange(lon_count, dtype=jnp.int32)
    product = positions[None, :, None] * wavenumbers[None, None, :] % points[:, None, None]
    angle = (
        product.astype(jnp.float32) * (2.0 * math.pi / points.astype(jnp.float32))[:, None, None]
    )
    return jnp.stack([jnp.cos(angle), -jnp.sin(angle)], axis=2).astype(jnp.bfloat16)


def valid_points(points, lon_count):
    positions = jnp.arange(lon_count, dtype=jnp.int32)
    return positions[None, :] < points[:, None]


def half_mask(my_pairs, slot_total):
    positions = jnp.arange(slot_total, dtype=jnp.int32)
    return positions[None, :] < (slot_total - 1 - my_pairs)[:, None]


def implicit(summed, my_pairs, depth_part, diff_part):
    slot_total = summed.shape[3]
    slot_count = summed.shape[2]
    highest = slot_total - 1
    positions = jnp.arange(slot_total, dtype=jnp.int32)[None, :]
    first_half = positions < (highest - my_pairs)[:, None]
    total = jnp.where(first_half, my_pairs[:, None] + positions, positions - 1).astype(jnp.float32)
    harmonic_operator_spectrum = total * (total + 1.0) / float(highest * highest)
    bundled_prognostics = summed.reshape(-1, 3, 2, slot_count, slot_total)
    vorticity = bundled_prognostics[:, 0]
    spreading_rate_grid = bundled_prognostics[:, 1]
    thermal_state_grid = bundled_prognostics[:, 2]
    layer_stack_count = depth_part[:, None, None, None]
    diff_cols = diff_part[:, None, None, None]
    advanced_curl_rate = vorticity / (
        1.0 + diff_cols * harmonic_operator_spectrum * harmonic_operator_spectrum
    )
    advanced_spreading_rate = (
        spreading_rate_grid + harmonic_operator_spectrum * thermal_state_grid
    ) / (1.0 + layer_stack_count * harmonic_operator_spectrum)
    advanced_thermal_state = thermal_state_grid - layer_stack_count * advanced_spreading_rate
    piled_prognostics = jnp.stack(
        [advanced_curl_rate, advanced_spreading_rate, advanced_thermal_state], axis=1
    )
    return piled_prognostics.reshape(summed.shape).astype(jnp.bfloat16)


def general_body(
    prognostic_arrays, coriolis, weights, row_points, owner_pairs, legendre, depths, diffusion
):
    levels = prognostic_arrays.shape[0]
    row_count = prognostic_arrays.shape[2]
    lon_count = prognostic_arrays.shape[3]
    group_count = owner_pairs.shape[0]
    slot_count = owner_pairs.shape[1]
    local_basis = legendre[0]
    slot_total = local_basis.shape[1]
    highest = slot_total - 1
    channels = levels * 3
    packed = channels * 4 * slot_count
    wavenumbers = owner_waves(owner_pairs, highest).reshape(-1)
    valid = valid_points(row_points, lon_count)
    gridded = tendencies(prognostic_arrays, coriolis).reshape(channels, row_count, lon_count)
    gridded = jnp.where(valid[None], gridded, jnp.zeros((), gridded.dtype))
    phases = phase_table(row_points, wavenumbers, lon_count).reshape(
        row_count, lon_count, 2, group_count, 2, slot_count
    )
    row_scale = weights / row_points.astype(jnp.float32)
    fourier = jnp.einsum("crx,rxqght->grcqht", gridded, phases, preferred_element_type=jnp.float32)
    fourier = (fourier * row_scale[None, :, None, None, None, None]).astype(jnp.bfloat16)
    band_data = lax.all_to_all(
        fourier.reshape(group_count, row_count, packed),
        "lev",
        split_axis=0,
        concat_axis=0,
        tiled=True,
    )
    band_block = band_data.reshape(group_count * row_count, channels, 2, 2, slot_count)
    owner_index = lax.axis_index("lev")
    my_pairs = lax.dynamic_index_in_dim(owner_pairs, owner_index, 0, keepdims=False)
    first_half = half_mask(my_pairs, slot_total)
    half_masks = jnp.stack([first_half, jnp.logical_not(first_half)], axis=0)
    doubling = jnp.where(owner_waves(my_pairs[None], highest)[0] == 0, 1.0, 2.0).astype(jnp.float32)
    both_halves = jnp.einsum(
        "lkqht,tpl->kqhtp", band_block, local_basis, preferred_element_type=jnp.float32
    )
    summed = lax.psum(jnp.where(first_half, both_halves[:, :, 0], both_halves[:, :, 1]), "lat")
    solved = implicit(summed, my_pairs, depths, diffusion)
    masked_spec = jnp.where(half_masks[None, None], solved[:, :, None], jnp.zeros((), solved.dtype))
    inverted = jnp.einsum(
        "kqhtp,tpl->lkqht", masked_spec, local_basis, preferred_element_type=jnp.float32
    )
    inverted = (inverted * doubling[None, None, None]).astype(jnp.bfloat16)
    returned = lax.all_to_all(
        inverted.reshape(group_count, row_count, packed),
        "lev",
        split_axis=0,
        concat_axis=0,
        tiled=True,
    )
    returned = returned.reshape(group_count, row_count, channels, 2, 2, slot_count)
    outgrid = jnp.einsum("grcqht,rxqght->crx", returned, phases, preferred_element_type=jnp.float32)
    outgrid = jnp.where(valid[None], outgrid, jnp.zeros((), outgrid.dtype))
    return outgrid.reshape(levels, 3, row_count, lon_count)


lane_count = 128
piece_rows = 8


def turn_cos_sin(turns):
    scaled = turns * 4.0
    nearest = jnp.floor(scaled + 0.5)
    arc = (scaled - nearest) * (0.5 * math.pi)
    square = arc * arc
    sine = arc + arc * square * (
        -1.6666654611e-1 + square * (8.3321608736e-3 + square * -1.9515295891e-4)
    )
    cosine = (
        1.0
        - 0.5 * square
        + square
        * square
        * (4.166664568298827e-2 + square * (-1.388731625493765e-3 + square * 2.443315711809948e-5))
    )
    swapped = jnp.logical_or(nearest == 1.0, nearest == 3.0)
    cos_part = jnp.where(swapped, sine, cosine)
    sin_part = jnp.where(swapped, cosine, sine)
    cos_part = jnp.where(jnp.logical_or(nearest == 1.0, nearest == 2.0), -cos_part, cos_part)
    sin_part = jnp.where(jnp.logical_or(nearest == 2.0, nearest == 3.0), -sin_part, sin_part)
    return cos_part, sin_part


def turns_of(product, points, inverse):
    rest = product - jnp.floor(product * inverse) * points
    rest = jnp.where(rest < 0.0, rest + points, rest)
    rest = jnp.where(rest >= points, rest - points, rest)
    return rest * inverse


def analysis_kernel(
    dims,
    grid_hbm,
    coriolis_hbm,
    weights_hbm,
    points_hbm,
    pairs_hbm,
    legendre_hbm,
    sent_ref,
    near_ref,
    far_ref,
    grid_ref,
    coriolis_ref,
    weights_ref,
    points_ref,
    pairs_ref,
    legendre_ref,
    rhs_ref,
    wave_ref,
    sems,
):
    levels, lon_count, group_count, slot_count, parts, per_part, highest = dims
    channels = 3 * levels
    blocks = lon_count // lane_count
    active = slot_count // per_part
    sources = parts * group_count
    copies = [
        pltpu.make_async_copy(source, target, sems.at[at])
        for at, (source, target) in enumerate(
            (
                (pairs_hbm, pairs_ref),
                (points_hbm, points_ref),
                (grid_hbm, grid_ref),
                (coriolis_hbm, coriolis_ref),
                (weights_hbm, weights_ref),
                (legendre_hbm, legendre_ref),
            )
        )
    ]
    for copy in copies:
        copy.start()
    copies[0].wait()
    copies[1].wait()

    tile = (piece_rows, lane_count)
    row = lax.broadcasted_iota(jnp.int32, tile, 0)
    lane = lax.broadcasted_iota(jnp.int32, tile, 1)
    lane_slot = lane // group_count % parts * per_part + lane // sources % per_part
    at_group = lane % group_count == row
    pairs = pairs_ref[...].astype(jnp.float32)
    spread = jnp.zeros(tile, jnp.float32)
    for slot in range(slot_count):
        chosen = jnp.logical_and(at_group, lane_slot == slot)
        spread = jnp.where(chosen, pairs[:, slot : slot + 1], spread)
    pair = jnp.sum(spread, axis=0, keepdims=True)
    lane_row = lax.broadcasted_iota(jnp.int32, (1, lane_count), 1)
    wave = jnp.where(lane_row >= per_part * sources, float(highest - 1) - pair, pair)
    points = jnp.broadcast_to(points_ref[...], (1, lane_count))
    points_row = points.astype(jnp.float32)
    inverse = 1.0 / points_row

    def factors(first, count, step):
        place = (first + lax.broadcasted_iota(jnp.int32, (count, lane_count), 0)) * step
        cosine, sine = turn_cos_sin(turns_of(place.astype(jnp.float32) * wave, points_row, inverse))
        return jnp.concatenate([cosine, -sine], axis=1)

    near_ref[...] = factors(0, lane_count, 1).astype(jnp.bfloat16)
    far_ref[...] = factors(0, far_ref.shape[0], lane_count)

    copies[3].wait()
    rotation = jnp.broadcast_to(coriolis_ref[...], (levels, lane_count))
    lane_wide = lax.broadcasted_iota(jnp.int32, (levels, lane_count), 1)
    points_wide = jnp.broadcast_to(points, (levels, lane_count))
    copies[2].wait()
    for block in range(blocks):
        vorticity, spreading, thermal = (
            grid_ref[pl.ds(field * blocks + block, levels, stride=3 * blocks), :]
            for field in range(3)
        )
        inside = lane_wide + block * lane_count < points_wide
        advanced = (
            vorticity - stepsize_delta * (rotation + vorticity) * spreading,
            spreading + stepsize_delta * (rotation * vorticity - spreading * spreading),
            thermal - stepsize_delta * thermal * spreading,
        )
        for field in range(3):
            at = block * channels + field * levels
            rhs_ref[at : at + levels, :] = jnp.where(inside, advanced[field], 0.0).astype(
                jnp.bfloat16
            )
    partial = jnp.dot(rhs_ref[...], near_ref[...], preferred_element_type=jnp.float32)
    real = jnp.zeros((channels, lane_count), jnp.float32)
    imag = jnp.zeros((channels, lane_count), jnp.float32)
    for block in range(blocks):
        part_real = partial[block * channels : (block + 1) * channels, :lane_count]
        part_imag = partial[block * channels : (block + 1) * channels, lane_count:]
        far_real = far_ref[block : block + 1, :lane_count]
        far_imag = far_ref[block : block + 1, lane_count:]
        real = real + (part_real * far_real - part_imag * far_imag)
        imag = imag + (part_real * far_imag + part_imag * far_real)
    copies[4].wait()
    scale = jnp.broadcast_to(weights_ref[...], (1, lane_count)) / points_row
    half_rows = 2 * per_part
    for phase, value in enumerate((real, imag)):
        turned = jnp.pad(value * scale, ((0, lane_count - channels), (0, 0))).T
        for at in range(half_rows):
            wave_ref[pl.ds(phase * half_rows + at, sources, stride=piece_rows), :] = turned[
                at * sources : (at + 1) * sources
            ]

    copies[5].wait()
    slot_total = highest + 1
    left = lane_count - channels
    for part in range(active):
        first, second = (
            jnp.pad(
                legendre_ref[0, part * per_part + index].astype(jnp.float32),
                ((0, 0), (0, lane_count - slot_total)),
            )
            for index in range(2)
        )
        upper_basis = pltpu.roll(first, channels, 1)
        lower = jnp.where(
            lane < slot_total, second, pltpu.roll(first, (slot_total - left) % lane_count, 1)
        )
        for group in range(group_count):
            at = part * group_count + group
            upper = jnp.where(
                lane < channels,
                wave_ref[at * piece_rows : (at + 1) * piece_rows, :],
                upper_basis,
            )
            sent_ref[at] = jnp.concatenate([upper, lower], axis=0).astype(jnp.bfloat16)
    for at in range(active * group_count, sources):
        sent_ref[at] = jnp.zeros((2 * piece_rows, lane_count), jnp.bfloat16)


def spectral_kernel(
    dims,
    received_ref,
    position_ref,
    pairs_ref,
    depths_ref,
    diffusion_ref,
    sent_ref,
    wave_ref,
):
    levels, lon_count, group_count, slot_count, parts, per_part, highest = dims
    channels = 3 * levels
    slot_total = highest + 1
    left = lane_count - channels
    sources = parts * group_count
    part, group = position_ref[0], position_ref[1]
    tile = (piece_rows, lane_count)
    lane = lax.broadcasted_iota(jnp.int32, tile, 1)
    for source in range(sources):
        wave_ref[source * piece_rows : (source + 1) * piece_rows, :] = received_ref[
            source, :piece_rows, :
        ].astype(jnp.float32)
    first, second = [], []
    for band in range(parts):
        piece = received_ref[band * group_count + group].astype(jnp.float32)
        upper, lower = piece[:piece_rows], piece[piece_rows:]
        start = pltpu.roll(upper, left, 1)
        rest = pltpu.roll(lower, (lane_count - (slot_total - left)) % lane_count, 1)
        first.append(jnp.where(lane < left, start, jnp.where(lane < slot_total, rest, 0.0)))
        second.append(jnp.where(lane < slot_total, lower, 0.0))
    bases = [
        jnp.concatenate(first, axis=0).astype(jnp.bfloat16),
        jnp.concatenate(second, axis=0).astype(jnp.bfloat16),
    ]
    row_tile = (1, lane_count)
    lane_row = lax.broadcasted_iota(jnp.int32, row_tile, 1)
    depth_row = jnp.zeros(row_tile, jnp.float32)
    damp_row = jnp.zeros(row_tile, jnp.float32)
    for level in range(levels):
        depth_row = jnp.where(lane_row % levels == level, depths_ref[level], depth_row)
        damp_row = jnp.where(lane_row == level, diffusion_ref[level], damp_row)
    is_first = lane_row < levels
    is_last = lane_row >= 2 * levels
    coeff_row = jnp.where(is_first, damp_row, depth_row)
    column_tile = (lane_count, 1)
    position = lax.broadcasted_iota(jnp.int32, column_tile, 0)
    for index in range(per_part):
        pair = pairs_ref[group, jnp.minimum(part * per_part + index, slot_count - 1)]
        lower_half = position < highest - pair
        total = jnp.where(lower_half, pair + position, position - 1).astype(jnp.float32)
        operator = total * (total + 1.0) / float(highest * highest)
        factor = jnp.where(is_first, operator * operator, operator)
        divisor = 1.0 + coeff_row * factor
        basis = bases[index]
        basis_turned = basis.astype(jnp.float32).T.astype(jnp.bfloat16)
        solved = []
        for phase in range(2):
            halves = []
            for half in range(2):
                at = (phase * 2 + half) * per_part + index
                waves = wave_ref[pl.ds(at, sources, stride=piece_rows), :].astype(jnp.bfloat16)
                halves.append(
                    jnp.dot(basis_turned, waves, preferred_element_type=jnp.float32)
                )
            spec = jnp.where(lower_half, halves[0], halves[1])
            thermal = pltpu.roll(spec, lane_count - levels, 1)
            top = jnp.where(is_first, spec, spec + operator * thermal)
            quotient = top / divisor
            moved = pltpu.roll(quotient, levels, 1)
            solved.append(jnp.where(is_last, spec - depth_row * moved, quotient))
        for phase in range(2):
            for half in range(2):
                at = (phase * 2 + half) * per_part + index
                kept = jnp.where(
                    lower_half if half == 0 else jnp.logical_not(lower_half), solved[phase], 0.0
                )
                back = jnp.dot(
                    basis, kept.astype(jnp.bfloat16), preferred_element_type=jnp.float32
                )
                wavenumber = pair if half == 0 else highest - 1 - pair
                doubling = jnp.where(wavenumber == 0, 1.0, 2.0)
                wave_ref[pl.ds(at, sources, stride=piece_rows), :] = back * doubling
    for source in range(sources):
        sent_ref[source] = wave_ref[
            source * piece_rows : (source + 1) * piece_rows, :
        ].astype(jnp.bfloat16)


def synthesis_kernel(
    dims, received_ref, near_ref, far_ref, points_ref, out_ref, wave_ref, rotated_ref
):
    levels, lon_count, group_count, slot_count, parts, per_part, highest = dims
    channels = 3 * levels
    blocks = lon_count // lane_count
    sources = parts * group_count
    half_rows = 2 * per_part
    for source in range(sources):
        wave_ref[source * piece_rows : (source + 1) * piece_rows, :] = received_ref[source].astype(
            jnp.float32
        )
    real, imag = (
        jnp.concatenate(
            [
                wave_ref[pl.ds(phase * half_rows + at, sources, stride=piece_rows), :]
                for at in range(half_rows)
            ],
            axis=0,
        ).T[:channels]
        for phase in range(2)
    )
    for block in range(blocks):
        far_real = far_ref[block : block + 1, :lane_count]
        far_imag = far_ref[block : block + 1, lane_count:]
        rotated_ref[block * channels : (block + 1) * channels, :] = jnp.concatenate(
            [real * far_real + imag * far_imag, imag * far_real - real * far_imag], axis=1
        ).astype(jnp.bfloat16)
    result = lax.dot_general(
        rotated_ref[...],
        near_ref[...],
        (((1,), (1,)), ((), ())),
        preferred_element_type=jnp.float32,
    )
    lane_wide = lax.broadcasted_iota(jnp.int32, (levels, lane_count), 1)
    points = jnp.broadcast_to(points_ref[...], (levels, lane_count))
    for block in range(blocks):
        inside = lane_wide + block * lane_count < points
        for field in range(3):
            at = block * channels + field * levels
            out_ref[pl.ds(field * blocks + block, levels, stride=3 * blocks), :] = jnp.where(
                inside, result[at : at + levels], 0.0
            )


def packed_body(
    dims,
    prognostic_arrays,
    coriolis,
    weights,
    row_points,
    owner_pairs,
    legendre,
    depths,
    diffusion,
):
    levels, lon_count, group_count, slot_count, parts, per_part, highest = dims
    channels = 3 * levels
    blocks = lon_count // lane_count
    sources = parts * group_count
    far_rows = -(-blocks // piece_rows) * piece_rows
    in_vmem = pl.BlockSpec(memory_space=pltpu.VMEM)
    in_smem = pl.BlockSpec(memory_space=pltpu.SMEM)
    in_hbm = pl.BlockSpec(memory_space=pltpu.HBM)
    params = pltpu.CompilerParams(vmem_limit_bytes=16 << 20)
    grid = prognostic_arrays.reshape(channels * blocks, lane_count)
    position = jnp.stack([lax.axis_index("lat"), lax.axis_index("lev")]).astype(jnp.int32)
    points = row_points.reshape(1, 1)
    basis = jnp.swapaxes(legendre, 2, 3)
    sent, near, far = pl.pallas_call(
        functools.partial(analysis_kernel, dims),
        name="analysis",
        out_shape=(
            jax.ShapeDtypeStruct((sources, 2 * piece_rows, lane_count), jnp.bfloat16),
            jax.ShapeDtypeStruct((lane_count, 2 * lane_count), jnp.bfloat16),
            jax.ShapeDtypeStruct((far_rows, 2 * lane_count), jnp.float32),
        ),
        in_specs=[in_hbm] * 6,
        out_specs=(in_vmem, in_vmem, in_vmem),
        scratch_shapes=[
            pltpu.VMEM(grid.shape, jnp.float32),
            pltpu.VMEM((1, 1), jnp.float32),
            pltpu.VMEM((1, 1), jnp.float32),
            pltpu.VMEM((1, 1), jnp.int32),
            pltpu.VMEM(owner_pairs.shape, jnp.int32),
            pltpu.VMEM(basis.shape, jnp.bfloat16),
            pltpu.VMEM((blocks * channels, lane_count), jnp.bfloat16),
            pltpu.VMEM((sources * piece_rows, lane_count), jnp.float32),
            pltpu.SemaphoreType.DMA((6,)),
        ],
        compiler_params=params,
    )(grid, coriolis.reshape(1, 1), weights.reshape(1, 1), points, owner_pairs, basis)
    received = lax.all_to_all(sent, ("lat", "lev"), split_axis=0, concat_axis=0, tiled=True)
    solved = pl.pallas_call(
        functools.partial(spectral_kernel, dims),
        name="spectral",
        out_shape=jax.ShapeDtypeStruct((sources, piece_rows, lane_count), jnp.bfloat16),
        in_specs=[in_vmem, in_smem, in_smem, in_smem, in_smem],
        out_specs=in_vmem,
        scratch_shapes=[pltpu.VMEM((sources * piece_rows, lane_count), jnp.float32)],
        compiler_params=params,
    )(received, position, owner_pairs, depths, diffusion)
    returned = lax.all_to_all(solved, ("lat", "lev"), split_axis=0, concat_axis=0, tiled=True)
    updated = pl.pallas_call(
        functools.partial(synthesis_kernel, dims),
        name="synthesis",
        out_shape=jax.ShapeDtypeStruct((channels * blocks, lane_count), jnp.float32),
        in_specs=[in_vmem] * 4,
        out_specs=in_vmem,
        scratch_shapes=[
            pltpu.VMEM((sources * piece_rows, lane_count), jnp.float32),
            pltpu.VMEM((blocks * channels, 2 * lane_count), jnp.bfloat16),
        ],
        compiler_params=params,
    )(returned, near, far, points)
    return updated.reshape(prognostic_arrays.shape)


def body(prognostic_arrays, coriolis, weights, row_points, owner_pairs, legendre, depths, diffusion):
    levels, _, row_count, lon_count = prognostic_arrays.shape
    group_count, slot_count = owner_pairs.shape
    slot_total, band_rows = legendre.shape[2:]
    parts = lax.axis_size("lat")
    per_part = -(-slot_count // parts)
    channels = 3 * levels
    fits = (
        row_count == 1
        and band_rows == piece_rows == group_count
        and 4 * per_part == piece_rows
        and slot_count % per_part == 0
        and lon_count % lane_count == 0
        and 2 * per_part * parts * group_count == lane_count
        and levels % 16 == 0
        and channels < slot_total <= lane_count
        and 2 * slot_total + channels <= 2 * lane_count
        and lon_count * slot_total < 2**24
    )
    arguments = (
        prognostic_arrays, coriolis, weights, row_points, owner_pairs, legendre, depths, diffusion
    )
    if not fits:
        return general_body(*arguments)
    dims = (levels, lon_count, group_count, slot_count, parts, per_part, slot_total - 1)
    return packed_body(dims, *arguments)


def solution(mesh):
    in_specs = (
        P(None, None, ("lat", "lev"), None),
        P(("lat", "lev")),
        P(("lat", "lev")),
        P(("lat", "lev")),
        P(),
        P("lev", None, None, "lat"),
        P(),
        P(),
    )
    out_specs = P(None, None, ("lat", "lev"), None)
    return jax.shard_map(body, mesh=mesh, in_specs=in_specs, out_specs=out_specs, check_vma=False)
```

```python
import functools
import math

import jax
import jax.numpy as jnp
from jax import lax
from jax.experimental import pallas as pl
from jax.experimental.pallas import tpu as pltpu
from jax.sharding import PartitionSpec as P

stepsize_delta = 0.5


def tendencies(prognostic_arrays, coriolis):
    vorticity = prognostic_arrays[:, 0]
    spreading_rate_grid = prognostic_arrays[:, 1]
    thermal_state_grid = prognostic_arrays[:, 2]
    rotation = coriolis[None, :, None]
    advanced_curl_rate = vorticity - stepsize_delta * (rotation + vorticity) * spreading_rate_grid
    advanced_spreading_rate = spreading_rate_grid + stepsize_delta * (
        rotation * vorticity - spreading_rate_grid * spreading_rate_grid
    )
    advanced_thermal_state = (
        thermal_state_grid - stepsize_delta * thermal_state_grid * spreading_rate_grid
    )
    return jnp.stack(
        [advanced_curl_rate, advanced_spreading_rate, advanced_thermal_state], axis=1
    ).astype(jnp.bfloat16)


def owner_waves(owner_pairs, highest):
    return jnp.stack([owner_pairs, highest - 1 - owner_pairs], axis=1)


def phase_table(points, wavenumbers, lon_count):
    positions = jnp.arange(lon_count, dtype=jnp.int32)
    product = positions[None, :, None] * wavenumbers[None, None, :] % points[:, None, None]
    angle = (
        product.astype(jnp.float32) * (2.0 * math.pi / points.astype(jnp.float32))[:, None, None]
    )
    return jnp.stack([jnp.cos(angle), -jnp.sin(angle)], axis=2).astype(jnp.bfloat16)


def valid_points(points, lon_count):
    positions = jnp.arange(lon_count, dtype=jnp.int32)
    return positions[None, :] < points[:, None]


def half_mask(my_pairs, slot_total):
    positions = jnp.arange(slot_total, dtype=jnp.int32)
    return positions[None, :] < (slot_total - 1 - my_pairs)[:, None]


def implicit(summed, my_pairs, depth_part, diff_part):
    slot_total = summed.shape[3]
    slot_count = summed.shape[2]
    highest = slot_total - 1
    positions = jnp.arange(slot_total, dtype=jnp.int32)[None, :]
    first_half = positions < (highest - my_pairs)[:, None]
    total = jnp.where(first_half, my_pairs[:, None] + positions, positions - 1).astype(jnp.float32)
    harmonic_operator_spectrum = total * (total + 1.0) / float(highest * highest)
    bundled_prognostics = summed.reshape(-1, 3, 2, slot_count, slot_total)
    vorticity = bundled_prognostics[:, 0]
    spreading_rate_grid = bundled_prognostics[:, 1]
    thermal_state_grid = bundled_prognostics[:, 2]
    layer_stack_count = depth_part[:, None, None, None]
    diff_cols = diff_part[:, None, None, None]
    advanced_curl_rate = vorticity / (
        1.0 + diff_cols * harmonic_operator_spectrum * harmonic_operator_spectrum
    )
    advanced_spreading_rate = (
        spreading_rate_grid + harmonic_operator_spectrum * thermal_state_grid
    ) / (1.0 + layer_stack_count * harmonic_operator_spectrum)
    advanced_thermal_state = thermal_state_grid - layer_stack_count * advanced_spreading_rate
    piled_prognostics = jnp.stack(
        [advanced_curl_rate, advanced_spreading_rate, advanced_thermal_state], axis=1
    )
    return piled_prognostics.reshape(summed.shape).astype(jnp.bfloat16)


def general_body(
    prognostic_arrays, coriolis, weights, row_points, owner_pairs, legendre, depths, diffusion
):
    levels = prognostic_arrays.shape[0]
    row_count = prognostic_arrays.shape[2]
    lon_count = prognostic_arrays.shape[3]
    group_count = owner_pairs.shape[0]
    slot_count = owner_pairs.shape[1]
    local_basis = legendre[0]
    slot_total = local_basis.shape[1]
    highest = slot_total - 1
    channels = levels * 3
    packed = channels * 4 * slot_count
    wavenumbers = owner_waves(owner_pairs, highest).reshape(-1)
    valid = valid_points(row_points, lon_count)
    gridded = tendencies(prognostic_arrays, coriolis).reshape(channels, row_count, lon_count)
    gridded = jnp.where(valid[None], gridded, jnp.zeros((), gridded.dtype))
    phases = phase_table(row_points, wavenumbers, lon_count).reshape(
        row_count, lon_count, 2, group_count, 2, slot_count
    )
    row_scale = weights / row_points.astype(jnp.float32)
    fourier = jnp.einsum("crx,rxqght->grcqht", gridded, phases, preferred_element_type=jnp.float32)
    fourier = (fourier * row_scale[None, :, None, None, None, None]).astype(jnp.bfloat16)
    band_data = lax.all_to_all(
        fourier.reshape(group_count, row_count, packed),
        "lev",
        split_axis=0,
        concat_axis=0,
        tiled=True,
    )
    band_block = band_data.reshape(group_count * row_count, channels, 2, 2, slot_count)
    owner_index = lax.axis_index("lev")
    my_pairs = lax.dynamic_index_in_dim(owner_pairs, owner_index, 0, keepdims=False)
    first_half = half_mask(my_pairs, slot_total)
    half_masks = jnp.stack([first_half, jnp.logical_not(first_half)], axis=0)
    doubling = jnp.where(owner_waves(my_pairs[None], highest)[0] == 0, 1.0, 2.0).astype(jnp.float32)
    both_halves = jnp.einsum(
        "lkqht,tpl->kqhtp", band_block, local_basis, preferred_element_type=jnp.float32
    )
    summed = lax.psum(jnp.where(first_half, both_halves[:, :, 0], both_halves[:, :, 1]), "lat")
    solved = implicit(summed, my_pairs, depths, diffusion)
    masked_spec = jnp.where(half_masks[None, None], solved[:, :, None], jnp.zeros((), solved.dtype))
    inverted = jnp.einsum(
        "kqhtp,tpl->lkqht", masked_spec, local_basis, preferred_element_type=jnp.float32
    )
    inverted = (inverted * doubling[None, None, None]).astype(jnp.bfloat16)
    returned = lax.all_to_all(
        inverted.reshape(group_count, row_count, packed),
        "lev",
        split_axis=0,
        concat_axis=0,
        tiled=True,
    )
    returned = returned.reshape(group_count, row_count, channels, 2, 2, slot_count)
    outgrid = jnp.einsum("grcqht,rxqght->crx", returned, phases, preferred_element_type=jnp.float32)
    outgrid = jnp.where(valid[None], outgrid, jnp.zeros((), outgrid.dtype))
    return outgrid.reshape(levels, 3, row_count, lon_count)


lane_count = 128
piece_rows = 8


def turn_cos_sin(turns):
    scaled = turns * 4.0
    nearest = jnp.floor(scaled + 0.5)
    arc = (scaled - nearest) * (0.5 * math.pi)
    square = arc * arc
    sine = arc + arc * square * (
        -1.6666654611e-1 + square * (8.3321608736e-3 + square * -1.9515295891e-4)
    )
    cosine = (
        1.0
        - 0.5 * square
        + square
        * square
        * (4.166664568298827e-2 + square * (-1.388731625493765e-3 + square * 2.443315711809948e-5))
    )
    swapped = jnp.logical_or(nearest == 1.0, nearest == 3.0)
    cos_part = jnp.where(swapped, sine, cosine)
    sin_part = jnp.where(swapped, cosine, sine)
    cos_part = jnp.where(jnp.logical_or(nearest == 1.0, nearest == 2.0), -cos_part, cos_part)
    sin_part = jnp.where(jnp.logical_or(nearest == 2.0, nearest == 3.0), -sin_part, sin_part)
    return cos_part, sin_part


def turns_of(product, points, inverse):
    rest = product - jnp.floor(product * inverse) * points
    rest = jnp.where(rest < 0.0, rest + points, rest)
    rest = jnp.where(rest >= points, rest - points, rest)
    return rest * inverse


def analysis_kernel(
    dims,
    grid_hbm,
    coriolis_ref,
    weights_ref,
    points_ref,
    pairs_hbm,
    legendre_hbm,
    sent_ref,
    near_ref,
    far_ref,
    grid_ref,
    pairs_ref,
    legendre_ref,
    rhs_ref,
    wave_ref,
    sems,
):
    levels, lon_count, group_count, slot_count, parts, per_part, highest = dims
    channels = 3 * levels
    blocks = lon_count // lane_count
    active = slot_count // per_part
    sources = parts * group_count
    copies = [
        pltpu.make_async_copy(source, target, sems.at[at])
        for at, (source, target) in enumerate(
            (
                (pairs_hbm, pairs_ref),
                (grid_hbm, grid_ref),
                (legendre_hbm, legendre_ref),
            )
        )
    ]
    for copy in copies:
        copy.start()
    copies[0].wait()

    tile = (piece_rows, lane_count)
    row = lax.broadcasted_iota(jnp.int32, tile, 0)
    lane = lax.broadcasted_iota(jnp.int32, tile, 1)
    lane_slot = lane // group_count % parts * per_part + lane // sources % per_part
    at_group = lane % group_count == row
    pairs = pairs_ref[...].astype(jnp.float32)
    spread = jnp.zeros(tile, jnp.float32)
    for slot in range(slot_count):
        chosen = jnp.logical_and(at_group, lane_slot == slot)
        spread = jnp.where(chosen, pairs[:, slot : slot + 1], spread)
    pair = jnp.sum(spread, axis=0, keepdims=True)
    lane_row = lax.broadcasted_iota(jnp.int32, (1, lane_count), 1)
    wave = jnp.where(lane_row >= per_part * sources, float(highest - 1) - pair, pair)
    points = jnp.full((1, lane_count), points_ref[0], jnp.int32)
    points_row = points.astype(jnp.float32)
    inverse = 1.0 / points_row

    def factors(first, count, step):
        place = (first + lax.broadcasted_iota(jnp.int32, (count, lane_count), 0)) * step
        cosine, sine = turn_cos_sin(turns_of(place.astype(jnp.float32) * wave, points_row, inverse))
        return jnp.concatenate([cosine, -sine], axis=1)

    near_ref[...] = factors(0, lane_count, 1).astype(jnp.bfloat16)
    far_ref[...] = factors(0, far_ref.shape[0], lane_count)

    rotation = coriolis_ref[0]
    lane_wide = lax.broadcasted_iota(jnp.int32, (levels, lane_count), 1)
    points_wide = jnp.broadcast_to(points, (levels, lane_count))
    copies[1].wait()
    for block in range(blocks):
        vorticity, spreading, thermal = (
            grid_ref[pl.ds(field * blocks + block, levels, stride=3 * blocks), :]
            for field in range(3)
        )
        inside = lane_wide + block * lane_count < points_wide
        advanced = (
            vorticity - stepsize_delta * (rotation + vorticity) * spreading,
            spreading + stepsize_delta * (rotation * vorticity - spreading * spreading),
            thermal - stepsize_delta * thermal * spreading,
        )
        for field in range(3):
            at = block * channels + field * levels
            rhs_ref[at : at + levels, :] = jnp.where(inside, advanced[field], 0.0).astype(
                jnp.bfloat16
            )
    partial = jnp.dot(rhs_ref[...], near_ref[...], preferred_element_type=jnp.float32)
    real = jnp.zeros((channels, lane_count), jnp.float32)
    imag = jnp.zeros((channels, lane_count), jnp.float32)
    for block in range(blocks):
        part_real = partial[block * channels : (block + 1) * channels, :lane_count]
        part_imag = partial[block * channels : (block + 1) * channels, lane_count:]
        far_real = far_ref[block : block + 1, :lane_count]
        far_imag = far_ref[block : block + 1, lane_count:]
        real = real + (part_real * far_real - part_imag * far_imag)
        imag = imag + (part_real * far_imag + part_imag * far_real)
    scale = jnp.full((1, lane_count), weights_ref[0], jnp.float32) / points_row
    half_rows = 2 * per_part
    for phase, value in enumerate((real, imag)):
        turned = jnp.pad(value * scale, ((0, lane_count - channels), (0, 0))).T
        for at in range(half_rows):
            wave_ref[pl.ds(phase * half_rows + at, sources, stride=piece_rows), :] = turned[
                at * sources : (at + 1) * sources
            ]

    copies[2].wait()
    slot_total = highest + 1
    left = lane_count - channels
    for part in range(active):
        first, second = (
            jnp.pad(
                legendre_ref[0, part * per_part + index].astype(jnp.float32),
                ((0, 0), (0, lane_count - slot_total)),
            )
            for index in range(2)
        )
        upper_basis = pltpu.roll(first, channels, 1)
        lower = jnp.where(
            lane < slot_total, second, pltpu.roll(first, (slot_total - left) % lane_count, 1)
        )
        for group in range(group_count):
            at = part * group_count + group
            upper = jnp.where(
                lane < channels,
                wave_ref[at * piece_rows : (at + 1) * piece_rows, :],
                upper_basis,
            )
            sent_ref[at] = jnp.concatenate([upper, lower], axis=0).astype(jnp.bfloat16)
    for at in range(active * group_count, sources):
        sent_ref[at] = jnp.zeros((2 * piece_rows, lane_count), jnp.bfloat16)


def spectral_kernel(
    dims,
    received_ref,
    position_ref,
    pairs_ref,
    depths_ref,
    diffusion_ref,
    sent_ref,
    wave_ref,
):
    levels, lon_count, group_count, slot_count, parts, per_part, highest = dims
    channels = 3 * levels
    slot_total = highest + 1
    left = lane_count - channels
    sources = parts * group_count
    part, group = position_ref[0], position_ref[1]
    tile = (piece_rows, lane_count)
    lane = lax.broadcasted_iota(jnp.int32, tile, 1)
    for source in range(sources):
        wave_ref[source * piece_rows : (source + 1) * piece_rows, :] = received_ref[
            source, :piece_rows, :
        ].astype(jnp.float32)
    first, second = [], []
    for band in range(parts):
        piece = received_ref[band * group_count + group].astype(jnp.float32)
        upper, lower = piece[:piece_rows], piece[piece_rows:]
        start = pltpu.roll(upper, left, 1)
        rest = pltpu.roll(lower, (lane_count - (slot_total - left)) % lane_count, 1)
        first.append(jnp.where(lane < left, start, jnp.where(lane < slot_total, rest, 0.0)))
        second.append(jnp.where(lane < slot_total, lower, 0.0))
    bases = [
        jnp.concatenate(first, axis=0).astype(jnp.bfloat16),
        jnp.concatenate(second, axis=0).astype(jnp.bfloat16),
    ]
    row_tile = (1, lane_count)
    lane_row = lax.broadcasted_iota(jnp.int32, row_tile, 1)
    depth_row = jnp.zeros(row_tile, jnp.float32)
    damp_row = jnp.zeros(row_tile, jnp.float32)
    for level in range(levels):
        depth_row = jnp.where(lane_row % levels == level, depths_ref[level], depth_row)
        damp_row = jnp.where(lane_row == level, diffusion_ref[level], damp_row)
    is_first = lane_row < levels
    is_last = lane_row >= 2 * levels
    coeff_row = jnp.where(is_first, damp_row, depth_row)
    column_tile = (lane_count, 1)
    position = lax.broadcasted_iota(jnp.int32, column_tile, 0)
    for index in range(per_part):
        pair = pairs_ref[group, jnp.minimum(part * per_part + index, slot_count - 1)]
        lower_half = position < highest - pair
        total = jnp.where(lower_half, pair + position, position - 1).astype(jnp.float32)
        operator = total * (total + 1.0) / float(highest * highest)
        factor = jnp.where(is_first, operator * operator, operator)
        divisor = 1.0 + coeff_row * factor
        basis = bases[index]
        basis_turned = basis.astype(jnp.float32).T.astype(jnp.bfloat16)
        solved = []
        for phase in range(2):
            halves = []
            for half in range(2):
                at = (phase * 2 + half) * per_part + index
                waves = wave_ref[pl.ds(at, sources, stride=piece_rows), :].astype(jnp.bfloat16)
                halves.append(
                    jnp.dot(basis_turned, waves, preferred_element_type=jnp.float32)
                )
            spec = jnp.where(lower_half, halves[0], halves[1])
            thermal = pltpu.roll(spec, lane_count - levels, 1)
            top = jnp.where(is_first, spec, spec + operator * thermal)
            quotient = top / divisor
            moved = pltpu.roll(quotient, levels, 1)
            solved.append(jnp.where(is_last, spec - depth_row * moved, quotient))
        for phase in range(2):
            for half in range(2):
                at = (phase * 2 + half) * per_part + index
                kept = jnp.where(
                    lower_half if half == 0 else jnp.logical_not(lower_half), solved[phase], 0.0
                )
                back = jnp.dot(
                    basis, kept.astype(jnp.bfloat16), preferred_element_type=jnp.float32
                )
                wavenumber = pair if half == 0 else highest - 1 - pair
                doubling = jnp.where(wavenumber == 0, 1.0, 2.0)
                wave_ref[pl.ds(at, sources, stride=piece_rows), :] = back * doubling
    for source in range(sources):
        sent_ref[source] = wave_ref[
            source * piece_rows : (source + 1) * piece_rows, :
        ].astype(jnp.bfloat16)


def synthesis_kernel(
    dims, received_ref, near_ref, far_ref, points_ref, out_ref, wave_ref, rotated_ref
):
    levels, lon_count, group_count, slot_count, parts, per_part, highest = dims
    channels = 3 * levels
    blocks = lon_count // lane_count
    sources = parts * group_count
    half_rows = 2 * per_part
    for source in range(sources):
        wave_ref[source * piece_rows : (source + 1) * piece_rows, :] = received_ref[source].astype(
            jnp.float32
        )
    real, imag = (
        jnp.concatenate(
            [
                wave_ref[pl.ds(phase * half_rows + at, sources, stride=piece_rows), :]
                for at in range(half_rows)
            ],
            axis=0,
        ).T[:channels]
        for phase in range(2)
    )
    for block in range(blocks):
        far_real = far_ref[block : block + 1, :lane_count]
        far_imag = far_ref[block : block + 1, lane_count:]
        rotated_ref[block * channels : (block + 1) * channels, :] = jnp.concatenate(
            [real * far_real + imag * far_imag, imag * far_real - real * far_imag], axis=1
        ).astype(jnp.bfloat16)
    result = lax.dot_general(
        rotated_ref[...],
        near_ref[...],
        (((1,), (1,)), ((), ())),
        preferred_element_type=jnp.float32,
    )
    lane_wide = lax.broadcasted_iota(jnp.int32, (levels, lane_count), 1)
    points = points_ref[0]
    for block in range(blocks):
        inside = lane_wide + block * lane_count < points
        for field in range(3):
            at = block * channels + field * levels
            out_ref[pl.ds(field * blocks + block, levels, stride=3 * blocks), :] = jnp.where(
                inside, result[at : at + levels], 0.0
            )


def packed_body(
    dims,
    prognostic_arrays,
    coriolis,
    weights,
    row_points,
    owner_pairs,
    legendre,
    depths,
    diffusion,
):
    levels, lon_count, group_count, slot_count, parts, per_part, highest = dims
    channels = 3 * levels
    blocks = lon_count // lane_count
    sources = parts * group_count
    far_rows = -(-blocks // piece_rows) * piece_rows
    in_vmem = pl.BlockSpec(memory_space=pltpu.VMEM)
    in_smem = pl.BlockSpec(memory_space=pltpu.SMEM)
    in_hbm = pl.BlockSpec(memory_space=pltpu.HBM)
    params = pltpu.CompilerParams(vmem_limit_bytes=16 << 20)
    grid = prognostic_arrays.reshape(channels * blocks, lane_count)
    position = jnp.stack([lax.axis_index("lat"), lax.axis_index("lev")]).astype(jnp.int32)
    basis = jnp.swapaxes(legendre, 2, 3)
    sent, near, far = pl.pallas_call(
        functools.partial(analysis_kernel, dims),
        name="analysis",
        out_shape=(
            jax.ShapeDtypeStruct((sources, 2 * piece_rows, lane_count), jnp.bfloat16),
            jax.ShapeDtypeStruct((lane_count, 2 * lane_count), jnp.bfloat16),
            jax.ShapeDtypeStruct((far_rows, 2 * lane_count), jnp.float32),
        ),
        in_specs=[in_hbm, in_smem, in_smem, in_smem, in_hbm, in_hbm],
        out_specs=(in_vmem, in_vmem, in_vmem),
        scratch_shapes=[
            pltpu.VMEM(grid.shape, jnp.float32),
            pltpu.VMEM(owner_pairs.shape, jnp.int32),
            pltpu.VMEM(basis.shape, jnp.bfloat16),
            pltpu.VMEM((blocks * channels, lane_count), jnp.bfloat16),
            pltpu.VMEM((sources * piece_rows, lane_count), jnp.float32),
            pltpu.SemaphoreType.DMA((3,)),
        ],
        compiler_params=pltpu.CompilerParams(vmem_limit_bytes=67043328),
    )(grid, coriolis, weights, row_points, owner_pairs, basis)
    received = lax.all_to_all(sent, ("lat", "lev"), split_axis=0, concat_axis=0, tiled=True)
    solved = pl.pallas_call(
        functools.partial(spectral_kernel, dims),
        name="spectral",
        out_shape=jax.ShapeDtypeStruct((sources, piece_rows, lane_count), jnp.bfloat16),
        in_specs=[in_vmem, in_smem, in_smem, in_smem, in_smem],
        out_specs=in_vmem,
        scratch_shapes=[pltpu.VMEM((sources * piece_rows, lane_count), jnp.float32)],
        compiler_params=params,
    )(received, position, owner_pairs, depths, diffusion)
    returned = lax.all_to_all(solved, ("lat", "lev"), split_axis=0, concat_axis=0, tiled=True)
    updated = pl.pallas_call(
        functools.partial(synthesis_kernel, dims),
        name="synthesis",
        out_shape=jax.ShapeDtypeStruct((channels * blocks, lane_count), jnp.float32),
        in_specs=[in_vmem, in_vmem, in_vmem, in_smem],
        out_specs=in_vmem,
        scratch_shapes=[
            pltpu.VMEM((sources * piece_rows, lane_count), jnp.float32),
            pltpu.VMEM((blocks * channels, 2 * lane_count), jnp.bfloat16),
        ],
        compiler_params=params,
    )(returned, near, far, row_points)
    return updated.reshape(prognostic_arrays.shape)


def body(prognostic_arrays, coriolis, weights, row_points, owner_pairs, legendre, depths, diffusion):
    levels, _, row_count, lon_count = prognostic_arrays.shape
    group_count, slot_count = owner_pairs.shape
    slot_total, band_rows = legendre.shape[2:]
    parts = lax.axis_size("lat")
    per_part = -(-slot_count // parts)
    channels = 3 * levels
    fits = (
        row_count == 1
        and band_rows == piece_rows == group_count
        and 4 * per_part == piece_rows
        and slot_count % per_part == 0
        and lon_count % lane_count == 0
        and 2 * per_part * parts * group_count == lane_count
        and levels % 16 == 0
        and channels < slot_total <= lane_count
        and 2 * slot_total + channels <= 2 * lane_count
        and lon_count * slot_total < 2**24
    )
    arguments = (
        prognostic_arrays, coriolis, weights, row_points, owner_pairs, legendre, depths, diffusion
    )
    if not fits:
        return general_body(*arguments)
    dims = (levels, lon_count, group_count, slot_count, parts, per_part, slot_total - 1)
    return packed_body(dims, *arguments)


def solution(mesh):
    in_specs = (
        P(None, None, ("lat", "lev"), None),
        P(("lat", "lev")),
        P(("lat", "lev")),
        P(("lat", "lev")),
        P(),
        P("lev", None, None, "lat"),
        P(),
        P(),
    )
    out_specs = P(None, None, ("lat", "lev"), None)
    return jax.shard_map(body, mesh=mesh, in_specs=in_specs, out_specs=out_specs, check_vma=False)
```

```python
import functools
import math

import jax
import jax.numpy as jnp
from jax import lax
from jax.experimental import pallas as pl
from jax.experimental.pallas import tpu as pltpu
from jax.sharding import PartitionSpec as P

stepsize_delta = 0.5


def tendencies(prognostic_arrays, coriolis):
    vorticity = prognostic_arrays[:, 0]
    spreading_rate_grid = prognostic_arrays[:, 1]
    thermal_state_grid = prognostic_arrays[:, 2]
    rotation = coriolis[None, :, None]
    advanced_curl_rate = vorticity - stepsize_delta * (rotation + vorticity) * spreading_rate_grid
    advanced_spreading_rate = spreading_rate_grid + stepsize_delta * (
        rotation * vorticity - spreading_rate_grid * spreading_rate_grid
    )
    advanced_thermal_state = (
        thermal_state_grid - stepsize_delta * thermal_state_grid * spreading_rate_grid
    )
    return jnp.stack(
        [advanced_curl_rate, advanced_spreading_rate, advanced_thermal_state], axis=1
    ).astype(jnp.bfloat16)


def owner_waves(owner_pairs, highest):
    return jnp.stack([owner_pairs, highest - 1 - owner_pairs], axis=1)


def phase_table(points, wavenumbers, lon_count):
    positions = jnp.arange(lon_count, dtype=jnp.int32)
    product = positions[None, :, None] * wavenumbers[None, None, :] % points[:, None, None]
    angle = (
        product.astype(jnp.float32) * (2.0 * math.pi / points.astype(jnp.float32))[:, None, None]
    )
    return jnp.stack([jnp.cos(angle), -jnp.sin(angle)], axis=2).astype(jnp.bfloat16)


def valid_points(points, lon_count):
    positions = jnp.arange(lon_count, dtype=jnp.int32)
    return positions[None, :] < points[:, None]


def half_mask(my_pairs, slot_total):
    positions = jnp.arange(slot_total, dtype=jnp.int32)
    return positions[None, :] < (slot_total - 1 - my_pairs)[:, None]


def implicit(summed, my_pairs, depth_part, diff_part):
    slot_total = summed.shape[3]
    slot_count = summed.shape[2]
    highest = slot_total - 1
    positions = jnp.arange(slot_total, dtype=jnp.int32)[None, :]
    first_half = positions < (highest - my_pairs)[:, None]
    total = jnp.where(first_half, my_pairs[:, None] + positions, positions - 1).astype(jnp.float32)
    harmonic_operator_spectrum = total * (total + 1.0) / float(highest * highest)
    bundled_prognostics = summed.reshape(-1, 3, 2, slot_count, slot_total)
    vorticity = bundled_prognostics[:, 0]
    spreading_rate_grid = bundled_prognostics[:, 1]
    thermal_state_grid = bundled_prognostics[:, 2]
    layer_stack_count = depth_part[:, None, None, None]
    diff_cols = diff_part[:, None, None, None]
    advanced_curl_rate = vorticity / (
        1.0 + diff_cols * harmonic_operator_spectrum * harmonic_operator_spectrum
    )
    advanced_spreading_rate = (
        spreading_rate_grid + harmonic_operator_spectrum * thermal_state_grid
    ) / (1.0 + layer_stack_count * harmonic_operator_spectrum)
    advanced_thermal_state = thermal_state_grid - layer_stack_count * advanced_spreading_rate
    piled_prognostics = jnp.stack(
        [advanced_curl_rate, advanced_spreading_rate, advanced_thermal_state], axis=1
    )
    return piled_prognostics.reshape(summed.shape).astype(jnp.bfloat16)


def general_body(
    prognostic_arrays, coriolis, weights, row_points, owner_pairs, legendre, depths, diffusion
):
    levels = prognostic_arrays.shape[0]
    row_count = prognostic_arrays.shape[2]
    lon_count = prognostic_arrays.shape[3]
    group_count = owner_pairs.shape[0]
    slot_count = owner_pairs.shape[1]
    local_basis = legendre[0]
    slot_total = local_basis.shape[1]
    highest = slot_total - 1
    channels = levels * 3
    packed = channels * 4 * slot_count
    wavenumbers = owner_waves(owner_pairs, highest).reshape(-1)
    valid = valid_points(row_points, lon_count)
    gridded = tendencies(prognostic_arrays, coriolis).reshape(channels, row_count, lon_count)
    gridded = jnp.where(valid[None], gridded, jnp.zeros((), gridded.dtype))
    phases = phase_table(row_points, wavenumbers, lon_count).reshape(
        row_count, lon_count, 2, group_count, 2, slot_count
    )
    row_scale = weights / row_points.astype(jnp.float32)
    fourier = jnp.einsum("crx,rxqght->grcqht", gridded, phases, preferred_element_type=jnp.float32)
    fourier = (fourier * row_scale[None, :, None, None, None, None]).astype(jnp.bfloat16)
    band_data = lax.all_to_all(
        fourier.reshape(group_count, row_count, packed),
        "lev",
        split_axis=0,
        concat_axis=0,
        tiled=True,
    )
    band_block = band_data.reshape(group_count * row_count, channels, 2, 2, slot_count)
    owner_index = lax.axis_index("lev")
    my_pairs = lax.dynamic_index_in_dim(owner_pairs, owner_index, 0, keepdims=False)
    first_half = half_mask(my_pairs, slot_total)
    half_masks = jnp.stack([first_half, jnp.logical_not(first_half)], axis=0)
    doubling = jnp.where(owner_waves(my_pairs[None], highest)[0] == 0, 1.0, 2.0).astype(jnp.float32)
    both_halves = jnp.einsum(
        "lkqht,tpl->kqhtp", band_block, local_basis, preferred_element_type=jnp.float32
    )
    summed = lax.psum(jnp.where(first_half, both_halves[:, :, 0], both_halves[:, :, 1]), "lat")
    solved = implicit(summed, my_pairs, depths, diffusion)
    masked_spec = jnp.where(half_masks[None, None], solved[:, :, None], jnp.zeros((), solved.dtype))
    inverted = jnp.einsum(
        "kqhtp,tpl->lkqht", masked_spec, local_basis, preferred_element_type=jnp.float32
    )
    inverted = (inverted * doubling[None, None, None]).astype(jnp.bfloat16)
    returned = lax.all_to_all(
        inverted.reshape(group_count, row_count, packed),
        "lev",
        split_axis=0,
        concat_axis=0,
        tiled=True,
    )
    returned = returned.reshape(group_count, row_count, channels, 2, 2, slot_count)
    outgrid = jnp.einsum("grcqht,rxqght->crx", returned, phases, preferred_element_type=jnp.float32)
    outgrid = jnp.where(valid[None], outgrid, jnp.zeros((), outgrid.dtype))
    return outgrid.reshape(levels, 3, row_count, lon_count)


lane_count = 128
piece_rows = 8


def turn_cos_sin(turns):
    scaled = turns * 4.0
    nearest = jnp.floor(scaled + 0.5)
    arc = (scaled - nearest) * (0.5 * math.pi)
    square = arc * arc
    sine = arc + arc * square * (
        -1.6666654611e-1 + square * (8.3321608736e-3 + square * -1.9515295891e-4)
    )
    cosine = (
        1.0
        - 0.5 * square
        + square
        * square
        * (4.166664568298827e-2 + square * (-1.388731625493765e-3 + square * 2.443315711809948e-5))
    )
    swapped = jnp.logical_or(nearest == 1.0, nearest == 3.0)
    cos_part = jnp.where(swapped, sine, cosine)
    sin_part = jnp.where(swapped, cosine, sine)
    cos_part = jnp.where(jnp.logical_or(nearest == 1.0, nearest == 2.0), -cos_part, cos_part)
    sin_part = jnp.where(jnp.logical_or(nearest == 2.0, nearest == 3.0), -sin_part, sin_part)
    return cos_part, sin_part


def turns_of(product, points, inverse):
    rest = product - jnp.floor(product * inverse) * points
    rest = jnp.where(rest < 0.0, rest + points, rest)
    rest = jnp.where(rest >= points, rest - points, rest)
    return rest * inverse


def analysis_kernel(
    dims,
    grid_hbm,
    coriolis_hbm,
    weights_hbm,
    points_hbm,
    pairs_hbm,
    legendre_hbm,
    sent_ref,
    near_ref,
    far_ref,
    grid_ref,
    coriolis_ref,
    weights_ref,
    points_ref,
    pairs_ref,
    legendre_ref,
    rhs_ref,
    wave_ref,
    sems,
):
    levels, lon_count, group_count, slot_count, parts, per_part, highest = dims
    channels = 3 * levels
    blocks = lon_count // lane_count
    active = slot_count // per_part
    sources = parts * group_count
    copies = [
        pltpu.make_async_copy(source, target, sems.at[at])
        for at, (source, target) in enumerate(
            (
                (pairs_hbm, pairs_ref),
                (points_hbm, points_ref),
                (grid_hbm, grid_ref),
                (coriolis_hbm, coriolis_ref),
                (weights_hbm, weights_ref),
                (legendre_hbm, legendre_ref),
            )
        )
    ]
    for copy in copies:
        copy.start()
    copies[0].wait()
    copies[1].wait()

    tile = (piece_rows, lane_count)
    row = lax.broadcasted_iota(jnp.int32, tile, 0)
    lane = lax.broadcasted_iota(jnp.int32, tile, 1)
    lane_slot = lane // group_count % parts * per_part + lane // sources % per_part
    at_group = lane % group_count == row
    pairs = pairs_ref[...].astype(jnp.float32)
    spread = jnp.zeros(tile, jnp.float32)
    for slot in range(slot_count):
        chosen = jnp.logical_and(at_group, lane_slot == slot)
        spread = jnp.where(chosen, pairs[:, slot : slot + 1], spread)
    pair = jnp.sum(spread, axis=0, keepdims=True)
    lane_row = lax.broadcasted_iota(jnp.int32, (1, lane_count), 1)
    wave = jnp.where(lane_row >= per_part * sources, float(highest - 1) - pair, pair)
    points = jnp.full((1, lane_count), points_ref[0], jnp.int32)
    points_row = points.astype(jnp.float32)
    inverse = 1.0 / points_row

    def factors(first, count, step):
        place = (first + lax.broadcasted_iota(jnp.int32, (count, lane_count), 0)) * step
        cosine, sine = turn_cos_sin(turns_of(place.astype(jnp.float32) * wave, points_row, inverse))
        return jnp.concatenate([cosine, -sine], axis=1)

    near_ref[...] = factors(0, lane_count, 1).astype(jnp.bfloat16)
    far_ref[...] = factors(0, far_ref.shape[0], lane_count)

    copies[3].wait()
    rotation = coriolis_ref[0]
    lane_wide = lax.broadcasted_iota(jnp.int32, (levels, lane_count), 1)
    points_wide = jnp.broadcast_to(points, (levels, lane_count))
    copies[2].wait()
    for block in range(blocks):
        vorticity, spreading, thermal = (
            grid_ref[pl.ds(field * blocks + block, levels, stride=3 * blocks), :]
            for field in range(3)
        )
        inside = lane_wide + block * lane_count < points_wide
        advanced = (
            vorticity - stepsize_delta * (rotation + vorticity) * spreading,
            spreading + stepsize_delta * (rotation * vorticity - spreading * spreading),
            thermal - stepsize_delta * thermal * spreading,
        )
        for field in range(3):
            at = block * channels + field * levels
            rhs_ref[at : at + levels, :] = jnp.where(inside, advanced[field], 0.0).astype(
                jnp.bfloat16
            )
    partial = jnp.dot(rhs_ref[...], near_ref[...], preferred_element_type=jnp.float32)
    real = jnp.zeros((channels, lane_count), jnp.float32)
    imag = jnp.zeros((channels, lane_count), jnp.float32)
    for block in range(blocks):
        part_real = partial[block * channels : (block + 1) * channels, :lane_count]
        part_imag = partial[block * channels : (block + 1) * channels, lane_count:]
        far_real = far_ref[block : block + 1, :lane_count]
        far_imag = far_ref[block : block + 1, lane_count:]
        real = real + (part_real * far_real - part_imag * far_imag)
        imag = imag + (part_real * far_imag + part_imag * far_real)
    copies[4].wait()
    scale = jnp.full((1, lane_count), weights_ref[0], jnp.float32) / points_row
    half_rows = 2 * per_part
    for phase, value in enumerate((real, imag)):
        turned = jnp.pad(value * scale, ((0, lane_count - channels), (0, 0))).T
        for at in range(half_rows):
            wave_ref[pl.ds(phase * half_rows + at, sources, stride=piece_rows), :] = turned[
                at * sources : (at + 1) * sources
            ]

    copies[5].wait()
    slot_total = highest + 1
    left = lane_count - channels
    for part in range(active):
        first, second = (
            jnp.pad(
                legendre_ref[0, part * per_part + index].astype(jnp.float32),
                ((0, 0), (0, lane_count - slot_total)),
            )
            for index in range(2)
        )
        upper_basis = pltpu.roll(first, channels, 1)
        lower = jnp.where(
            lane < slot_total, second, pltpu.roll(first, (slot_total - left) % lane_count, 1)
        )
        for group in range(group_count):
            at = part * group_count + group
            upper = jnp.where(
                lane < channels,
                wave_ref[at * piece_rows : (at + 1) * piece_rows, :],
                upper_basis,
            )
            sent_ref[at] = jnp.concatenate([upper, lower], axis=0).astype(jnp.bfloat16)
    for at in range(active * group_count, sources):
        sent_ref[at] = jnp.zeros((2 * piece_rows, lane_count), jnp.bfloat16)


def spectral_kernel(
    dims,
    received_ref,
    position_ref,
    pairs_ref,
    depths_ref,
    diffusion_ref,
    sent_ref,
    wave_ref,
):
    levels, lon_count, group_count, slot_count, parts, per_part, highest = dims
    channels = 3 * levels
    slot_total = highest + 1
    left = lane_count - channels
    sources = parts * group_count
    part, group = position_ref[0], position_ref[1]
    tile = (piece_rows, lane_count)
    lane = lax.broadcasted_iota(jnp.int32, tile, 1)
    for source in range(sources):
        wave_ref[source * piece_rows : (source + 1) * piece_rows, :] = received_ref[
            source, :piece_rows, :
        ].astype(jnp.float32)
    first, second = [], []
    for band in range(parts):
        piece = received_ref[band * group_count + group].astype(jnp.float32)
        upper, lower = piece[:piece_rows], piece[piece_rows:]
        start = pltpu.roll(upper, left, 1)
        rest = pltpu.roll(lower, (lane_count - (slot_total - left)) % lane_count, 1)
        first.append(jnp.where(lane < left, start, jnp.where(lane < slot_total, rest, 0.0)))
        second.append(jnp.where(lane < slot_total, lower, 0.0))
    bases = [
        jnp.concatenate(first, axis=0).astype(jnp.bfloat16),
        jnp.concatenate(second, axis=0).astype(jnp.bfloat16),
    ]
    row_tile = (1, lane_count)
    lane_row = lax.broadcasted_iota(jnp.int32, row_tile, 1)
    depth_row = jnp.zeros(row_tile, jnp.float32)
    damp_row = jnp.zeros(row_tile, jnp.float32)
    for level in range(levels):
        depth_row = jnp.where(lane_row % levels == level, depths_ref[level], depth_row)
        damp_row = jnp.where(lane_row == level, diffusion_ref[level], damp_row)
    is_first = lane_row < levels
    is_last = lane_row >= 2 * levels
    coeff_row = jnp.where(is_first, damp_row, depth_row)
    column_tile = (lane_count, 1)
    position = lax.broadcasted_iota(jnp.int32, column_tile, 0)
    for index in range(per_part):
        pair = pairs_ref[group, jnp.minimum(part * per_part + index, slot_count - 1)]
        lower_half = position < highest - pair
        total = jnp.where(lower_half, pair + position, position - 1).astype(jnp.float32)
        operator = total * (total + 1.0) / float(highest * highest)
        factor = jnp.where(is_first, operator * operator, operator)
        divisor = 1.0 + coeff_row * factor
        basis = bases[index]
        basis_turned = basis.astype(jnp.float32).T.astype(jnp.bfloat16)
        solved = []
        for phase in range(2):
            halves = []
            for half in range(2):
                at = (phase * 2 + half) * per_part + index
                waves = wave_ref[pl.ds(at, sources, stride=piece_rows), :].astype(jnp.bfloat16)
                halves.append(
                    jnp.dot(basis_turned, waves, preferred_element_type=jnp.float32)
                )
            spec = jnp.where(lower_half, halves[0], halves[1])
            thermal = pltpu.roll(spec, lane_count - levels, 1)
            top = jnp.where(is_first, spec, spec + operator * thermal)
            quotient = top / divisor
            moved = pltpu.roll(quotient, levels, 1)
            solved.append(jnp.where(is_last, spec - depth_row * moved, quotient))
        for phase in range(2):
            for half in range(2):
                at = (phase * 2 + half) * per_part + index
                kept = jnp.where(
                    lower_half if half == 0 else jnp.logical_not(lower_half), solved[phase], 0.0
                )
                back = jnp.dot(
                    basis, kept.astype(jnp.bfloat16), preferred_element_type=jnp.float32
                )
                wavenumber = pair if half == 0 else highest - 1 - pair
                doubling = jnp.where(wavenumber == 0, 1.0, 2.0)
                wave_ref[pl.ds(at, sources, stride=piece_rows), :] = back * doubling
    for source in range(sources):
        sent_ref[source] = wave_ref[
            source * piece_rows : (source + 1) * piece_rows, :
        ].astype(jnp.bfloat16)


def synthesis_kernel(
    dims, received_ref, near_ref, far_ref, points_ref, out_ref, wave_ref, rotated_ref
):
    levels, lon_count, group_count, slot_count, parts, per_part, highest = dims
    channels = 3 * levels
    blocks = lon_count // lane_count
    sources = parts * group_count
    half_rows = 2 * per_part
    for source in range(sources):
        wave_ref[source * piece_rows : (source + 1) * piece_rows, :] = received_ref[source].astype(
            jnp.float32
        )
    real, imag = (
        jnp.concatenate(
            [
                wave_ref[pl.ds(phase * half_rows + at, sources, stride=piece_rows), :]
                for at in range(half_rows)
            ],
            axis=0,
        ).T[:channels]
        for phase in range(2)
    )
    for block in range(blocks):
        far_real = far_ref[block : block + 1, :lane_count]
        far_imag = far_ref[block : block + 1, lane_count:]
        rotated_ref[block * channels : (block + 1) * channels, :] = jnp.concatenate(
            [real * far_real + imag * far_imag, imag * far_real - real * far_imag], axis=1
        ).astype(jnp.bfloat16)
    result = lax.dot_general(
        rotated_ref[...],
        near_ref[...],
        (((1,), (1,)), ((), ())),
        preferred_element_type=jnp.float32,
    )
    lane_wide = lax.broadcasted_iota(jnp.int32, (levels, lane_count), 1)
    points = points_ref[0]
    for block in range(blocks):
        inside = lane_wide + block * lane_count < points
        for field in range(3):
            at = block * channels + field * levels
            out_ref[pl.ds(field * blocks + block, levels, stride=3 * blocks), :] = jnp.where(
                inside, result[at : at + levels], 0.0
            )


def packed_body(
    dims,
    prognostic_arrays,
    coriolis,
    weights,
    row_points,
    owner_pairs,
    legendre,
    depths,
    diffusion,
):
    levels, lon_count, group_count, slot_count, parts, per_part, highest = dims
    channels = 3 * levels
    blocks = lon_count // lane_count
    sources = parts * group_count
    far_rows = -(-blocks // piece_rows) * piece_rows
    in_vmem = pl.BlockSpec(memory_space=pltpu.VMEM)
    in_smem = pl.BlockSpec(memory_space=pltpu.SMEM)
    in_hbm = pl.BlockSpec(memory_space=pltpu.HBM)
    params = pltpu.CompilerParams(vmem_limit_bytes=16 << 20)
    grid = prognostic_arrays.reshape(channels * blocks, lane_count)
    position = jnp.stack([lax.axis_index("lat"), lax.axis_index("lev")]).astype(jnp.int32)
    basis = jnp.swapaxes(legendre, 2, 3)
    analysis_shapes = (
        jax.ShapeDtypeStruct((sources, 2 * piece_rows, lane_count), jnp.bfloat16),
        jax.ShapeDtypeStruct((lane_count, 2 * lane_count), jnp.bfloat16),
        jax.ShapeDtypeStruct((far_rows, 2 * lane_count), jnp.float32),
    )
    analysis = pl.pallas_call(
        functools.partial(analysis_kernel, dims),
        name="analysis",
        out_shape=analysis_shapes,
        in_specs=[in_hbm] * 6,
        out_specs=(in_vmem, in_vmem, in_vmem),
        scratch_shapes=[
            pltpu.VMEM(grid.shape, jnp.float32),
            pltpu.SMEM((1,), jnp.float32),
            pltpu.SMEM((1,), jnp.float32),
            pltpu.SMEM((1,), jnp.int32),
            pltpu.VMEM(owner_pairs.shape, jnp.int32),
            pltpu.VMEM(basis.shape, jnp.bfloat16),
            pltpu.VMEM((blocks * channels, lane_count), jnp.bfloat16),
            pltpu.VMEM((sources * piece_rows, lane_count), jnp.float32),
            pltpu.SemaphoreType.DMA((6,)),
        ],
        compiler_params=pltpu.CompilerParams(vmem_limit_bytes=67043328),
    )
    sent, near, far = lax.cond(
        position[0] >= 0,
        lambda *inputs: tuple(analysis(*inputs)),
        lambda *inputs: tuple(jnp.zeros(made.shape, made.dtype) for made in analysis_shapes),
        grid,
        coriolis,
        weights,
        row_points,
        owner_pairs,
        basis,
    )
    received = lax.all_to_all(sent, ("lat", "lev"), split_axis=0, concat_axis=0, tiled=True)
    solved = pl.pallas_call(
        functools.partial(spectral_kernel, dims),
        name="spectral",
        out_shape=jax.ShapeDtypeStruct((sources, piece_rows, lane_count), jnp.bfloat16),
        in_specs=[in_vmem, in_smem, in_smem, in_smem, in_smem],
        out_specs=in_vmem,
        scratch_shapes=[pltpu.VMEM((sources * piece_rows, lane_count), jnp.float32)],
        compiler_params=params,
    )(received, position, owner_pairs, depths, diffusion)
    returned = lax.all_to_all(solved, ("lat", "lev"), split_axis=0, concat_axis=0, tiled=True)
    updated = pl.pallas_call(
        functools.partial(synthesis_kernel, dims),
        name="synthesis",
        out_shape=jax.ShapeDtypeStruct((channels * blocks, lane_count), jnp.float32),
        in_specs=[in_vmem, in_vmem, in_vmem, in_smem],
        out_specs=in_vmem,
        scratch_shapes=[
            pltpu.VMEM((sources * piece_rows, lane_count), jnp.float32),
            pltpu.VMEM((blocks * channels, 2 * lane_count), jnp.bfloat16),
        ],
        compiler_params=params,
    )(returned, near, far, row_points)
    return updated.reshape(prognostic_arrays.shape)


def body(prognostic_arrays, coriolis, weights, row_points, owner_pairs, legendre, depths, diffusion):
    levels, _, row_count, lon_count = prognostic_arrays.shape
    group_count, slot_count = owner_pairs.shape
    slot_total, band_rows = legendre.shape[2:]
    parts = lax.axis_size("lat")
    per_part = -(-slot_count // parts)
    channels = 3 * levels
    fits = (
        row_count == 1
        and band_rows == piece_rows == group_count
        and 4 * per_part == piece_rows
        and slot_count % per_part == 0
        and lon_count % lane_count == 0
        and 2 * per_part * parts * group_count == lane_count
        and levels % 16 == 0
        and channels < slot_total <= lane_count
        and 2 * slot_total + channels <= 2 * lane_count
        and lon_count * slot_total < 2**24
    )
    arguments = (
        prognostic_arrays, coriolis, weights, row_points, owner_pairs, legendre, depths, diffusion
    )
    if not fits:
        return general_body(*arguments)
    dims = (levels, lon_count, group_count, slot_count, parts, per_part, slot_total - 1)
    return packed_body(dims, *arguments)


def solution(mesh):
    in_specs = (
        P(None, None, ("lat", "lev"), None),
        P(("lat", "lev")),
        P(("lat", "lev")),
        P(("lat", "lev")),
        P(),
        P("lev", None, None, "lat"),
        P(),
        P(),
    )
    out_specs = P(None, None, ("lat", "lev"), None)
    return jax.shard_map(body, mesh=mesh, in_specs=in_specs, out_specs=out_specs, check_vma=False)
```

```python
import functools
import math

import jax
import jax.numpy as jnp
from jax import lax
from jax.experimental import pallas as pl
from jax.experimental.pallas import tpu as pltpu
from jax.sharding import PartitionSpec as P

stepsize_delta = 0.5


def tendencies(prognostic_arrays, coriolis):
    vorticity = prognostic_arrays[:, 0]
    spreading_rate_grid = prognostic_arrays[:, 1]
    thermal_state_grid = prognostic_arrays[:, 2]
    rotation = coriolis[None, :, None]
    advanced_curl_rate = vorticity - stepsize_delta * (rotation + vorticity) * spreading_rate_grid
    advanced_spreading_rate = spreading_rate_grid + stepsize_delta * (
        rotation * vorticity - spreading_rate_grid * spreading_rate_grid
    )
    advanced_thermal_state = (
        thermal_state_grid - stepsize_delta * thermal_state_grid * spreading_rate_grid
    )
    return jnp.stack(
        [advanced_curl_rate, advanced_spreading_rate, advanced_thermal_state], axis=1
    ).astype(jnp.bfloat16)


def owner_waves(owner_pairs, highest):
    return jnp.stack([owner_pairs, highest - 1 - owner_pairs], axis=1)


def phase_table(points, wavenumbers, lon_count):
    positions = jnp.arange(lon_count, dtype=jnp.int32)
    product = positions[None, :, None] * wavenumbers[None, None, :] % points[:, None, None]
    angle = (
        product.astype(jnp.float32) * (2.0 * math.pi / points.astype(jnp.float32))[:, None, None]
    )
    return jnp.stack([jnp.cos(angle), -jnp.sin(angle)], axis=2).astype(jnp.bfloat16)


def valid_points(points, lon_count):
    positions = jnp.arange(lon_count, dtype=jnp.int32)
    return positions[None, :] < points[:, None]


def half_mask(my_pairs, slot_total):
    positions = jnp.arange(slot_total, dtype=jnp.int32)
    return positions[None, :] < (slot_total - 1 - my_pairs)[:, None]


def implicit(summed, my_pairs, depth_part, diff_part):
    slot_total = summed.shape[3]
    slot_count = summed.shape[2]
    highest = slot_total - 1
    positions = jnp.arange(slot_total, dtype=jnp.int32)[None, :]
    first_half = positions < (highest - my_pairs)[:, None]
    total = jnp.where(first_half, my_pairs[:, None] + positions, positions - 1).astype(jnp.float32)
    harmonic_operator_spectrum = total * (total + 1.0) / float(highest * highest)
    bundled_prognostics = summed.reshape(-1, 3, 2, slot_count, slot_total)
    vorticity = bundled_prognostics[:, 0]
    spreading_rate_grid = bundled_prognostics[:, 1]
    thermal_state_grid = bundled_prognostics[:, 2]
    layer_stack_count = depth_part[:, None, None, None]
    diff_cols = diff_part[:, None, None, None]
    advanced_curl_rate = vorticity / (
        1.0 + diff_cols * harmonic_operator_spectrum * harmonic_operator_spectrum
    )
    advanced_spreading_rate = (
        spreading_rate_grid + harmonic_operator_spectrum * thermal_state_grid
    ) / (1.0 + layer_stack_count * harmonic_operator_spectrum)
    advanced_thermal_state = thermal_state_grid - layer_stack_count * advanced_spreading_rate
    piled_prognostics = jnp.stack(
        [advanced_curl_rate, advanced_spreading_rate, advanced_thermal_state], axis=1
    )
    return piled_prognostics.reshape(summed.shape).astype(jnp.bfloat16)


def general_body(
    prognostic_arrays, coriolis, weights, row_points, owner_pairs, legendre, depths, diffusion
):
    levels = prognostic_arrays.shape[0]
    row_count = prognostic_arrays.shape[2]
    lon_count = prognostic_arrays.shape[3]
    group_count = owner_pairs.shape[0]
    slot_count = owner_pairs.shape[1]
    local_basis = legendre[0]
    slot_total = local_basis.shape[1]
    highest = slot_total - 1
    channels = levels * 3
    packed = channels * 4 * slot_count
    wavenumbers = owner_waves(owner_pairs, highest).reshape(-1)
    valid = valid_points(row_points, lon_count)
    gridded = tendencies(prognostic_arrays, coriolis).reshape(channels, row_count, lon_count)
    gridded = jnp.where(valid[None], gridded, jnp.zeros((), gridded.dtype))
    phases = phase_table(row_points, wavenumbers, lon_count).reshape(
        row_count, lon_count, 2, group_count, 2, slot_count
    )
    row_scale = weights / row_points.astype(jnp.float32)
    fourier = jnp.einsum("crx,rxqght->grcqht", gridded, phases, preferred_element_type=jnp.float32)
    fourier = (fourier * row_scale[None, :, None, None, None, None]).astype(jnp.bfloat16)
    band_data = lax.all_to_all(
        fourier.reshape(group_count, row_count, packed),
        "lev",
        split_axis=0,
        concat_axis=0,
        tiled=True,
    )
    band_block = band_data.reshape(group_count * row_count, channels, 2, 2, slot_count)
    owner_index = lax.axis_index("lev")
    my_pairs = lax.dynamic_index_in_dim(owner_pairs, owner_index, 0, keepdims=False)
    first_half = half_mask(my_pairs, slot_total)
    half_masks = jnp.stack([first_half, jnp.logical_not(first_half)], axis=0)
    doubling = jnp.where(owner_waves(my_pairs[None], highest)[0] == 0, 1.0, 2.0).astype(jnp.float32)
    both_halves = jnp.einsum(
        "lkqht,tpl->kqhtp", band_block, local_basis, preferred_element_type=jnp.float32
    )
    summed = lax.psum(jnp.where(first_half, both_halves[:, :, 0], both_halves[:, :, 1]), "lat")
    solved = implicit(summed, my_pairs, depths, diffusion)
    masked_spec = jnp.where(half_masks[None, None], solved[:, :, None], jnp.zeros((), solved.dtype))
    inverted = jnp.einsum(
        "kqhtp,tpl->lkqht", masked_spec, local_basis, preferred_element_type=jnp.float32
    )
    inverted = (inverted * doubling[None, None, None]).astype(jnp.bfloat16)
    returned = lax.all_to_all(
        inverted.reshape(group_count, row_count, packed),
        "lev",
        split_axis=0,
        concat_axis=0,
        tiled=True,
    )
    returned = returned.reshape(group_count, row_count, channels, 2, 2, slot_count)
    outgrid = jnp.einsum("grcqht,rxqght->crx", returned, phases, preferred_element_type=jnp.float32)
    outgrid = jnp.where(valid[None], outgrid, jnp.zeros((), outgrid.dtype))
    return outgrid.reshape(levels, 3, row_count, lon_count)


lane_count = 128
piece_rows = 8


def turn_cos_sin(turns):
    scaled = turns * 4.0
    nearest = jnp.floor(scaled + 0.5)
    arc = (scaled - nearest) * (0.5 * math.pi)
    square = arc * arc
    sine = arc + arc * square * (
        -1.6666654611e-1 + square * (8.3321608736e-3 + square * -1.9515295891e-4)
    )
    cosine = (
        1.0
        - 0.5 * square
        + square
        * square
        * (4.166664568298827e-2 + square * (-1.388731625493765e-3 + square * 2.443315711809948e-5))
    )
    swapped = jnp.logical_or(nearest == 1.0, nearest == 3.0)
    cos_part = jnp.where(swapped, sine, cosine)
    sin_part = jnp.where(swapped, cosine, sine)
    cos_part = jnp.where(jnp.logical_or(nearest == 1.0, nearest == 2.0), -cos_part, cos_part)
    sin_part = jnp.where(jnp.logical_or(nearest == 2.0, nearest == 3.0), -sin_part, sin_part)
    return cos_part, sin_part


def turns_of(product, points, inverse):
    rest = product - jnp.floor(product * inverse) * points
    rest = jnp.where(rest < 0.0, rest + points, rest)
    rest = jnp.where(rest >= points, rest - points, rest)
    return rest * inverse


def wave_row(dims, pairs):
    levels, lon_count, group_count, slot_count, parts, per_part, highest = dims
    sources = parts * group_count
    tile = (piece_rows, lane_count)
    row = lax.broadcasted_iota(jnp.int32, tile, 0)
    lane = lax.broadcasted_iota(jnp.int32, tile, 1)
    lane_slot = lane // group_count % parts * per_part + lane // sources % per_part
    at_group = lane % group_count == row
    spread = jnp.zeros(tile, jnp.float32)
    for slot in range(slot_count):
        chosen = jnp.logical_and(at_group, lane_slot == slot)
        spread = jnp.where(chosen, pairs[:, slot : slot + 1].astype(jnp.float32), spread)
    pair = jnp.sum(spread, axis=0, keepdims=True)
    lane_row = lax.broadcasted_iota(jnp.int32, (1, lane_count), 1)
    return jnp.where(lane_row >= per_part * sources, float(highest - 1) - pair, pair)


def factors(count, step, wave, points_row):
    place = lax.broadcasted_iota(jnp.int32, (count, lane_count), 0) * step
    cosine, sine = turn_cos_sin(
        turns_of(place.astype(jnp.float32) * wave, points_row, 1.0 / points_row)
    )
    return jnp.concatenate([cosine, -sine], axis=1)


def pair_rows(units):
    if len(units) % 2:
        units = units + [jnp.zeros_like(units[0])]
    return [jnp.concatenate(units[at : at + 2], axis=0) for at in range(0, len(units), 2)]


def analysis_kernel(
    dims,
    grid_hbm,
    coriolis_ref,
    weights_ref,
    points_ref,
    pairs_hbm,
    legendre_hbm,
    sent_ref,
    grid_ref,
    pairs_ref,
    legendre_ref,
    near_ref,
    far_ref,
    rhs_ref,
    wave_ref,
    sems,
):
    levels, lon_count, group_count, slot_count, parts, per_part, highest = dims
    channels = 3 * levels
    blocks = lon_count // lane_count
    active = slot_count // per_part
    sources = parts * group_count
    level_rows = 3 * blocks
    chunks = levels // piece_rows
    chunk_rows = piece_rows * level_rows
    copies = [pltpu.make_async_copy(pairs_hbm, pairs_ref, sems.at[0])]
    for chunk in range(chunks):
        rows = pl.ds(chunk * chunk_rows, chunk_rows)
        copies.append(
            pltpu.make_async_copy(grid_hbm.at[rows], grid_ref.at[rows], sems.at[1 + chunk])
        )
    copies.append(pltpu.make_async_copy(legendre_hbm, legendre_ref, sems.at[1 + chunks]))
    for copy in copies:
        copy.start()
    copies[0].wait()

    points = points_ref[0]
    points_row = jnp.full((1, lane_count), points, jnp.int32).astype(jnp.float32)
    wave = wave_row(dims, pairs_ref[...])
    near_ref[...] = factors(lane_count, 1, wave, points_row).astype(jnp.bfloat16)
    far_ref[...] = factors(far_ref.shape[0], lane_count, wave, points_row)
    rotation = coriolis_ref[0]
    tile = (piece_rows, lane_count)
    lane = lax.broadcasted_iota(jnp.int32, tile, 1)
    padded = (level_rows + level_rows % 2) * piece_rows
    real = [None] * (3 * chunks)
    imag = [None] * (3 * chunks)
    for chunk in range(chunks):
        copies[1 + chunk].wait()
        units = []
        for field in range(3):
            for block in range(blocks):

                def load(which):
                    at = chunk * chunk_rows + which * blocks + block
                    return grid_ref[pl.ds(at, piece_rows, stride=level_rows), :]

                spreading = load(1)
                if field == 0:
                    vorticity = load(0)
                    value = vorticity - stepsize_delta * (rotation + vorticity) * spreading
                elif field == 1:
                    value = spreading + stepsize_delta * (
                        rotation * load(0) - spreading * spreading
                    )
                else:
                    thermal = load(2)
                    value = thermal - stepsize_delta * thermal * spreading
                units.append(jnp.where(lane < points - block * lane_count, value, 0.0))
        for at, two in enumerate(pair_rows(units)):
            start = chunk * padded + at * 2 * piece_rows
            rhs_ref[start : start + 2 * piece_rows, :] = two.astype(jnp.bfloat16)
        partial = jnp.dot(
            rhs_ref[chunk * padded : (chunk + 1) * padded, :],
            near_ref[...],
            preferred_element_type=jnp.float32,
        )
        for field in range(3):
            for block in range(blocks):
                at = (field * blocks + block) * piece_rows
                part_real = partial[at : at + piece_rows, :lane_count]
                part_imag = partial[at : at + piece_rows, lane_count:]
                far_real = far_ref[block : block + 1, :lane_count]
                far_imag = far_ref[block : block + 1, lane_count:]
                add_real = part_real * far_real - part_imag * far_imag
                add_imag = part_real * far_imag + part_imag * far_real
                total = field * chunks + chunk
                real[total] = add_real if block == 0 else real[total] + add_real
                imag[total] = add_imag if block == 0 else imag[total] + add_imag
    scale = jnp.full((1, lane_count), weights_ref[0], jnp.float32) / points_row
    half_rows = 2 * per_part
    rest = jnp.zeros((lane_count - channels, lane_count), jnp.float32)
    for phase, values in enumerate((real, imag)):
        turned = jnp.concatenate([value * scale for value in values] + [rest], axis=0).T
        for at in range(half_rows):
            wave_ref[pl.ds(phase * half_rows + at, sources, stride=piece_rows), :] = turned[
                at * sources : (at + 1) * sources
            ]

    copies[1 + chunks].wait()
    slot_total = highest + 1
    left = lane_count - channels
    for part in range(active):
        first, second = (
            jnp.pad(
                legendre_ref[0, part * per_part + index].astype(jnp.float32),
                ((0, 0), (0, lane_count - slot_total)),
            )
            for index in range(2)
        )
        upper_basis = pltpu.roll(first, channels, 1)
        lower = jnp.where(
            lane < slot_total, second, pltpu.roll(first, (slot_total - left) % lane_count, 1)
        )
        for group in range(group_count):
            at = part * group_count + group
            upper = jnp.where(
                lane < channels,
                wave_ref[at * piece_rows : (at + 1) * piece_rows, :],
                upper_basis,
            )
            sent_ref[at] = jnp.concatenate([upper, lower], axis=0).astype(jnp.bfloat16)
    for at in range(active * group_count, sources):
        sent_ref[at] = jnp.zeros((2 * piece_rows, lane_count), jnp.bfloat16)


def prepare_kernel(
    dims,
    part_ref,
    group_ref,
    points_ref,
    table_ref,
    pairs_ref,
    depths_ref,
    diffusion_ref,
    near_ref,
    far_ref,
    solve_ref,
    rows_ref,
):
    levels, lon_count, group_count, slot_count, parts, per_part, highest = dims
    points_row = jnp.full((1, lane_count), points_ref[0], jnp.int32).astype(jnp.float32)
    wave = wave_row(dims, table_ref[...])
    near_ref[...] = factors(lane_count, 1, wave, points_row).astype(jnp.bfloat16)
    far_ref[...] = factors(far_ref.shape[0], lane_count, wave, points_row)

    part, group = part_ref[0], group_ref[0]
    lane_row = lax.broadcasted_iota(jnp.int32, (1, lane_count), 1)
    depth_row = jnp.zeros((1, lane_count), jnp.float32)
    damp_row = jnp.zeros((1, lane_count), jnp.float32)
    for level in range(levels):
        depth_row = jnp.where(lane_row % levels == level, depths_ref[level], depth_row)
        damp_row = jnp.where(lane_row == level, diffusion_ref[level], damp_row)
    is_first = lane_row < levels
    coeff_row = jnp.where(is_first, damp_row, depth_row)
    rows_ref[0:1, :] = depth_row
    position = lax.broadcasted_iota(jnp.int32, (lane_count, lane_count), 0)
    for index in range(per_part):
        pair = pairs_ref[group, jnp.minimum(part * per_part + index, slot_count - 1)]
        lower_half = position < highest - pair
        total = jnp.where(lower_half, pair + position, position - 1).astype(jnp.float32)
        operator = total * (total + 1.0) / float(highest * highest)
        factor = jnp.where(is_first, operator * operator, operator)
        solve_ref[3 * index] = 1.0 + coeff_row * factor
        solve_ref[3 * index + 1] = jnp.where(is_first, 0.0, operator)
        solve_ref[3 * index + 2] = jnp.where(lower_half, 1.0, 0.0)
        for half in range(2):
            wavenumber = pair if half == 0 else highest - 1 - pair
            at = 1 + half * per_part + index
            rows_ref[at : at + 1, :] = jnp.full(
                (1, lane_count), jnp.where(wavenumber == 0, 1.0, 2.0), jnp.float32
            )


def spectral_kernel(dims, received_ref, group_ref, solve_ref, rows_ref, sent_ref, wave_ref):
    levels, lon_count, group_count, slot_count, parts, per_part, highest = dims
    channels = 3 * levels
    slot_total = highest + 1
    left = lane_count - channels
    sources = parts * group_count
    group = group_ref[0]
    lane = lax.broadcasted_iota(jnp.int32, (piece_rows, lane_count), 1)
    for source in range(sources):
        wave_ref[source * piece_rows : (source + 1) * piece_rows, :] = received_ref[
            source, :piece_rows, :
        ].astype(jnp.float32)
    first, second = [], []
    for band in range(parts):
        piece = received_ref[band * group_count + group].astype(jnp.float32)
        upper, lower = piece[:piece_rows], piece[piece_rows:]
        start = pltpu.roll(upper, left, 1)
        rest = pltpu.roll(lower, (lane_count - (slot_total - left)) % lane_count, 1)
        first.append(jnp.where(lane < left, start, jnp.where(lane < slot_total, rest, 0.0)))
        second.append(jnp.where(lane < slot_total, lower, 0.0))
    bases = [jnp.concatenate(first, axis=0), jnp.concatenate(second, axis=0)]
    lane_row = lax.broadcasted_iota(jnp.int32, (1, lane_count), 1)
    is_last = lane_row >= 2 * levels
    depth_row = rows_ref[0:1, :]
    for index in range(per_part):
        basis = bases[index].astype(jnp.bfloat16)
        basis_turned = bases[index].T.astype(jnp.bfloat16)
        specs = []
        for half in range(2):
            waves = jnp.concatenate(
                [
                    wave_ref[
                        pl.ds((phase * 2 + half) * per_part + index, sources, stride=piece_rows), :
                    ]
                    for phase in range(2)
                ],
                axis=1,
            ).astype(jnp.bfloat16)
            specs.append(jnp.dot(basis_turned, waves, preferred_element_type=jnp.float32))
        lower_half = solve_ref[3 * index + 2] > 0.5
        solved = []
        for phase in range(2):
            lanes = slice(phase * lane_count, (phase + 1) * lane_count)
            spec = jnp.where(lower_half, specs[0][:, lanes], specs[1][:, lanes])
            thermal = pltpu.roll(spec, lane_count - levels, 1)
            quotient = (spec + solve_ref[3 * index + 1] * thermal) / solve_ref[3 * index]
            moved = pltpu.roll(quotient, levels, 1)
            solved.append(jnp.where(is_last, spec - depth_row * moved, quotient))
        for half in range(2):
            kept = jnp.concatenate(
                [
                    jnp.where(lower_half, value, 0.0)
                    if half == 0
                    else jnp.where(lower_half, 0.0, value)
                    for value in solved
                ],
                axis=1,
            ).astype(jnp.bfloat16)
            back = jnp.dot(basis, kept, preferred_element_type=jnp.float32)
            row = 1 + half * per_part + index
            doubling = rows_ref[row : row + 1, :]
            for phase in range(2):
                at = (phase * 2 + half) * per_part + index
                wave_ref[pl.ds(at, sources, stride=piece_rows), :] = (
                    back[:, phase * lane_count : (phase + 1) * lane_count] * doubling
                )
    for source in range(sources):
        sent_ref[source] = wave_ref[
            source * piece_rows : (source + 1) * piece_rows, :
        ].astype(jnp.bfloat16)


def synthesis_kernel(
    dims,
    received_ref,
    near_ref,
    far_ref,
    points_ref,
    out_hbm,
    wave_ref,
    rotated_ref,
    out_ref,
    sems,
):
    levels, lon_count, group_count, slot_count, parts, per_part, highest = dims
    blocks = lon_count // lane_count
    sources = parts * group_count
    half_rows = 2 * per_part
    level_rows = 3 * blocks
    chunks = levels // piece_rows
    chunk_rows = piece_rows * level_rows
    padded = (level_rows + level_rows % 2) * piece_rows
    for source in range(sources):
        wave_ref[source * piece_rows : (source + 1) * piece_rows, :] = received_ref[source].astype(
            jnp.float32
        )
    real, imag = (
        jnp.concatenate(
            [
                wave_ref[pl.ds(phase * half_rows + at, sources, stride=piece_rows), :]
                for at in range(half_rows)
            ],
            axis=0,
        ).T
        for phase in range(2)
    )
    points = points_ref[0]
    lane = lax.broadcasted_iota(jnp.int32, (piece_rows, lane_count), 1)
    copies = []
    for chunk in range(chunks):
        units = []
        for field in range(3):
            at = field * levels + chunk * piece_rows
            part_real, part_imag = real[at : at + piece_rows], imag[at : at + piece_rows]
            for block in range(blocks):
                far_real = far_ref[block : block + 1, :lane_count]
                far_imag = far_ref[block : block + 1, lane_count:]
                units.append(
                    jnp.concatenate(
                        [
                            part_real * far_real + part_imag * far_imag,
                            part_imag * far_real - part_real * far_imag,
                        ],
                        axis=1,
                    )
                )
        for at, two in enumerate(pair_rows(units)):
            start = chunk * padded + at * 2 * piece_rows
            rotated_ref[start : start + 2 * piece_rows, :] = two.astype(jnp.bfloat16)
        result = lax.dot_general(
            rotated_ref[chunk * padded : (chunk + 1) * padded, :],
            near_ref[...],
            (((1,), (1,)), ((), ())),
            preferred_element_type=jnp.float32,
        )
        for unit in range(level_rows):
            inside = lane < points - unit % blocks * lane_count
            out_ref[pl.ds(chunk * chunk_rows + unit, piece_rows, stride=level_rows), :] = (
                jnp.where(inside, result[unit * piece_rows : (unit + 1) * piece_rows], 0.0)
            )
        rows = pl.ds(chunk * chunk_rows, chunk_rows)
        copies.append(pltpu.make_async_copy(out_ref.at[rows], out_hbm.at[rows], sems.at[chunk]))
        copies[-1].start()
    for copy in copies:
        copy.wait()


def packed_body(
    dims,
    prognostic_arrays,
    coriolis,
    weights,
    row_points,
    owner_pairs,
    legendre,
    depths,
    diffusion,
):
    levels, lon_count, group_count, slot_count, parts, per_part, highest = dims
    channels = 3 * levels
    blocks = lon_count // lane_count
    sources = parts * group_count
    far_rows = -(-blocks // piece_rows) * piece_rows
    chunks = levels // piece_rows
    padded = (3 * blocks + 3 * blocks % 2) * piece_rows * chunks
    in_vmem = pl.BlockSpec(memory_space=pltpu.VMEM)
    in_smem = pl.BlockSpec(memory_space=pltpu.SMEM)
    in_hbm = pl.BlockSpec(memory_space=pltpu.HBM)
    params = pltpu.CompilerParams(vmem_limit_bytes=16 << 20)
    grid = prognostic_arrays.reshape(channels * blocks, lane_count)
    basis = jnp.swapaxes(legendre, 2, 3)
    part = lax.axis_index("lat").astype(jnp.int32).reshape(1)
    group = lax.axis_index("lev").astype(jnp.int32).reshape(1)
    sent = pl.pallas_call(
        functools.partial(analysis_kernel, dims),
        name="analysis",
        out_shape=jax.ShapeDtypeStruct((sources, 2 * piece_rows, lane_count), jnp.bfloat16),
        in_specs=[in_hbm, in_smem, in_smem, in_smem, in_hbm, in_hbm],
        out_specs=in_vmem,
        scratch_shapes=[
            pltpu.VMEM(grid.shape, jnp.float32),
            pltpu.VMEM(owner_pairs.shape, jnp.int32),
            pltpu.VMEM(basis.shape, jnp.bfloat16),
            pltpu.VMEM((lane_count, 2 * lane_count), jnp.bfloat16),
            pltpu.VMEM((far_rows, 2 * lane_count), jnp.float32),
            pltpu.VMEM((padded, lane_count), jnp.bfloat16),
            pltpu.VMEM((sources * piece_rows, lane_count), jnp.float32),
            pltpu.SemaphoreType.DMA((2 + chunks,)),
        ],
        compiler_params=pltpu.CompilerParams(vmem_limit_bytes=67043328),
    )(grid, coriolis, weights, row_points, owner_pairs, basis)
    received = lax.all_to_all(sent, ("lat", "lev"), split_axis=0, concat_axis=0, tiled=True)
    near, far, solve, rows = pl.pallas_call(
        functools.partial(prepare_kernel, dims),
        name="prepare",
        out_shape=(
            jax.ShapeDtypeStruct((lane_count, 2 * lane_count), jnp.bfloat16),
            jax.ShapeDtypeStruct((far_rows, 2 * lane_count), jnp.float32),
            jax.ShapeDtypeStruct((3 * per_part, lane_count, lane_count), jnp.float32),
            jax.ShapeDtypeStruct((piece_rows, lane_count), jnp.float32),
        ),
        in_specs=[in_smem, in_smem, in_smem, in_vmem, in_smem, in_smem, in_smem],
        out_specs=(in_vmem,) * 4,
        compiler_params=params,
        cost_estimate=pl.CostEstimate(
            flops=40 * lane_count * lane_count, bytes_accessed=1 << 19, transcendentals=0
        ),
    )(part, group, row_points, owner_pairs, owner_pairs, depths, diffusion)
    solved = pl.pallas_call(
        functools.partial(spectral_kernel, dims),
        name="spectral",
        out_shape=jax.ShapeDtypeStruct((sources, piece_rows, lane_count), jnp.bfloat16),
        in_specs=[in_vmem, in_smem, in_vmem, in_vmem],
        out_specs=in_vmem,
        scratch_shapes=[pltpu.VMEM((sources * piece_rows, lane_count), jnp.float32)],
        compiler_params=params,
    )(received, group, solve, rows)
    returned = lax.all_to_all(solved, ("lat", "lev"), split_axis=0, concat_axis=0, tiled=True)
    updated = pl.pallas_call(
        functools.partial(synthesis_kernel, dims),
        name="synthesis",
        out_shape=jax.ShapeDtypeStruct((channels * blocks, lane_count), jnp.float32),
        in_specs=[in_vmem, in_vmem, in_vmem, in_smem],
        out_specs=in_hbm,
        scratch_shapes=[
            pltpu.VMEM((sources * piece_rows, lane_count), jnp.float32),
            pltpu.VMEM((padded, 2 * lane_count), jnp.bfloat16),
            pltpu.VMEM((channels * blocks, lane_count), jnp.float32),
            pltpu.SemaphoreType.DMA((chunks,)),
        ],
        compiler_params=params,
    )(returned, near, far, row_points)
    return updated.reshape(prognostic_arrays.shape)


def body(prognostic_arrays, coriolis, weights, row_points, owner_pairs, legendre, depths, diffusion):
    levels, _, row_count, lon_count = prognostic_arrays.shape
    group_count, slot_count = owner_pairs.shape
    slot_total, band_rows = legendre.shape[2:]
    parts = lax.axis_size("lat")
    per_part = -(-slot_count // parts)
    channels = 3 * levels
    fits = (
        row_count == 1
        and band_rows == piece_rows == group_count
        and 4 * per_part == piece_rows
        and slot_count % per_part == 0
        and lon_count % lane_count == 0
        and 2 * per_part * parts * group_count == lane_count
        and levels % 16 == 0
        and channels < slot_total <= lane_count
        and 2 * slot_total + channels <= 2 * lane_count
        and lon_count * slot_total < 2**24
    )
    arguments = (
        prognostic_arrays, coriolis, weights, row_points, owner_pairs, legendre, depths, diffusion
    )
    if not fits:
        return general_body(*arguments)
    dims = (levels, lon_count, group_count, slot_count, parts, per_part, slot_total - 1)
    return packed_body(dims, *arguments)


def solution(mesh):
    in_specs = (
        P(None, None, ("lat", "lev"), None),
        P(("lat", "lev")),
        P(("lat", "lev")),
        P(("lat", "lev")),
        P(),
        P("lev", None, None, "lat"),
        P(),
        P(),
    )
    out_specs = P(None, None, ("lat", "lev"), None)
    return jax.shard_map(body, mesh=mesh, in_specs=in_specs, out_specs=out_specs, check_vma=False)
```

```python
import functools
import math

import jax
import jax.numpy as jnp
from jax import lax
from jax.experimental import pallas as pl
from jax.experimental.pallas import tpu as pltpu
from jax.sharding import PartitionSpec as P

stepsize_delta = 0.5


def tendencies(prognostic_arrays, coriolis):
    vorticity = prognostic_arrays[:, 0]
    spreading_rate_grid = prognostic_arrays[:, 1]
    thermal_state_grid = prognostic_arrays[:, 2]
    rotation = coriolis[None, :, None]
    advanced_curl_rate = vorticity - stepsize_delta * (rotation + vorticity) * spreading_rate_grid
    advanced_spreading_rate = spreading_rate_grid + stepsize_delta * (
        rotation * vorticity - spreading_rate_grid * spreading_rate_grid
    )
    advanced_thermal_state = (
        thermal_state_grid - stepsize_delta * thermal_state_grid * spreading_rate_grid
    )
    return jnp.stack(
        [advanced_curl_rate, advanced_spreading_rate, advanced_thermal_state], axis=1
    ).astype(jnp.bfloat16)


def owner_waves(owner_pairs, highest):
    return jnp.stack([owner_pairs, highest - 1 - owner_pairs], axis=1)


def phase_table(points, wavenumbers, lon_count):
    positions = jnp.arange(lon_count, dtype=jnp.int32)
    product = positions[None, :, None] * wavenumbers[None, None, :] % points[:, None, None]
    angle = (
        product.astype(jnp.float32) * (2.0 * math.pi / points.astype(jnp.float32))[:, None, None]
    )
    return jnp.stack([jnp.cos(angle), -jnp.sin(angle)], axis=2).astype(jnp.bfloat16)


def valid_points(points, lon_count):
    positions = jnp.arange(lon_count, dtype=jnp.int32)
    return positions[None, :] < points[:, None]


def half_mask(my_pairs, slot_total):
    positions = jnp.arange(slot_total, dtype=jnp.int32)
    return positions[None, :] < (slot_total - 1 - my_pairs)[:, None]


def implicit(summed, my_pairs, depth_part, diff_part):
    slot_total = summed.shape[3]
    slot_count = summed.shape[2]
    highest = slot_total - 1
    positions = jnp.arange(slot_total, dtype=jnp.int32)[None, :]
    first_half = positions < (highest - my_pairs)[:, None]
    total = jnp.where(first_half, my_pairs[:, None] + positions, positions - 1).astype(jnp.float32)
    harmonic_operator_spectrum = total * (total + 1.0) / float(highest * highest)
    bundled_prognostics = summed.reshape(-1, 3, 2, slot_count, slot_total)
    vorticity = bundled_prognostics[:, 0]
    spreading_rate_grid = bundled_prognostics[:, 1]
    thermal_state_grid = bundled_prognostics[:, 2]
    layer_stack_count = depth_part[:, None, None, None]
    diff_cols = diff_part[:, None, None, None]
    advanced_curl_rate = vorticity / (
        1.0 + diff_cols * harmonic_operator_spectrum * harmonic_operator_spectrum
    )
    advanced_spreading_rate = (
        spreading_rate_grid + harmonic_operator_spectrum * thermal_state_grid
    ) / (1.0 + layer_stack_count * harmonic_operator_spectrum)
    advanced_thermal_state = thermal_state_grid - layer_stack_count * advanced_spreading_rate
    piled_prognostics = jnp.stack(
        [advanced_curl_rate, advanced_spreading_rate, advanced_thermal_state], axis=1
    )
    return piled_prognostics.reshape(summed.shape).astype(jnp.bfloat16)


def general_body(
    prognostic_arrays, coriolis, weights, row_points, owner_pairs, legendre, depths, diffusion
):
    levels = prognostic_arrays.shape[0]
    row_count = prognostic_arrays.shape[2]
    lon_count = prognostic_arrays.shape[3]
    group_count = owner_pairs.shape[0]
    slot_count = owner_pairs.shape[1]
    local_basis = legendre[0]
    slot_total = local_basis.shape[1]
    highest = slot_total - 1
    channels = levels * 3
    packed = channels * 4 * slot_count
    wavenumbers = owner_waves(owner_pairs, highest).reshape(-1)
    valid = valid_points(row_points, lon_count)
    gridded = tendencies(prognostic_arrays, coriolis).reshape(channels, row_count, lon_count)
    gridded = jnp.where(valid[None], gridded, jnp.zeros((), gridded.dtype))
    phases = phase_table(row_points, wavenumbers, lon_count).reshape(
        row_count, lon_count, 2, group_count, 2, slot_count
    )
    row_scale = weights / row_points.astype(jnp.float32)
    fourier = jnp.einsum("crx,rxqght->grcqht", gridded, phases, preferred_element_type=jnp.float32)
    fourier = (fourier * row_scale[None, :, None, None, None, None]).astype(jnp.bfloat16)
    band_data = lax.all_to_all(
        fourier.reshape(group_count, row_count, packed),
        "lev",
        split_axis=0,
        concat_axis=0,
        tiled=True,
    )
    band_block = band_data.reshape(group_count * row_count, channels, 2, 2, slot_count)
    owner_index = lax.axis_index("lev")
    my_pairs = lax.dynamic_index_in_dim(owner_pairs, owner_index, 0, keepdims=False)
    first_half = half_mask(my_pairs, slot_total)
    half_masks = jnp.stack([first_half, jnp.logical_not(first_half)], axis=0)
    doubling = jnp.where(owner_waves(my_pairs[None], highest)[0] == 0, 1.0, 2.0).astype(jnp.float32)
    both_halves = jnp.einsum(
        "lkqht,tpl->kqhtp", band_block, local_basis, preferred_element_type=jnp.float32
    )
    summed = lax.psum(jnp.where(first_half, both_halves[:, :, 0], both_halves[:, :, 1]), "lat")
    solved = implicit(summed, my_pairs, depths, diffusion)
    masked_spec = jnp.where(half_masks[None, None], solved[:, :, None], jnp.zeros((), solved.dtype))
    inverted = jnp.einsum(
        "kqhtp,tpl->lkqht", masked_spec, local_basis, preferred_element_type=jnp.float32
    )
    inverted = (inverted * doubling[None, None, None]).astype(jnp.bfloat16)
    returned = lax.all_to_all(
        inverted.reshape(group_count, row_count, packed),
        "lev",
        split_axis=0,
        concat_axis=0,
        tiled=True,
    )
    returned = returned.reshape(group_count, row_count, channels, 2, 2, slot_count)
    outgrid = jnp.einsum("grcqht,rxqght->crx", returned, phases, preferred_element_type=jnp.float32)
    outgrid = jnp.where(valid[None], outgrid, jnp.zeros((), outgrid.dtype))
    return outgrid.reshape(levels, 3, row_count, lon_count)


lane_count = 128
piece_rows = 8


def turn_cos_sin(turns):
    scaled = turns * 4.0
    nearest = jnp.floor(scaled + 0.5)
    arc = (scaled - nearest) * (0.5 * math.pi)
    square = arc * arc
    sine = arc + arc * square * (
        -1.6666654611e-1 + square * (8.3321608736e-3 + square * -1.9515295891e-4)
    )
    cosine = (
        1.0
        - 0.5 * square
        + square
        * square
        * (4.166664568298827e-2 + square * (-1.388731625493765e-3 + square * 2.443315711809948e-5))
    )
    swapped = jnp.logical_or(nearest == 1.0, nearest == 3.0)
    cos_part = jnp.where(swapped, sine, cosine)
    sin_part = jnp.where(swapped, cosine, sine)
    cos_part = jnp.where(jnp.logical_or(nearest == 1.0, nearest == 2.0), -cos_part, cos_part)
    sin_part = jnp.where(jnp.logical_or(nearest == 2.0, nearest == 3.0), -sin_part, sin_part)
    return cos_part, sin_part


def turns_of(product, points, inverse):
    rest = product - jnp.floor(product * inverse) * points
    rest = jnp.where(rest < 0.0, rest + points, rest)
    rest = jnp.where(rest >= points, rest - points, rest)
    return rest * inverse


def wave_row(dims, pairs):
    levels, lon_count, group_count, slot_count, parts, per_part, highest = dims
    sources = parts * group_count
    tile = (piece_rows, lane_count)
    row = lax.broadcasted_iota(jnp.int32, tile, 0)
    lane = lax.broadcasted_iota(jnp.int32, tile, 1)
    lane_part = (lane >> (group_count.bit_length() - 1)) & (parts - 1)
    lane_slot = lane_part * per_part + ((lane >> (sources.bit_length() - 1)) & (per_part - 1))
    at_group = (lane & (group_count - 1)) == row
    spread = jnp.zeros(tile, jnp.float32)
    for slot in range(slot_count):
        chosen = jnp.logical_and(at_group, lane_slot == slot)
        spread = jnp.where(chosen, pairs[:, slot : slot + 1].astype(jnp.float32), spread)
    pair = jnp.sum(spread, axis=0, keepdims=True)
    lane_row = lax.broadcasted_iota(jnp.int32, (1, lane_count), 1)
    return jnp.where(lane_row >= per_part * sources, float(highest - 1) - pair, pair)


def factors(count, step, wave, points_row):
    place = lax.broadcasted_iota(jnp.int32, (count, lane_count), 0) * step
    cosine, sine = turn_cos_sin(
        turns_of(place.astype(jnp.float32) * wave, points_row, 1.0 / points_row)
    )
    return cosine, -sine


def fill_factors(wave, points_row, near_ref, far_ref, step_ref):
    span = near_ref.shape[0]
    base_real, base_imag = factors(piece_rows, 1, wave, points_row)
    step_real, step_imag = factors(span // piece_rows, piece_rows, wave, points_row)
    step_ref[:, :lane_count] = step_real
    step_ref[:, lane_count:] = step_imag
    for at in range(0, span // piece_rows, 2):
        rows = []
        for index in (at, at + 1):
            real = step_ref[index : index + 1, :lane_count]
            imag = step_ref[index : index + 1, lane_count:]
            rows.append(
                jnp.concatenate(
                    [base_real * real - base_imag * imag, base_real * imag + base_imag * real],
                    axis=1,
                )
            )
        near_ref[at * piece_rows : (at + 2) * piece_rows, :] = jnp.concatenate(
            rows, axis=0
        ).astype(jnp.bfloat16)
    far_real, far_imag = factors(far_ref.shape[0], span, wave, points_row)
    far_ref[:, :lane_count] = far_real
    far_ref[:, lane_count:] = far_imag


def analysis_kernel(
    dims,
    grid_hbm,
    coriolis_ref,
    weights_ref,
    points_ref,
    pairs_hbm,
    legendre_hbm,
    sent_ref,
    grid_ref,
    pairs_ref,
    legendre_ref,
    near_ref,
    far_ref,
    step_ref,
    rhs_ref,
    wave_ref,
    sems,
):
    levels, lon_count, group_count, slot_count, parts, per_part, highest = dims
    channels = 3 * levels
    blocks = lon_count // lane_count
    active = slot_count // per_part
    sources = parts * group_count
    level_rows = 3 * blocks
    chunks = levels // piece_rows
    chunk_rows = piece_rows * level_rows
    copies = [pltpu.make_async_copy(pairs_hbm, pairs_ref, sems.at[0])]
    for chunk in range(chunks):
        rows = pl.ds(chunk * chunk_rows, chunk_rows)
        copies.append(
            pltpu.make_async_copy(grid_hbm.at[rows], grid_ref.at[rows], sems.at[1 + chunk])
        )
    copies.append(pltpu.make_async_copy(legendre_hbm, legendre_ref, sems.at[1 + chunks]))
    for copy in copies:
        copy.start()
    copies[0].wait()

    points = points_ref[0]
    points_row = jnp.full((1, lane_count), points, jnp.int32).astype(jnp.float32)
    wave = wave_row(dims, pairs_ref[...])
    fill_factors(wave, points_row, near_ref, far_ref, step_ref)
    tiles = near_ref.shape[0] // lane_count
    rotation = coriolis_ref[0]
    half_rotation = stepsize_delta * rotation
    lane = lax.broadcasted_iota(jnp.int32, (piece_rows, lane_count), 1)
    lane_wide = lax.broadcasted_iota(jnp.int32, (levels, lane_count), 1)
    for chunk in range(chunks):
        copies[1 + chunk].wait()
    for block in range(blocks):
        vorticity, spreading, thermal = (
            grid_ref[pl.ds(field * blocks + block, levels, stride=level_rows), :]
            for field in range(3)
        )
        inside = lane_wide < points - block * lane_count
        stepped = stepsize_delta * spreading
        advanced = (
            vorticity - (rotation + vorticity) * stepped,
            spreading + (half_rotation * vorticity - spreading * stepped),
            thermal - thermal * stepped,
        )
        lanes = slice(block % tiles * lane_count, (block % tiles + 1) * lane_count)
        for field in range(3):
            at = block // tiles * channels + field * levels
            rhs_ref[at : at + levels, lanes] = jnp.where(inside, advanced[field], 0.0).astype(
                jnp.bfloat16
            )
    partial = jnp.dot(rhs_ref[...], near_ref[...], preferred_element_type=jnp.float32)
    real, imag = None, None
    for block in range(blocks // tiles):
        part_real = partial[block * channels : (block + 1) * channels, :lane_count]
        part_imag = partial[block * channels : (block + 1) * channels, lane_count:]
        far_real = far_ref[block : block + 1, :lane_count]
        far_imag = far_ref[block : block + 1, lane_count:]
        add_real = part_real * far_real - part_imag * far_imag
        add_imag = part_real * far_imag + part_imag * far_real
        real = add_real if block == 0 else real + add_real
        imag = add_imag if block == 0 else imag + add_imag
    scale = jnp.full((1, lane_count), weights_ref[0], jnp.float32) / points_row
    half_rows = 2 * per_part
    rest = jnp.zeros((lane_count - channels, lane_count), jnp.float32)
    for phase, value in enumerate((real, imag)):
        turned = jnp.concatenate([value * scale, rest], axis=0).T
        for at in range(half_rows):
            wave_ref[pl.ds(phase * half_rows + at, sources, stride=piece_rows), :] = turned[
                at * sources : (at + 1) * sources
            ]

    copies[1 + chunks].wait()
    slot_total = highest + 1
    left = lane_count - channels
    for part in range(active):
        first, second = (
            jnp.pad(
                legendre_ref[0, part * per_part + index].astype(jnp.float32),
                ((0, 0), (0, lane_count - slot_total)),
            )
            for index in range(2)
        )
        upper_basis = pltpu.roll(first, channels, 1)
        lower = jnp.where(
            lane < slot_total, second, pltpu.roll(first, (slot_total - left) % lane_count, 1)
        )
        for group in range(group_count):
            at = part * group_count + group
            upper = jnp.where(
                lane < channels,
                wave_ref[at * piece_rows : (at + 1) * piece_rows, :],
                upper_basis,
            )
            sent_ref[at] = jnp.concatenate([upper, lower], axis=0).astype(jnp.bfloat16)
    for at in range(active * group_count, sources):
        sent_ref[at] = jnp.zeros((2 * piece_rows, lane_count), jnp.bfloat16)


def prepare_kernel(
    dims,
    part_ref,
    group_ref,
    points_ref,
    table_ref,
    pairs_ref,
    depths_ref,
    diffusion_ref,
    near_ref,
    far_ref,
    solve_ref,
    rows_ref,
    step_ref,
):
    levels, lon_count, group_count, slot_count, parts, per_part, highest = dims
    points_row = jnp.full((1, lane_count), points_ref[0], jnp.int32).astype(jnp.float32)
    wave = wave_row(dims, table_ref[...])
    fill_factors(wave, points_row, near_ref, far_ref, step_ref)

    part, group = part_ref[0], group_ref[0]
    lane_row = lax.broadcasted_iota(jnp.int32, (1, lane_count), 1)
    depth_row = jnp.zeros((1, lane_count), jnp.float32)
    damp_row = jnp.zeros((1, lane_count), jnp.float32)
    for level in range(levels):
        depth_row = jnp.where(lane_row % levels == level, depths_ref[level], depth_row)
        damp_row = jnp.where(lane_row == level, diffusion_ref[level], damp_row)
    is_first = lane_row < levels
    coeff_row = jnp.where(is_first, damp_row, depth_row)
    rows_ref[0:1, :] = depth_row
    position = lax.broadcasted_iota(jnp.int32, (solve_ref.shape[1], lane_count), 0)
    for index in range(per_part):
        pair = pairs_ref[group, jnp.minimum(part * per_part + index, slot_count - 1)]
        lower_half = position < highest - pair
        total = jnp.where(lower_half, pair + position, position - 1).astype(jnp.float32)
        operator = total * (total + 1.0) / float(highest * highest)
        factor = jnp.where(is_first, operator * operator, operator)
        solve_ref[3 * index] = 1.0 / (1.0 + coeff_row * factor)
        solve_ref[3 * index + 1] = jnp.where(is_first, 0.0, operator)
        solve_ref[3 * index + 2] = jnp.where(lower_half, 1.0, 0.0)
        for half in range(2):
            wavenumber = pair if half == 0 else highest - 1 - pair
            at = 1 + half * per_part + index
            rows_ref[at : at + 1, :] = jnp.full(
                (1, lane_count), jnp.where(wavenumber == 0, 1.0, 2.0), jnp.float32
            )


def spectral_kernel(dims, received_ref, group_ref, solve_ref, rows_ref, sent_ref, wave_ref):
    levels, lon_count, group_count, slot_count, parts, per_part, highest = dims
    channels = 3 * levels
    slot_total = highest + 1
    left = lane_count - channels
    sources = parts * group_count
    group = group_ref[0]
    lane = lax.broadcasted_iota(jnp.int32, (piece_rows, lane_count), 1)
    for source in range(sources):
        wave_ref[source * piece_rows : (source + 1) * piece_rows, :] = received_ref[
            source, :piece_rows, :
        ].astype(jnp.float32)
    first, second = [], []
    for band in range(parts):
        piece = received_ref[band * group_count + group].astype(jnp.float32)
        upper, lower = piece[:piece_rows], piece[piece_rows:]
        start = pltpu.roll(upper, left, 1)
        rest = pltpu.roll(lower, (lane_count - (slot_total - left)) % lane_count, 1)
        first.append(jnp.where(lane < left, start, jnp.where(lane < slot_total, rest, 0.0)))
        second.append(jnp.where(lane < slot_total, lower, 0.0))
    bases = [jnp.concatenate(first, axis=0), jnp.concatenate(second, axis=0)]
    lane_row = lax.broadcasted_iota(jnp.int32, (1, lane_count), 1)
    is_last = lane_row >= 2 * levels
    depth_row = rows_ref[0:1, :]
    held = solve_ref.shape[1]
    for index in range(per_part):
        basis = bases[index].astype(jnp.bfloat16)[:, :held]
        basis_turned = bases[index].T[:held].astype(jnp.bfloat16)
        specs = []
        for half in range(2):
            waves = jnp.concatenate(
                [
                    wave_ref[
                        pl.ds((phase * 2 + half) * per_part + index, sources, stride=piece_rows), :
                    ]
                    for phase in range(2)
                ],
                axis=1,
            ).astype(jnp.bfloat16)
            specs.append(jnp.dot(basis_turned, waves, preferred_element_type=jnp.float32))
        lower_half = solve_ref[3 * index + 2] > 0.5
        solved = []
        for phase in range(2):
            lanes = slice(phase * lane_count, (phase + 1) * lane_count)
            spec = jnp.where(lower_half, specs[0][:, lanes], specs[1][:, lanes])
            thermal = pltpu.roll(spec, lane_count - levels, 1)
            quotient = (spec + solve_ref[3 * index + 1] * thermal) * solve_ref[3 * index]
            moved = pltpu.roll(quotient, levels, 1)
            solved.append(jnp.where(is_last, spec - depth_row * moved, quotient))
        for half in range(2):
            kept = jnp.concatenate(
                [
                    jnp.where(lower_half, value, 0.0)
                    if half == 0
                    else jnp.where(lower_half, 0.0, value)
                    for value in solved
                ],
                axis=1,
            ).astype(jnp.bfloat16)
            back = jnp.dot(basis, kept, preferred_element_type=jnp.float32)
            row = 1 + half * per_part + index
            doubling = rows_ref[row : row + 1, :]
            for phase in range(2):
                at = (phase * 2 + half) * per_part + index
                wave_ref[pl.ds(at, sources, stride=piece_rows), :] = (
                    back[:, phase * lane_count : (phase + 1) * lane_count] * doubling
                )
    for source in range(sources):
        sent_ref[source] = wave_ref[
            source * piece_rows : (source + 1) * piece_rows, :
        ].astype(jnp.bfloat16)


def synthesis_kernel(
    dims,
    received_ref,
    near_ref,
    far_ref,
    points_ref,
    out_hbm,
    wave_ref,
    rotated_ref,
    out_ref,
    sems,
):
    levels, lon_count, group_count, slot_count, parts, per_part, highest = dims
    channels = 3 * levels
    blocks = lon_count // lane_count
    sources = parts * group_count
    half_rows = 2 * per_part
    level_rows = 3 * blocks
    chunks = levels // piece_rows
    chunk_rows = piece_rows * level_rows
    for source in range(sources):
        wave_ref[source * piece_rows : (source + 1) * piece_rows, :] = received_ref[source].astype(
            jnp.float32
        )
    real, imag = (
        jnp.concatenate(
            [
                wave_ref[pl.ds(phase * half_rows + at, sources, stride=piece_rows), :]
                for at in range(half_rows)
            ],
            axis=0,
        ).T
        for phase in range(2)
    )
    real, imag = real[:channels], imag[:channels]
    tiles = near_ref.shape[0] // lane_count
    for block in range(blocks // tiles):
        far_real = far_ref[block : block + 1, :lane_count]
        far_imag = far_ref[block : block + 1, lane_count:]
        rotated_ref[block * channels : (block + 1) * channels, :] = jnp.concatenate(
            [real * far_real + imag * far_imag, imag * far_real - real * far_imag], axis=1
        ).astype(jnp.bfloat16)
    result = lax.dot_general(
        rotated_ref[...],
        near_ref[...],
        (((1,), (1,)), ((), ())),
        preferred_element_type=jnp.float32,
    )
    points = points_ref[0]
    lane_wide = lax.broadcasted_iota(jnp.int32, (levels, lane_count), 1)
    for block in range(blocks):
        inside = lane_wide < points - block * lane_count
        lanes = slice(block % tiles * lane_count, (block % tiles + 1) * lane_count)
        for field in range(3):
            at = block // tiles * channels + field * levels
            out_ref[pl.ds(field * blocks + block, levels, stride=level_rows), :] = jnp.where(
                inside, result[at : at + levels, lanes], 0.0
            )
    copies = []
    for chunk in range(chunks):
        rows = pl.ds(chunk * chunk_rows, chunk_rows)
        copies.append(pltpu.make_async_copy(out_ref.at[rows], out_hbm.at[rows], sems.at[chunk]))
        copies[-1].start()
    for copy in copies:
        copy.wait()


def packed_body(
    dims,
    prognostic_arrays,
    coriolis,
    weights,
    row_points,
    owner_pairs,
    legendre,
    depths,
    diffusion,
):
    levels, lon_count, group_count, slot_count, parts, per_part, highest = dims
    channels = 3 * levels
    blocks = lon_count // lane_count
    sources = parts * group_count
    tiles = max(count for count in (1, 2, 3) if blocks % count == 0)
    span = tiles * lane_count
    far_rows = -(-(blocks // tiles) // piece_rows) * piece_rows
    chunks = levels // piece_rows
    slot_rows = -(-(highest + 1) // 16) * 16
    steps = pltpu.VMEM((span // piece_rows, 2 * lane_count), jnp.float32)
    in_vmem = pl.BlockSpec(memory_space=pltpu.VMEM)
    in_smem = pl.BlockSpec(memory_space=pltpu.SMEM)
    in_hbm = pl.BlockSpec(memory_space=pltpu.HBM)
    params = pltpu.CompilerParams(vmem_limit_bytes=16 << 20)
    grid = prognostic_arrays.reshape(channels * blocks, lane_count)
    basis = jnp.swapaxes(legendre, 2, 3)
    part = lax.axis_index("lat").astype(jnp.int32).reshape(1)
    group = lax.axis_index("lev").astype(jnp.int32).reshape(1)
    sent = pl.pallas_call(
        functools.partial(analysis_kernel, dims),
        name="analysis",
        out_shape=jax.ShapeDtypeStruct((sources, 2 * piece_rows, lane_count), jnp.bfloat16),
        in_specs=[in_hbm, in_smem, in_smem, in_smem, in_hbm, in_hbm],
        out_specs=in_vmem,
        scratch_shapes=[
            pltpu.VMEM(grid.shape, jnp.float32),
            pltpu.VMEM(owner_pairs.shape, jnp.int32),
            pltpu.VMEM(basis.shape, jnp.bfloat16),
            pltpu.VMEM((span, 2 * lane_count), jnp.bfloat16),
            pltpu.VMEM((far_rows, 2 * lane_count), jnp.float32),
            steps,
            pltpu.VMEM((blocks // tiles * channels, span), jnp.bfloat16),
            pltpu.VMEM((sources * piece_rows, lane_count), jnp.float32),
            pltpu.SemaphoreType.DMA((2 + chunks,)),
        ],
        compiler_params=pltpu.CompilerParams(vmem_limit_bytes=67043328),
    )(grid, coriolis, weights, row_points, owner_pairs, basis)
    received = lax.all_to_all(sent, ("lat", "lev"), split_axis=0, concat_axis=0, tiled=True)
    near, far, solve, rows = pl.pallas_call(
        functools.partial(prepare_kernel, dims),
        name="prepare",
        out_shape=(
            jax.ShapeDtypeStruct((span, 2 * lane_count), jnp.bfloat16),
            jax.ShapeDtypeStruct((far_rows, 2 * lane_count), jnp.float32),
            jax.ShapeDtypeStruct((3 * per_part, slot_rows, lane_count), jnp.float32),
            jax.ShapeDtypeStruct((piece_rows, lane_count), jnp.float32),
        ),
        in_specs=[in_smem, in_smem, in_smem, in_vmem, in_smem, in_smem, in_smem],
        out_specs=(in_vmem,) * 4,
        scratch_shapes=[steps],
        compiler_params=params,
        cost_estimate=pl.CostEstimate(
            flops=40 * lane_count * lane_count, bytes_accessed=1 << 19, transcendentals=0
        ),
    )(part, group, row_points, owner_pairs, owner_pairs, depths, diffusion)
    solved = pl.pallas_call(
        functools.partial(spectral_kernel, dims),
        name="spectral",
        out_shape=jax.ShapeDtypeStruct((sources, piece_rows, lane_count), jnp.bfloat16),
        in_specs=[in_vmem, in_smem, in_vmem, in_vmem],
        out_specs=in_vmem,
        scratch_shapes=[pltpu.VMEM((sources * piece_rows, lane_count), jnp.float32)],
        compiler_params=params,
    )(received, group, solve, rows)
    returned = lax.all_to_all(solved, ("lat", "lev"), split_axis=0, concat_axis=0, tiled=True)
    updated = pl.pallas_call(
        functools.partial(synthesis_kernel, dims),
        name="synthesis",
        out_shape=jax.ShapeDtypeStruct((channels * blocks, lane_count), jnp.float32),
        in_specs=[in_vmem, in_vmem, in_vmem, in_smem],
        out_specs=in_hbm,
        scratch_shapes=[
            pltpu.VMEM((sources * piece_rows, lane_count), jnp.float32),
            pltpu.VMEM((blocks // tiles * channels, 2 * lane_count), jnp.bfloat16),
            pltpu.VMEM((channels * blocks, lane_count), jnp.float32),
            pltpu.SemaphoreType.DMA((chunks,)),
        ],
        compiler_params=params,
    )(returned, near, far, row_points)
    return updated.reshape(prognostic_arrays.shape)


def body(prognostic_arrays, coriolis, weights, row_points, owner_pairs, legendre, depths, diffusion):
    levels, _, row_count, lon_count = prognostic_arrays.shape
    group_count, slot_count = owner_pairs.shape
    slot_total, band_rows = legendre.shape[2:]
    parts = lax.axis_size("lat")
    per_part = -(-slot_count // parts)
    channels = 3 * levels
    fits = (
        row_count == 1
        and band_rows == piece_rows == group_count
        and 4 * per_part == piece_rows
        and slot_count % per_part == 0
        and lon_count % lane_count == 0
        and 2 * per_part * parts * group_count == lane_count
        and levels % 16 == 0
        and channels < slot_total <= lane_count
        and 2 * slot_total + channels <= 2 * lane_count
        and lon_count * slot_total < 2**24
    )
    arguments = (
        prognostic_arrays, coriolis, weights, row_points, owner_pairs, legendre, depths, diffusion
    )
    if not fits:
        return general_body(*arguments)
    dims = (levels, lon_count, group_count, slot_count, parts, per_part, slot_total - 1)
    return packed_body(dims, *arguments)


def solution(mesh):
    in_specs = (
        P(None, None, ("lat", "lev"), None),
        P(("lat", "lev")),
        P(("lat", "lev")),
        P(("lat", "lev")),
        P(),
        P("lev", None, None, "lat"),
        P(),
        P(),
    )
    out_specs = P(None, None, ("lat", "lev"), None)
    return jax.shard_map(body, mesh=mesh, in_specs=in_specs, out_specs=out_specs, check_vma=False)
```

```python
import functools
import math

import jax
import jax.numpy as jnp
from jax import lax
from jax.experimental import pallas as pl
from jax.experimental.pallas import tpu as pltpu
from jax.sharding import PartitionSpec as P

stepsize_delta = 0.5


def tendencies(prognostic_arrays, coriolis):
    vorticity = prognostic_arrays[:, 0]
    spreading_rate_grid = prognostic_arrays[:, 1]
    thermal_state_grid = prognostic_arrays[:, 2]
    rotation = coriolis[None, :, None]
    advanced_curl_rate = vorticity - stepsize_delta * (rotation + vorticity) * spreading_rate_grid
    advanced_spreading_rate = spreading_rate_grid + stepsize_delta * (
        rotation * vorticity - spreading_rate_grid * spreading_rate_grid
    )
    advanced_thermal_state = (
        thermal_state_grid - stepsize_delta * thermal_state_grid * spreading_rate_grid
    )
    return jnp.stack(
        [advanced_curl_rate, advanced_spreading_rate, advanced_thermal_state], axis=1
    ).astype(jnp.bfloat16)


def owner_waves(owner_pairs, highest):
    return jnp.stack([owner_pairs, highest - 1 - owner_pairs], axis=1)


def phase_table(points, wavenumbers, lon_count):
    positions = jnp.arange(lon_count, dtype=jnp.int32)
    product = positions[None, :, None] * wavenumbers[None, None, :] % points[:, None, None]
    angle = (
        product.astype(jnp.float32) * (2.0 * math.pi / points.astype(jnp.float32))[:, None, None]
    )
    return jnp.stack([jnp.cos(angle), -jnp.sin(angle)], axis=2).astype(jnp.bfloat16)


def valid_points(points, lon_count):
    positions = jnp.arange(lon_count, dtype=jnp.int32)
    return positions[None, :] < points[:, None]


def half_mask(my_pairs, slot_total):
    positions = jnp.arange(slot_total, dtype=jnp.int32)
    return positions[None, :] < (slot_total - 1 - my_pairs)[:, None]


def implicit(summed, my_pairs, depth_part, diff_part):
    slot_total = summed.shape[3]
    slot_count = summed.shape[2]
    highest = slot_total - 1
    positions = jnp.arange(slot_total, dtype=jnp.int32)[None, :]
    first_half = positions < (highest - my_pairs)[:, None]
    total = jnp.where(first_half, my_pairs[:, None] + positions, positions - 1).astype(jnp.float32)
    harmonic_operator_spectrum = total * (total + 1.0) / float(highest * highest)
    bundled_prognostics = summed.reshape(-1, 3, 2, slot_count, slot_total)
    vorticity = bundled_prognostics[:, 0]
    spreading_rate_grid = bundled_prognostics[:, 1]
    thermal_state_grid = bundled_prognostics[:, 2]
    layer_stack_count = depth_part[:, None, None, None]
    diff_cols = diff_part[:, None, None, None]
    advanced_curl_rate = vorticity / (
        1.0 + diff_cols * harmonic_operator_spectrum * harmonic_operator_spectrum
    )
    advanced_spreading_rate = (
        spreading_rate_grid + harmonic_operator_spectrum * thermal_state_grid
    ) / (1.0 + layer_stack_count * harmonic_operator_spectrum)
    advanced_thermal_state = thermal_state_grid - layer_stack_count * advanced_spreading_rate
    piled_prognostics = jnp.stack(
        [advanced_curl_rate, advanced_spreading_rate, advanced_thermal_state], axis=1
    )
    return piled_prognostics.reshape(summed.shape).astype(jnp.bfloat16)


def general_body(
    prognostic_arrays, coriolis, weights, row_points, owner_pairs, legendre, depths, diffusion
):
    levels = prognostic_arrays.shape[0]
    row_count = prognostic_arrays.shape[2]
    lon_count = prognostic_arrays.shape[3]
    group_count = owner_pairs.shape[0]
    slot_count = owner_pairs.shape[1]
    local_basis = legendre[0]
    slot_total = local_basis.shape[1]
    highest = slot_total - 1
    channels = levels * 3
    packed = channels * 4 * slot_count
    wavenumbers = owner_waves(owner_pairs, highest).reshape(-1)
    valid = valid_points(row_points, lon_count)
    gridded = tendencies(prognostic_arrays, coriolis).reshape(channels, row_count, lon_count)
    gridded = jnp.where(valid[None], gridded, jnp.zeros((), gridded.dtype))
    phases = phase_table(row_points, wavenumbers, lon_count).reshape(
        row_count, lon_count, 2, group_count, 2, slot_count
    )
    row_scale = weights / row_points.astype(jnp.float32)
    fourier = jnp.einsum("crx,rxqght->grcqht", gridded, phases, preferred_element_type=jnp.float32)
    fourier = (fourier * row_scale[None, :, None, None, None, None]).astype(jnp.bfloat16)
    band_data = lax.all_to_all(
        fourier.reshape(group_count, row_count, packed),
        "lev",
        split_axis=0,
        concat_axis=0,
        tiled=True,
    )
    band_block = band_data.reshape(group_count * row_count, channels, 2, 2, slot_count)
    owner_index = lax.axis_index("lev")
    my_pairs = lax.dynamic_index_in_dim(owner_pairs, owner_index, 0, keepdims=False)
    first_half = half_mask(my_pairs, slot_total)
    half_masks = jnp.stack([first_half, jnp.logical_not(first_half)], axis=0)
    doubling = jnp.where(owner_waves(my_pairs[None], highest)[0] == 0, 1.0, 2.0).astype(jnp.float32)
    both_halves = jnp.einsum(
        "lkqht,tpl->kqhtp", band_block, local_basis, preferred_element_type=jnp.float32
    )
    summed = lax.psum(jnp.where(first_half, both_halves[:, :, 0], both_halves[:, :, 1]), "lat")
    solved = implicit(summed, my_pairs, depths, diffusion)
    masked_spec = jnp.where(half_masks[None, None], solved[:, :, None], jnp.zeros((), solved.dtype))
    inverted = jnp.einsum(
        "kqhtp,tpl->lkqht", masked_spec, local_basis, preferred_element_type=jnp.float32
    )
    inverted = (inverted * doubling[None, None, None]).astype(jnp.bfloat16)
    returned = lax.all_to_all(
        inverted.reshape(group_count, row_count, packed),
        "lev",
        split_axis=0,
        concat_axis=0,
        tiled=True,
    )
    returned = returned.reshape(group_count, row_count, channels, 2, 2, slot_count)
    outgrid = jnp.einsum("grcqht,rxqght->crx", returned, phases, preferred_element_type=jnp.float32)
    outgrid = jnp.where(valid[None], outgrid, jnp.zeros((), outgrid.dtype))
    return outgrid.reshape(levels, 3, row_count, lon_count)


lane_count = 128
piece_rows = 8


def turn_cos_sin(turns):
    scaled = turns * 4.0
    nearest = jnp.floor(scaled + 0.5)
    arc = (scaled - nearest) * (0.5 * math.pi)
    square = arc * arc
    sine = arc + arc * square * (
        -1.6666654611e-1 + square * (8.3321608736e-3 + square * -1.9515295891e-4)
    )
    cosine = (
        1.0
        - 0.5 * square
        + square
        * square
        * (4.166664568298827e-2 + square * (-1.388731625493765e-3 + square * 2.443315711809948e-5))
    )
    swapped = jnp.logical_or(nearest == 1.0, nearest == 3.0)
    cos_part = jnp.where(swapped, sine, cosine)
    sin_part = jnp.where(swapped, cosine, sine)
    cos_part = jnp.where(jnp.logical_or(nearest == 1.0, nearest == 2.0), -cos_part, cos_part)
    sin_part = jnp.where(jnp.logical_or(nearest == 2.0, nearest == 3.0), -sin_part, sin_part)
    return cos_part, sin_part


def turns_of(product, points, inverse):
    rest = product - jnp.floor(product * inverse) * points
    rest = jnp.where(rest < 0.0, rest + points, rest)
    rest = jnp.where(rest >= points, rest - points, rest)
    return rest * inverse


def wave_row(dims, pairs):
    levels, lon_count, group_count, slot_count, parts, per_part, highest = dims
    sources = parts * group_count
    tile = (piece_rows, lane_count)
    row = lax.broadcasted_iota(jnp.int32, tile, 0)
    lane = lax.broadcasted_iota(jnp.int32, tile, 1)
    lane_part = (lane >> (group_count.bit_length() - 1)) & (parts - 1)
    lane_slot = lane_part * per_part + ((lane >> (sources.bit_length() - 1)) & (per_part - 1))
    at_group = (lane & (group_count - 1)) == row
    spread = jnp.zeros(tile, jnp.float32)
    for slot in range(slot_count):
        chosen = jnp.logical_and(at_group, lane_slot == slot)
        spread = jnp.where(chosen, pairs[:, slot : slot + 1].astype(jnp.float32), spread)
    pair = jnp.sum(spread, axis=0, keepdims=True)
    lane_row = lax.broadcasted_iota(jnp.int32, (1, lane_count), 1)
    return jnp.where(lane_row >= per_part * sources, float(highest - 1) - pair, pair)


def factors(count, step, wave, points_row):
    place = lax.broadcasted_iota(jnp.int32, (count, lane_count), 0) * step
    cosine, sine = turn_cos_sin(
        turns_of(place.astype(jnp.float32) * wave, points_row, 1.0 / points_row)
    )
    return cosine, -sine


def fill_factors(wave, points_row, near_ref, far_ref, step_ref):
    span = near_ref.shape[0]
    base_real, base_imag = factors(piece_rows, 1, wave, points_row)
    step_real, step_imag = factors(span // piece_rows, piece_rows, wave, points_row)
    step_ref[:, :lane_count] = step_real
    step_ref[:, lane_count:] = step_imag
    for at in range(0, span // piece_rows, 2):
        rows = []
        for index in (at, at + 1):
            real = step_ref[index : index + 1, :lane_count]
            imag = step_ref[index : index + 1, lane_count:]
            rows.append(
                jnp.concatenate(
                    [base_real * real - base_imag * imag, base_real * imag + base_imag * real],
                    axis=1,
                )
            )
        near_ref[at * piece_rows : (at + 2) * piece_rows, :] = jnp.concatenate(
            rows, axis=0
        ).astype(jnp.bfloat16)
    far_real, far_imag = factors(far_ref.shape[0], span, wave, points_row)
    far_ref[:, :lane_count] = far_real
    far_ref[:, lane_count:] = far_imag


def fill_solve(dims, part, group, pairs, depths, diffusion, solve_ref, rows_ref):
    levels, lon_count, group_count, slot_count, parts, per_part, highest = dims
    lane_row = lax.broadcasted_iota(jnp.int32, (1, lane_count), 1)
    wide = jnp.pad(depths, ((0, 0), (0, lane_count - levels)))
    is_first = lane_row < levels
    depth_row = pltpu.roll(wide, levels, 1) + pltpu.roll(wide, 2 * levels, 1)
    coeff_row = depth_row + jnp.pad(diffusion, ((0, 0), (0, lane_count - levels)))
    rows_ref[0:1, :] = depth_row
    row = lax.broadcasted_iota(jnp.int32, pairs.shape, 0)
    column = lax.broadcasted_iota(jnp.int32, pairs.shape, 1)
    position = lax.broadcasted_iota(jnp.int32, (solve_ref.shape[1], lane_count), 0).astype(
        jnp.float32
    )
    for index in range(per_part):
        slot = jnp.minimum(part * per_part + index, slot_count - 1)
        chosen = jnp.logical_and(row == group, column == slot)
        pair = jnp.sum(jnp.where(chosen, pairs.astype(jnp.float32), 0.0), axis=0, keepdims=True)
        pair = jnp.broadcast_to(jnp.sum(pair, axis=1, keepdims=True), (1, lane_count))
        lower_half = position < float(highest) - pair
        total = jnp.where(lower_half, pair + position, position - 1.0)
        operator = total * (total + 1.0) / float(highest * highest)
        factor = jnp.where(is_first, operator * operator, operator)
        solve_ref[3 * index] = 1.0 / (1.0 + coeff_row * factor)
        solve_ref[3 * index + 1] = jnp.where(is_first, 0.0, operator)
        solve_ref[3 * index + 2] = jnp.where(lower_half, 1.0, 0.0)
        for half in range(2):
            wavenumber = pair if half == 0 else float(highest - 1) - pair
            at = 1 + half * per_part + index
            rows_ref[at : at + 1, :] = jnp.where(wavenumber == 0.0, 1.0, 2.0)


def analysis_kernel(
    dims,
    grid_hbm,
    coriolis_ref,
    weights_ref,
    points_ref,
    part_ref,
    group_ref,
    pairs_hbm,
    legendre_hbm,
    depths_hbm,
    diffusion_hbm,
    sent_ref,
    near_ref,
    far_ref,
    solve_ref,
    rows_ref,
    grid_ref,
    pairs_ref,
    legendre_ref,
    depths_ref,
    diffusion_ref,
    step_ref,
    rhs_ref,
    wave_ref,
    sems,
):
    levels, lon_count, group_count, slot_count, parts, per_part, highest = dims
    channels = 3 * levels
    blocks = lon_count // lane_count
    active = slot_count // per_part
    sources = parts * group_count
    level_rows = 3 * blocks
    chunks = levels // piece_rows
    chunk_rows = piece_rows * level_rows
    copies = [pltpu.make_async_copy(pairs_hbm, pairs_ref, sems.at[0])]
    small = (
        pltpu.make_async_copy(depths_hbm, depths_ref, sems.at[2 + chunks]),
        pltpu.make_async_copy(diffusion_hbm, diffusion_ref, sems.at[3 + chunks]),
    )
    for chunk in range(chunks):
        rows = pl.ds(chunk * chunk_rows, chunk_rows)
        copies.append(
            pltpu.make_async_copy(grid_hbm.at[rows], grid_ref.at[rows], sems.at[1 + chunk])
        )
    copies.append(pltpu.make_async_copy(legendre_hbm, legendre_ref, sems.at[1 + chunks]))
    copies[0].start()
    for copy in small:
        copy.start()
    for copy in copies[1:]:
        copy.start()
    copies[0].wait()

    points = points_ref[0]
    points_row = jnp.full((1, lane_count), points, jnp.int32).astype(jnp.float32)
    wave = wave_row(dims, pairs_ref[...])
    fill_factors(wave, points_row, near_ref, far_ref, step_ref)
    for copy in small:
        copy.wait()
    fill_solve(
        dims,
        part_ref[0],
        group_ref[0],
        pairs_ref[...],
        depths_ref[...],
        diffusion_ref[...],
        solve_ref,
        rows_ref,
    )
    tiles = near_ref.shape[0] // lane_count
    rotation = coriolis_ref[0]
    half_rotation = stepsize_delta * rotation
    lane = lax.broadcasted_iota(jnp.int32, (piece_rows, lane_count), 1)
    lane_wide = lax.broadcasted_iota(jnp.int32, (levels, lane_count), 1)
    for chunk in range(chunks):
        copies[1 + chunk].wait()
    for block in range(blocks):
        vorticity, spreading, thermal = (
            grid_ref[pl.ds(field * blocks + block, levels, stride=level_rows), :]
            for field in range(3)
        )
        inside = lane_wide < points - block * lane_count
        stepped = stepsize_delta * spreading
        advanced = (
            vorticity - (rotation + vorticity) * stepped,
            spreading + (half_rotation * vorticity - spreading * stepped),
            thermal - thermal * stepped,
        )
        lanes = slice(block % tiles * lane_count, (block % tiles + 1) * lane_count)
        for field in range(3):
            at = block // tiles * channels + field * levels
            rhs_ref[at : at + levels, lanes] = jnp.where(inside, advanced[field], 0.0).astype(
                jnp.bfloat16
            )
    partial = jnp.dot(rhs_ref[...], near_ref[...], preferred_element_type=jnp.float32)
    real, imag = None, None
    for block in range(blocks // tiles):
        part_real = partial[block * channels : (block + 1) * channels, :lane_count]
        part_imag = partial[block * channels : (block + 1) * channels, lane_count:]
        far_real = far_ref[block : block + 1, :lane_count]
        far_imag = far_ref[block : block + 1, lane_count:]
        add_real = part_real * far_real - part_imag * far_imag
        add_imag = part_real * far_imag + part_imag * far_real
        real = add_real if block == 0 else real + add_real
        imag = add_imag if block == 0 else imag + add_imag
    scale = jnp.full((1, lane_count), weights_ref[0], jnp.float32) / points_row
    half_rows = 2 * per_part
    rest = jnp.zeros((lane_count - channels, lane_count), jnp.float32)
    for phase, value in enumerate((real, imag)):
        turned = jnp.concatenate([value * scale, rest], axis=0).T
        for at in range(half_rows):
            wave_ref[pl.ds(phase * half_rows + at, sources, stride=piece_rows), :] = turned[
                at * sources : (at + 1) * sources
            ]

    copies[1 + chunks].wait()
    slot_total = highest + 1
    left = lane_count - channels
    for part in range(active):
        first, second = (
            jnp.pad(
                legendre_ref[0, part * per_part + index].astype(jnp.float32),
                ((0, 0), (0, lane_count - slot_total)),
            )
            for index in range(2)
        )
        upper_basis = pltpu.roll(first, channels, 1)
        lower = jnp.where(
            lane < slot_total, second, pltpu.roll(first, (slot_total - left) % lane_count, 1)
        )
        for group in range(group_count):
            at = part * group_count + group
            upper = jnp.where(
                lane < channels,
                wave_ref[at * piece_rows : (at + 1) * piece_rows, :],
                upper_basis,
            )
            sent_ref[at] = jnp.concatenate([upper, lower], axis=0).astype(jnp.bfloat16)
    for at in range(active * group_count, sources):
        sent_ref[at] = jnp.zeros((2 * piece_rows, lane_count), jnp.bfloat16)


def spectral_kernel(dims, received_ref, group_ref, solve_ref, rows_ref, sent_ref, wave_ref):
    levels, lon_count, group_count, slot_count, parts, per_part, highest = dims
    channels = 3 * levels
    slot_total = highest + 1
    left = lane_count - channels
    sources = parts * group_count
    group = group_ref[0]
    lane = lax.broadcasted_iota(jnp.int32, (piece_rows, lane_count), 1)
    for source in range(sources):
        wave_ref[source * piece_rows : (source + 1) * piece_rows, :] = received_ref[
            source, :piece_rows, :
        ].astype(jnp.float32)
    first, second = [], []
    for band in range(parts):
        piece = received_ref[band * group_count + group].astype(jnp.float32)
        upper, lower = piece[:piece_rows], piece[piece_rows:]
        start = pltpu.roll(upper, left, 1)
        rest = pltpu.roll(lower, (lane_count - (slot_total - left)) % lane_count, 1)
        first.append(jnp.where(lane < left, start, jnp.where(lane < slot_total, rest, 0.0)))
        second.append(jnp.where(lane < slot_total, lower, 0.0))
    bases = [jnp.concatenate(first, axis=0), jnp.concatenate(second, axis=0)]
    lane_row = lax.broadcasted_iota(jnp.int32, (1, lane_count), 1)
    is_last = lane_row >= 2 * levels
    depth_row = rows_ref[0:1, :]
    held = solve_ref.shape[1]
    for index in range(per_part):
        basis = bases[index].astype(jnp.bfloat16)[:, :held]
        basis_turned = bases[index].T[:held].astype(jnp.bfloat16)
        specs = []
        for half in range(2):
            waves = jnp.concatenate(
                [
                    wave_ref[
                        pl.ds((phase * 2 + half) * per_part + index, sources, stride=piece_rows), :
                    ]
                    for phase in range(2)
                ],
                axis=1,
            ).astype(jnp.bfloat16)
            specs.append(jnp.dot(basis_turned, waves, preferred_element_type=jnp.float32))
        lower_half = solve_ref[3 * index + 2] > 0.5
        solved = []
        for phase in range(2):
            lanes = slice(phase * lane_count, (phase + 1) * lane_count)
            spec = jnp.where(lower_half, specs[0][:, lanes], specs[1][:, lanes])
            thermal = pltpu.roll(spec, lane_count - levels, 1)
            quotient = (spec + solve_ref[3 * index + 1] * thermal) * solve_ref[3 * index]
            moved = pltpu.roll(quotient, levels, 1)
            solved.append(jnp.where(is_last, spec - depth_row * moved, quotient))
        for half in range(2):
            kept = jnp.concatenate(
                [
                    jnp.where(lower_half, value, 0.0)
                    if half == 0
                    else jnp.where(lower_half, 0.0, value)
                    for value in solved
                ],
                axis=1,
            ).astype(jnp.bfloat16)
            back = jnp.dot(basis, kept, preferred_element_type=jnp.float32)
            row = 1 + half * per_part + index
            doubling = rows_ref[row : row + 1, :]
            for phase in range(2):
                at = (phase * 2 + half) * per_part + index
                wave_ref[pl.ds(at, sources, stride=piece_rows), :] = (
                    back[:, phase * lane_count : (phase + 1) * lane_count] * doubling
                )
    for source in range(sources):
        sent_ref[source] = wave_ref[
            source * piece_rows : (source + 1) * piece_rows, :
        ].astype(jnp.bfloat16)


def synthesis_kernel(
    dims,
    received_ref,
    near_ref,
    far_ref,
    points_ref,
    out_hbm,
    wave_ref,
    rotated_ref,
    out_ref,
    sems,
):
    levels, lon_count, group_count, slot_count, parts, per_part, highest = dims
    channels = 3 * levels
    blocks = lon_count // lane_count
    sources = parts * group_count
    half_rows = 2 * per_part
    level_rows = 3 * blocks
    chunks = levels // piece_rows
    chunk_rows = piece_rows * level_rows
    for source in range(sources):
        wave_ref[source * piece_rows : (source + 1) * piece_rows, :] = received_ref[source].astype(
            jnp.float32
        )
    real, imag = (
        jnp.concatenate(
            [
                wave_ref[pl.ds(phase * half_rows + at, sources, stride=piece_rows), :]
                for at in range(half_rows)
            ],
            axis=0,
        ).T
        for phase in range(2)
    )
    real, imag = real[:channels], imag[:channels]
    tiles = near_ref.shape[0] // lane_count
    for block in range(blocks // tiles):
        far_real = far_ref[block : block + 1, :lane_count]
        far_imag = far_ref[block : block + 1, lane_count:]
        rotated_ref[block * channels : (block + 1) * channels, :] = jnp.concatenate(
            [real * far_real + imag * far_imag, imag * far_real - real * far_imag], axis=1
        ).astype(jnp.bfloat16)
    result = lax.dot_general(
        rotated_ref[...],
        near_ref[...],
        (((1,), (1,)), ((), ())),
        preferred_element_type=jnp.float32,
    )
    points = points_ref[0]
    lane_wide = lax.broadcasted_iota(jnp.int32, (levels, lane_count), 1)
    for block in range(blocks):
        inside = lane_wide < points - block * lane_count
        lanes = slice(block % tiles * lane_count, (block % tiles + 1) * lane_count)
        for field in range(3):
            at = block // tiles * channels + field * levels
            out_ref[pl.ds(field * blocks + block, levels, stride=level_rows), :] = jnp.where(
                inside, result[at : at + levels, lanes], 0.0
            )
    copies = []
    for chunk in range(chunks):
        rows = pl.ds(chunk * chunk_rows, chunk_rows)
        copies.append(pltpu.make_async_copy(out_ref.at[rows], out_hbm.at[rows], sems.at[chunk]))
        copies[-1].start()
    for copy in copies:
        copy.wait()


def packed_body(
    dims,
    prognostic_arrays,
    coriolis,
    weights,
    row_points,
    owner_pairs,
    legendre,
    depths,
    diffusion,
):
    levels, lon_count, group_count, slot_count, parts, per_part, highest = dims
    channels = 3 * levels
    blocks = lon_count // lane_count
    sources = parts * group_count
    tiles = max(count for count in (1, 2, 3) if blocks % count == 0)
    span = tiles * lane_count
    far_rows = -(-(blocks // tiles) // piece_rows) * piece_rows
    chunks = levels // piece_rows
    slot_rows = -(-(highest + 1) // 16) * 16
    steps = pltpu.VMEM((span // piece_rows, 2 * lane_count), jnp.float32)
    in_vmem = pl.BlockSpec(memory_space=pltpu.VMEM)
    in_smem = pl.BlockSpec(memory_space=pltpu.SMEM)
    in_hbm = pl.BlockSpec(memory_space=pltpu.HBM)
    params = pltpu.CompilerParams(vmem_limit_bytes=16 << 20)
    grid = prognostic_arrays.reshape(channels * blocks, lane_count)
    basis = jnp.swapaxes(legendre, 2, 3)
    part = lax.axis_index("lat").astype(jnp.int32).reshape(1)
    group = lax.axis_index("lev").astype(jnp.int32).reshape(1)
    sent, near, far, solve, rows = pl.pallas_call(
        functools.partial(analysis_kernel, dims),
        name="analysis",
        out_shape=(
            pltpu.VMEM((sources, 2 * piece_rows, lane_count), jnp.bfloat16),
            pltpu.VMEM((span, 2 * lane_count), jnp.bfloat16),
            pltpu.VMEM((far_rows, 2 * lane_count), jnp.float32),
            pltpu.VMEM((3 * per_part, slot_rows, lane_count), jnp.float32),
            pltpu.VMEM((piece_rows, lane_count), jnp.float32),
        ),
        in_specs=[in_hbm] + [in_smem] * 5 + [in_hbm] * 4,
        out_specs=(in_vmem,) * 5,
        scratch_shapes=[
            pltpu.VMEM(grid.shape, jnp.float32),
            pltpu.VMEM(owner_pairs.shape, jnp.int32),
            pltpu.VMEM(basis.shape, jnp.bfloat16),
            pltpu.VMEM((1, levels), jnp.float32),
            pltpu.VMEM((1, levels), jnp.float32),
            steps,
            pltpu.VMEM((blocks // tiles * channels, span), jnp.bfloat16),
            pltpu.VMEM((sources * piece_rows, lane_count), jnp.float32),
            pltpu.SemaphoreType.DMA((4 + chunks,)),
        ],
        compiler_params=pltpu.CompilerParams(vmem_limit_bytes=67043328 - (2000 << 10)),
    )(
        grid,
        coriolis,
        weights,
        row_points,
        part,
        group,
        owner_pairs,
        basis,
        depths.reshape(1, levels),
        diffusion.reshape(1, levels),
    )
    received = lax.all_to_all(sent, ("lat", "lev"), split_axis=0, concat_axis=0, tiled=True)
    solved = pl.pallas_call(
        functools.partial(spectral_kernel, dims),
        name="spectral",
        out_shape=jax.ShapeDtypeStruct((sources, piece_rows, lane_count), jnp.bfloat16),
        in_specs=[in_vmem, in_smem, in_vmem, in_vmem],
        out_specs=in_vmem,
        scratch_shapes=[pltpu.VMEM((sources * piece_rows, lane_count), jnp.float32)],
        compiler_params=params,
    )(received, group, solve, rows)
    returned = lax.all_to_all(solved, ("lat", "lev"), split_axis=0, concat_axis=0, tiled=True)
    updated = pl.pallas_call(
        functools.partial(synthesis_kernel, dims),
        name="synthesis",
        out_shape=jax.ShapeDtypeStruct((channels * blocks, lane_count), jnp.float32),
        in_specs=[in_vmem, in_vmem, in_vmem, in_smem],
        out_specs=in_hbm,
        scratch_shapes=[
            pltpu.VMEM((sources * piece_rows, lane_count), jnp.float32),
            pltpu.VMEM((blocks // tiles * channels, 2 * lane_count), jnp.bfloat16),
            pltpu.VMEM((channels * blocks, lane_count), jnp.float32),
            pltpu.SemaphoreType.DMA((chunks,)),
        ],
        compiler_params=params,
    )(returned, near, far, row_points)
    return updated.reshape(prognostic_arrays.shape)


def body(prognostic_arrays, coriolis, weights, row_points, owner_pairs, legendre, depths, diffusion):
    levels, _, row_count, lon_count = prognostic_arrays.shape
    group_count, slot_count = owner_pairs.shape
    slot_total, band_rows = legendre.shape[2:]
    parts = lax.axis_size("lat")
    per_part = -(-slot_count // parts)
    channels = 3 * levels
    fits = (
        row_count == 1
        and band_rows == piece_rows == group_count
        and 4 * per_part == piece_rows
        and slot_count % per_part == 0
        and lon_count % lane_count == 0
        and 2 * per_part * parts * group_count == lane_count
        and levels % 16 == 0
        and channels < slot_total <= lane_count
        and 2 * slot_total + channels <= 2 * lane_count
        and lon_count * slot_total < 2**24
    )
    arguments = (
        prognostic_arrays, coriolis, weights, row_points, owner_pairs, legendre, depths, diffusion
    )
    if not fits:
        return general_body(*arguments)
    dims = (levels, lon_count, group_count, slot_count, parts, per_part, slot_total - 1)
    return packed_body(dims, *arguments)


def solution(mesh):
    in_specs = (
        P(None, None, ("lat", "lev"), None),
        P(("lat", "lev")),
        P(("lat", "lev")),
        P(("lat", "lev")),
        P(),
        P("lev", None, None, "lat"),
        P(),
        P(),
    )
    out_specs = P(None, None, ("lat", "lev"), None)
    return jax.shard_map(body, mesh=mesh, in_specs=in_specs, out_specs=out_specs, check_vma=False)
```

```python
import functools
import math

import jax
import jax.numpy as jnp
from jax import lax
from jax.experimental import pallas as pl
from jax.experimental.pallas import tpu as pltpu
from jax.sharding import PartitionSpec as P

stepsize_delta = 0.5


def tendencies(prognostic_arrays, coriolis):
    vorticity = prognostic_arrays[:, 0]
    spreading_rate_grid = prognostic_arrays[:, 1]
    thermal_state_grid = prognostic_arrays[:, 2]
    rotation = coriolis[None, :, None]
    advanced_curl_rate = vorticity - stepsize_delta * (rotation + vorticity) * spreading_rate_grid
    advanced_spreading_rate = spreading_rate_grid + stepsize_delta * (
        rotation * vorticity - spreading_rate_grid * spreading_rate_grid
    )
    advanced_thermal_state = (
        thermal_state_grid - stepsize_delta * thermal_state_grid * spreading_rate_grid
    )
    return jnp.stack(
        [advanced_curl_rate, advanced_spreading_rate, advanced_thermal_state], axis=1
    ).astype(jnp.bfloat16)


def owner_waves(owner_pairs, highest):
    return jnp.stack([owner_pairs, highest - 1 - owner_pairs], axis=1)


def phase_table(points, wavenumbers, lon_count):
    positions = jnp.arange(lon_count, dtype=jnp.int32)
    product = positions[None, :, None] * wavenumbers[None, None, :] % points[:, None, None]
    angle = (
        product.astype(jnp.float32) * (2.0 * math.pi / points.astype(jnp.float32))[:, None, None]
    )
    return jnp.stack([jnp.cos(angle), -jnp.sin(angle)], axis=2).astype(jnp.bfloat16)


def valid_points(points, lon_count):
    positions = jnp.arange(lon_count, dtype=jnp.int32)
    return positions[None, :] < points[:, None]


def half_mask(my_pairs, slot_total):
    positions = jnp.arange(slot_total, dtype=jnp.int32)
    return positions[None, :] < (slot_total - 1 - my_pairs)[:, None]


def implicit(summed, my_pairs, depth_part, diff_part):
    slot_total = summed.shape[3]
    slot_count = summed.shape[2]
    highest = slot_total - 1
    positions = jnp.arange(slot_total, dtype=jnp.int32)[None, :]
    first_half = positions < (highest - my_pairs)[:, None]
    total = jnp.where(first_half, my_pairs[:, None] + positions, positions - 1).astype(jnp.float32)
    harmonic_operator_spectrum = total * (total + 1.0) / float(highest * highest)
    bundled_prognostics = summed.reshape(-1, 3, 2, slot_count, slot_total)
    vorticity = bundled_prognostics[:, 0]
    spreading_rate_grid = bundled_prognostics[:, 1]
    thermal_state_grid = bundled_prognostics[:, 2]
    layer_stack_count = depth_part[:, None, None, None]
    diff_cols = diff_part[:, None, None, None]
    advanced_curl_rate = vorticity / (
        1.0 + diff_cols * harmonic_operator_spectrum * harmonic_operator_spectrum
    )
    advanced_spreading_rate = (
        spreading_rate_grid + harmonic_operator_spectrum * thermal_state_grid
    ) / (1.0 + layer_stack_count * harmonic_operator_spectrum)
    advanced_thermal_state = thermal_state_grid - layer_stack_count * advanced_spreading_rate
    piled_prognostics = jnp.stack(
        [advanced_curl_rate, advanced_spreading_rate, advanced_thermal_state], axis=1
    )
    return piled_prognostics.reshape(summed.shape).astype(jnp.bfloat16)


def general_body(
    prognostic_arrays, coriolis, weights, row_points, owner_pairs, legendre, depths, diffusion
):
    levels = prognostic_arrays.shape[0]
    row_count = prognostic_arrays.shape[2]
    lon_count = prognostic_arrays.shape[3]
    group_count = owner_pairs.shape[0]
    slot_count = owner_pairs.shape[1]
    local_basis = legendre[0]
    slot_total = local_basis.shape[1]
    highest = slot_total - 1
    channels = levels * 3
    packed = channels * 4 * slot_count
    wavenumbers = owner_waves(owner_pairs, highest).reshape(-1)
    valid = valid_points(row_points, lon_count)
    gridded = tendencies(prognostic_arrays, coriolis).reshape(channels, row_count, lon_count)
    gridded = jnp.where(valid[None], gridded, jnp.zeros((), gridded.dtype))
    phases = phase_table(row_points, wavenumbers, lon_count).reshape(
        row_count, lon_count, 2, group_count, 2, slot_count
    )
    row_scale = weights / row_points.astype(jnp.float32)
    fourier = jnp.einsum("crx,rxqght->grcqht", gridded, phases, preferred_element_type=jnp.float32)
    fourier = (fourier * row_scale[None, :, None, None, None, None]).astype(jnp.bfloat16)
    band_data = lax.all_to_all(
        fourier.reshape(group_count, row_count, packed),
        "lev",
        split_axis=0,
        concat_axis=0,
        tiled=True,
    )
    band_block = band_data.reshape(group_count * row_count, channels, 2, 2, slot_count)
    owner_index = lax.axis_index("lev")
    my_pairs = lax.dynamic_index_in_dim(owner_pairs, owner_index, 0, keepdims=False)
    first_half = half_mask(my_pairs, slot_total)
    half_masks = jnp.stack([first_half, jnp.logical_not(first_half)], axis=0)
    doubling = jnp.where(owner_waves(my_pairs[None], highest)[0] == 0, 1.0, 2.0).astype(jnp.float32)
    both_halves = jnp.einsum(
        "lkqht,tpl->kqhtp", band_block, local_basis, preferred_element_type=jnp.float32
    )
    summed = lax.psum(jnp.where(first_half, both_halves[:, :, 0], both_halves[:, :, 1]), "lat")
    solved = implicit(summed, my_pairs, depths, diffusion)
    masked_spec = jnp.where(half_masks[None, None], solved[:, :, None], jnp.zeros((), solved.dtype))
    inverted = jnp.einsum(
        "kqhtp,tpl->lkqht", masked_spec, local_basis, preferred_element_type=jnp.float32
    )
    inverted = (inverted * doubling[None, None, None]).astype(jnp.bfloat16)
    returned = lax.all_to_all(
        inverted.reshape(group_count, row_count, packed),
        "lev",
        split_axis=0,
        concat_axis=0,
        tiled=True,
    )
    returned = returned.reshape(group_count, row_count, channels, 2, 2, slot_count)
    outgrid = jnp.einsum("grcqht,rxqght->crx", returned, phases, preferred_element_type=jnp.float32)
    outgrid = jnp.where(valid[None], outgrid, jnp.zeros((), outgrid.dtype))
    return outgrid.reshape(levels, 3, row_count, lon_count)


lane_count = 128
piece_rows = 8


def turn_cos_sin(turns):
    scaled = turns * 4.0
    nearest = jnp.floor(scaled + 0.5)
    arc = (scaled - nearest) * (0.5 * math.pi)
    square = arc * arc
    sine = arc + arc * square * (
        -1.6666654611e-1 + square * (8.3321608736e-3 + square * -1.9515295891e-4)
    )
    cosine = (
        1.0
        - 0.5 * square
        + square
        * square
        * (4.166664568298827e-2 + square * (-1.388731625493765e-3 + square * 2.443315711809948e-5))
    )
    swapped = jnp.logical_or(nearest == 1.0, nearest == 3.0)
    cos_part = jnp.where(swapped, sine, cosine)
    sin_part = jnp.where(swapped, cosine, sine)
    cos_part = jnp.where(jnp.logical_or(nearest == 1.0, nearest == 2.0), -cos_part, cos_part)
    sin_part = jnp.where(jnp.logical_or(nearest == 2.0, nearest == 3.0), -sin_part, sin_part)
    return cos_part, sin_part


def turns_of(product, points, inverse):
    rest = product - jnp.floor(product * inverse) * points
    rest = jnp.where(rest < 0.0, rest + points, rest)
    rest = jnp.where(rest >= points, rest - points, rest)
    return rest * inverse


def wave_row(dims, pairs):
    levels, lon_count, group_count, slot_count, parts, per_part, highest = dims
    sources = parts * group_count
    tile = (piece_rows, lane_count)
    row = lax.broadcasted_iota(jnp.int32, tile, 0)
    lane = lax.broadcasted_iota(jnp.int32, tile, 1)
    lane_part = (lane >> (group_count.bit_length() - 1)) & (parts - 1)
    lane_slot = lane_part * per_part + ((lane >> (sources.bit_length() - 1)) & (per_part - 1))
    at_group = (lane & (group_count - 1)) == row
    spread = jnp.zeros(tile, jnp.float32)
    for slot in range(slot_count):
        chosen = jnp.logical_and(at_group, lane_slot == slot)
        spread = jnp.where(chosen, pairs[:, slot : slot + 1].astype(jnp.float32), spread)
    pair = jnp.sum(spread, axis=0, keepdims=True)
    lane_row = lax.broadcasted_iota(jnp.int32, (1, lane_count), 1)
    return jnp.where(lane_row >= per_part * sources, float(highest - 1) - pair, pair)


def factors(count, step, wave, points_row):
    place = lax.broadcasted_iota(jnp.int32, (count, lane_count), 0) * step
    cosine, sine = turn_cos_sin(
        turns_of(place.astype(jnp.float32) * wave, points_row, 1.0 / points_row)
    )
    return cosine, -sine


def fill_factors(wave, points_row, near_ref, far_ref, step_ref):
    span = near_ref.shape[0]
    base_real, base_imag = factors(piece_rows, 1, wave, points_row)
    step_real, step_imag = factors(span // piece_rows, piece_rows, wave, points_row)
    step_ref[:, :lane_count] = step_real
    step_ref[:, lane_count:] = step_imag
    for at in range(0, span // piece_rows, 2):
        rows = []
        for index in (at, at + 1):
            real = step_ref[index : index + 1, :lane_count]
            imag = step_ref[index : index + 1, lane_count:]
            rows.append(
                jnp.concatenate(
                    [base_real * real - base_imag * imag, base_real * imag + base_imag * real],
                    axis=1,
                )
            )
        near_ref[at * piece_rows : (at + 2) * piece_rows, :] = jnp.concatenate(
            rows, axis=0
        ).astype(jnp.bfloat16)
    far_real, far_imag = factors(far_ref.shape[0], span, wave, points_row)
    far_ref[:, :lane_count] = far_real
    far_ref[:, lane_count:] = far_imag


def fill_solve(dims, part, group, pairs, depths, diffusion, solve_ref, rows_ref):
    levels, lon_count, group_count, slot_count, parts, per_part, highest = dims
    lane_row = lax.broadcasted_iota(jnp.int32, (1, lane_count), 1)
    wide = jnp.pad(depths, ((0, 0), (0, lane_count - levels)))
    is_first = lane_row < levels
    depth_row = pltpu.roll(wide, levels, 1) + pltpu.roll(wide, 2 * levels, 1)
    coeff_row = depth_row + jnp.pad(diffusion, ((0, 0), (0, lane_count - levels)))
    rows_ref[0:1, :] = depth_row
    row = lax.broadcasted_iota(jnp.int32, pairs.shape, 0)
    column = lax.broadcasted_iota(jnp.int32, pairs.shape, 1)
    position = lax.broadcasted_iota(jnp.int32, (solve_ref.shape[1], lane_count), 0).astype(
        jnp.float32
    )
    for index in range(per_part):
        slot = jnp.minimum(part * per_part + index, slot_count - 1)
        chosen = jnp.logical_and(row == group, column == slot)
        pair = jnp.sum(jnp.where(chosen, pairs.astype(jnp.float32), 0.0), axis=0, keepdims=True)
        pair = jnp.broadcast_to(jnp.sum(pair, axis=1, keepdims=True), (1, lane_count))
        lower_half = position < float(highest) - pair
        total = jnp.where(lower_half, pair + position, position - 1.0)
        operator = total * (total + 1.0) / float(highest * highest)
        factor = jnp.where(is_first, operator * operator, operator)
        solve_ref[3 * index] = 1.0 / (1.0 + coeff_row * factor)
        solve_ref[3 * index + 1] = jnp.where(is_first, 0.0, operator)
        solve_ref[3 * index + 2] = jnp.where(lower_half, 1.0, 0.0)
        for half in range(2):
            wavenumber = pair if half == 0 else float(highest - 1) - pair
            at = 1 + half * per_part + index
            rows_ref[at : at + 1, :] = jnp.where(wavenumber == 0.0, 1.0, 2.0)


def analysis_kernel(
    dims,
    grid_hbm,
    coriolis_ref,
    weights_ref,
    points_ref,
    part_ref,
    group_ref,
    pairs_hbm,
    legendre_hbm,
    depths_hbm,
    diffusion_hbm,
    sent_ref,
    near_ref,
    far_ref,
    solve_ref,
    rows_ref,
    grid_ref,
    pairs_ref,
    legendre_ref,
    depths_ref,
    diffusion_ref,
    step_ref,
    rhs_ref,
    wave_ref,
    sems,
):
    levels, lon_count, group_count, slot_count, parts, per_part, highest = dims
    channels = 3 * levels
    blocks = lon_count // lane_count
    active = slot_count // per_part
    sources = parts * group_count
    level_rows = 3 * blocks
    chunks = levels // piece_rows
    chunk_rows = piece_rows * level_rows
    copies = [pltpu.make_async_copy(pairs_hbm, pairs_ref, sems.at[0])]
    small = (
        pltpu.make_async_copy(depths_hbm, depths_ref, sems.at[2 + chunks]),
        pltpu.make_async_copy(diffusion_hbm, diffusion_ref, sems.at[3 + chunks]),
    )
    for chunk in range(chunks):
        rows = pl.ds(chunk * chunk_rows, chunk_rows)
        copies.append(
            pltpu.make_async_copy(grid_hbm.at[rows], grid_ref.at[rows], sems.at[1 + chunk])
        )
    copies.append(pltpu.make_async_copy(legendre_hbm, legendre_ref, sems.at[1 + chunks]))
    copies[0].start()
    for copy in small:
        copy.start()
    for copy in copies[1:]:
        copy.start()
    copies[0].wait()

    points = points_ref[0]
    points_row = jnp.full((1, lane_count), points, jnp.int32).astype(jnp.float32)
    wave = wave_row(dims, pairs_ref[...])
    fill_factors(wave, points_row, near_ref, far_ref, step_ref)
    for copy in small:
        copy.wait()
    fill_solve(
        dims,
        part_ref[0],
        group_ref[0],
        pairs_ref[...],
        depths_ref[...],
        diffusion_ref[...],
        solve_ref,
        rows_ref,
    )
    tiles = near_ref.shape[0] // lane_count
    rotation = coriolis_ref[0]
    half_rotation = stepsize_delta * rotation
    lane = lax.broadcasted_iota(jnp.int32, (piece_rows, lane_count), 1)
    lane_wide = lax.broadcasted_iota(jnp.int32, (levels, lane_count), 1)
    for chunk in range(chunks):
        copies[1 + chunk].wait()
    for block in range(blocks):
        vorticity, spreading, thermal = (
            grid_ref[pl.ds(field * blocks + block, levels, stride=level_rows), :]
            for field in range(3)
        )
        inside = lane_wide < points - block * lane_count
        stepped = stepsize_delta * spreading
        advanced = (
            vorticity - (rotation + vorticity) * stepped,
            spreading + (half_rotation * vorticity - spreading * stepped),
            thermal - thermal * stepped,
        )
        lanes = slice(block % tiles * lane_count, (block % tiles + 1) * lane_count)
        for field in range(3):
            at = block // tiles * channels + field * levels
            rhs_ref[at : at + levels, lanes] = jnp.where(inside, advanced[field], 0.0).astype(
                jnp.bfloat16
            )
    partial = jnp.dot(rhs_ref[...], near_ref[...], preferred_element_type=jnp.float32)
    real, imag = None, None
    for block in range(blocks // tiles):
        part_real = partial[block * channels : (block + 1) * channels, :lane_count]
        part_imag = partial[block * channels : (block + 1) * channels, lane_count:]
        far_real = far_ref[block : block + 1, :lane_count]
        far_imag = far_ref[block : block + 1, lane_count:]
        add_real = part_real * far_real - part_imag * far_imag
        add_imag = part_real * far_imag + part_imag * far_real
        real = add_real if block == 0 else real + add_real
        imag = add_imag if block == 0 else imag + add_imag
    scale = jnp.full((1, lane_count), weights_ref[0], jnp.float32) / points_row
    half_rows = 2 * per_part
    rest = jnp.zeros((lane_count - channels, lane_count), jnp.float32)
    for phase, value in enumerate((real, imag)):
        turned = jnp.concatenate([value * scale, rest], axis=0).T
        for at in range(half_rows):
            wave_ref[pl.ds(phase * half_rows + at, sources, stride=piece_rows), :] = turned[
                at * sources : (at + 1) * sources
            ]

    copies[1 + chunks].wait()
    slot_total = highest + 1
    left = lane_count - channels
    for part in range(active):
        first, second = (
            jnp.pad(
                legendre_ref[0, part * per_part + index].astype(jnp.float32),
                ((0, 0), (0, lane_count - slot_total)),
            )
            for index in range(2)
        )
        upper_basis = pltpu.roll(first, channels, 1)
        lower = jnp.where(
            lane < slot_total, second, pltpu.roll(first, (slot_total - left) % lane_count, 1)
        )
        for group in range(group_count):
            at = part * group_count + group
            upper = jnp.where(
                lane < channels,
                wave_ref[at * piece_rows : (at + 1) * piece_rows, :],
                upper_basis,
            )
            sent_ref[at] = jnp.concatenate([upper, lower], axis=0).astype(jnp.bfloat16)
    for at in range(active * group_count, sources):
        sent_ref[at] = jnp.zeros((2 * piece_rows, lane_count), jnp.bfloat16)


def spectral_kernel(
    dims, received_ref, group_ref, solve_ref, rows_ref, sent_ref, wave_ref, back_ref
):
    levels, lon_count, group_count, slot_count, parts, per_part, highest = dims
    channels = 3 * levels
    slot_total = highest + 1
    left = lane_count - channels
    sources = parts * group_count
    group = group_ref[0]
    lane = lax.broadcasted_iota(jnp.int32, (piece_rows, lane_count), 1)
    for source in range(sources):
        wave_ref[source * piece_rows : (source + 1) * piece_rows, :] = received_ref[
            source, :piece_rows, :
        ].astype(jnp.float32)
    first, second = [], []
    for band in range(parts):
        piece = received_ref[band * group_count + group].astype(jnp.float32)
        upper, lower = piece[:piece_rows], piece[piece_rows:]
        start = pltpu.roll(upper, left, 1)
        rest = pltpu.roll(lower, (lane_count - (slot_total - left)) % lane_count, 1)
        first.append(jnp.where(lane < left, start, jnp.where(lane < slot_total, rest, 0.0)))
        second.append(jnp.where(lane < slot_total, lower, 0.0))
    bases = [jnp.concatenate(first, axis=0), jnp.concatenate(second, axis=0)]
    lane_row = lax.broadcasted_iota(jnp.int32, (1, lane_count), 1)
    is_last = lane_row >= 2 * levels
    depth_row = rows_ref[0:1, :]
    held = solve_ref.shape[1]
    basis_rows = [value.astype(jnp.bfloat16)[:, :held] for value in bases]
    every = []
    for index in range(per_part):
        basis_turned = bases[index].T[:held].astype(jnp.bfloat16)
        specs = []
        for half in range(2):
            waves = jnp.concatenate(
                [
                    wave_ref[
                        pl.ds((phase * 2 + half) * per_part + index, sources, stride=piece_rows), :
                    ]
                    for phase in range(2)
                ],
                axis=1,
            ).astype(jnp.bfloat16)
            specs.append(jnp.dot(basis_turned, waves, preferred_element_type=jnp.float32))
        every.append(specs)
    for index in range(per_part):
        specs, basis = every[index], basis_rows[index]
        lower_half = solve_ref[3 * index + 2] > 0.5
        solved = []
        for phase in range(2):
            lanes = slice(phase * lane_count, (phase + 1) * lane_count)
            spec = jnp.where(lower_half, specs[0][:, lanes], specs[1][:, lanes])
            thermal = pltpu.roll(spec, lane_count - levels, 1)
            quotient = (spec + solve_ref[3 * index + 1] * thermal) * solve_ref[3 * index]
            moved = pltpu.roll(quotient, levels, 1)
            solved.append(jnp.where(is_last, spec - depth_row * moved, quotient))
        for half in range(2):
            kept = jnp.concatenate(
                [
                    jnp.where(lower_half, value, 0.0)
                    if half == 0
                    else jnp.where(lower_half, 0.0, value)
                    for value in solved
                ],
                axis=1,
            ).astype(jnp.bfloat16)
            back = jnp.dot(basis, kept, preferred_element_type=jnp.float32)
            row = 1 + half * per_part + index
            doubling = rows_ref[row : row + 1, :]
            for phase in range(2):
                at = (phase * 2 + half) * per_part + index
                back_ref[pl.ds(at, sources, stride=piece_rows), :] = (
                    back[:, phase * lane_count : (phase + 1) * lane_count] * doubling
                )
    for source in range(sources):
        sent_ref[source] = back_ref[
            source * piece_rows : (source + 1) * piece_rows, :
        ].astype(jnp.bfloat16)


def synthesis_kernel(
    dims,
    received_ref,
    near_ref,
    far_ref,
    points_ref,
    out_hbm,
    wave_ref,
    rotated_ref,
    out_ref,
    sems,
):
    levels, lon_count, group_count, slot_count, parts, per_part, highest = dims
    channels = 3 * levels
    blocks = lon_count // lane_count
    sources = parts * group_count
    half_rows = 2 * per_part
    level_rows = 3 * blocks
    chunks = levels // piece_rows
    chunk_rows = piece_rows * level_rows
    for source in range(sources):
        wave_ref[source * piece_rows : (source + 1) * piece_rows, :] = received_ref[source].astype(
            jnp.float32
        )
    real, imag = (
        jnp.concatenate(
            [
                wave_ref[pl.ds(phase * half_rows + at, sources, stride=piece_rows), :]
                for at in range(half_rows)
            ],
            axis=0,
        ).T
        for phase in range(2)
    )
    real, imag = real[:channels], imag[:channels]
    tiles = near_ref.shape[0] // lane_count
    for block in range(blocks // tiles):
        far_real = far_ref[block : block + 1, :lane_count]
        far_imag = far_ref[block : block + 1, lane_count:]
        rotated_ref[block * channels : (block + 1) * channels, :] = jnp.concatenate(
            [real * far_real + imag * far_imag, imag * far_real - real * far_imag], axis=1
        ).astype(jnp.bfloat16)
    result = lax.dot_general(
        rotated_ref[...],
        near_ref[...],
        (((1,), (1,)), ((), ())),
        preferred_element_type=jnp.float32,
    )
    points = points_ref[0]
    lane_wide = lax.broadcasted_iota(jnp.int32, (levels, lane_count), 1)
    for block in range(blocks):
        inside = lane_wide < points - block * lane_count
        lanes = slice(block % tiles * lane_count, (block % tiles + 1) * lane_count)
        for field in range(3):
            at = block // tiles * channels + field * levels
            out_ref[pl.ds(field * blocks + block, levels, stride=level_rows), :] = jnp.where(
                inside, result[at : at + levels, lanes], 0.0
            )
    copies = []
    for chunk in range(chunks):
        rows = pl.ds(chunk * chunk_rows, chunk_rows)
        copies.append(pltpu.make_async_copy(out_ref.at[rows], out_hbm.at[rows], sems.at[chunk]))
        copies[-1].start()
    for copy in copies:
        copy.wait()


def packed_body(
    dims,
    prognostic_arrays,
    coriolis,
    weights,
    row_points,
    owner_pairs,
    legendre,
    depths,
    diffusion,
):
    levels, lon_count, group_count, slot_count, parts, per_part, highest = dims
    channels = 3 * levels
    blocks = lon_count // lane_count
    sources = parts * group_count
    tiles = max(count for count in (1, 2, 3) if blocks % count == 0)
    span = tiles * lane_count
    far_rows = -(-(blocks // tiles) // piece_rows) * piece_rows
    chunks = levels // piece_rows
    slot_rows = -(-(highest + 1) // 16) * 16
    steps = pltpu.VMEM((span // piece_rows, 2 * lane_count), jnp.float32)
    in_vmem = pl.BlockSpec(memory_space=pltpu.VMEM)
    in_smem = pl.BlockSpec(memory_space=pltpu.SMEM)
    in_hbm = pl.BlockSpec(memory_space=pltpu.HBM)
    params = pltpu.CompilerParams(vmem_limit_bytes=16 << 20)
    grid = prognostic_arrays.reshape(channels * blocks, lane_count)
    basis = jnp.swapaxes(legendre, 2, 3)
    part = lax.axis_index("lat").astype(jnp.int32).reshape(1)
    group = lax.axis_index("lev").astype(jnp.int32).reshape(1)
    sent, near, far, solve, rows = pl.pallas_call(
        functools.partial(analysis_kernel, dims),
        name="analysis",
        out_shape=(
            pltpu.VMEM((sources, 2 * piece_rows, lane_count), jnp.bfloat16),
            pltpu.VMEM((span, 2 * lane_count), jnp.bfloat16),
            pltpu.VMEM((far_rows, 2 * lane_count), jnp.float32),
            pltpu.VMEM((3 * per_part, slot_rows, lane_count), jnp.float32),
            pltpu.VMEM((piece_rows, lane_count), jnp.float32),
        ),
        in_specs=[in_hbm] + [in_smem] * 5 + [in_hbm] * 4,
        out_specs=(in_vmem,) * 5,
        scratch_shapes=[
            pltpu.VMEM(grid.shape, jnp.float32),
            pltpu.VMEM(owner_pairs.shape, jnp.int32),
            pltpu.VMEM(basis.shape, jnp.bfloat16),
            pltpu.VMEM((1, levels), jnp.float32),
            pltpu.VMEM((1, levels), jnp.float32),
            steps,
            pltpu.VMEM((blocks // tiles * channels, span), jnp.bfloat16),
            pltpu.VMEM((sources * piece_rows, lane_count), jnp.float32),
            pltpu.SemaphoreType.DMA((4 + chunks,)),
        ],
        compiler_params=pltpu.CompilerParams(vmem_limit_bytes=67043328 - (2000 << 10)),
    )(
        grid,
        coriolis,
        weights,
        row_points,
        part,
        group,
        owner_pairs,
        basis,
        depths.reshape(1, levels),
        diffusion.reshape(1, levels),
    )
    received = lax.all_to_all(sent, ("lat", "lev"), split_axis=0, concat_axis=0, tiled=True)
    solved = pl.pallas_call(
        functools.partial(spectral_kernel, dims),
        name="spectral",
        out_shape=jax.ShapeDtypeStruct((sources, piece_rows, lane_count), jnp.bfloat16),
        in_specs=[in_vmem, in_smem, in_vmem, in_vmem],
        out_specs=in_vmem,
        scratch_shapes=[pltpu.VMEM((sources * piece_rows, lane_count), jnp.float32)] * 2,
        compiler_params=params,
    )(received, group, solve, rows)
    returned = lax.all_to_all(solved, ("lat", "lev"), split_axis=0, concat_axis=0, tiled=True)
    updated = pl.pallas_call(
        functools.partial(synthesis_kernel, dims),
        name="synthesis",
        out_shape=jax.ShapeDtypeStruct((channels * blocks, lane_count), jnp.float32),
        in_specs=[in_vmem, in_vmem, in_vmem, in_smem],
        out_specs=in_hbm,
        scratch_shapes=[
            pltpu.VMEM((sources * piece_rows, lane_count), jnp.float32),
            pltpu.VMEM((blocks // tiles * channels, 2 * lane_count), jnp.bfloat16),
            pltpu.VMEM((channels * blocks, lane_count), jnp.float32),
            pltpu.SemaphoreType.DMA((chunks,)),
        ],
        compiler_params=params,
    )(returned, near, far, row_points)
    return updated.reshape(prognostic_arrays.shape)


def body(prognostic_arrays, coriolis, weights, row_points, owner_pairs, legendre, depths, diffusion):
    levels, _, row_count, lon_count = prognostic_arrays.shape
    group_count, slot_count = owner_pairs.shape
    slot_total, band_rows = legendre.shape[2:]
    parts = lax.axis_size("lat")
    per_part = -(-slot_count // parts)
    channels = 3 * levels
    fits = (
        row_count == 1
        and band_rows == piece_rows == group_count
        and 4 * per_part == piece_rows
        and slot_count % per_part == 0
        and lon_count % lane_count == 0
        and 2 * per_part * parts * group_count == lane_count
        and levels % 16 == 0
        and channels < slot_total <= lane_count
        and 2 * slot_total + channels <= 2 * lane_count
        and lon_count * slot_total < 2**24
    )
    arguments = (
        prognostic_arrays, coriolis, weights, row_points, owner_pairs, legendre, depths, diffusion
    )
    if not fits:
        return general_body(*arguments)
    dims = (levels, lon_count, group_count, slot_count, parts, per_part, slot_total - 1)
    return packed_body(dims, *arguments)


def solution(mesh):
    in_specs = (
        P(None, None, ("lat", "lev"), None),
        P(("lat", "lev")),
        P(("lat", "lev")),
        P(("lat", "lev")),
        P(),
        P("lev", None, None, "lat"),
        P(),
        P(),
    )
    out_specs = P(None, None, ("lat", "lev"), None)
    return jax.shard_map(body, mesh=mesh, in_specs=in_specs, out_specs=out_specs, check_vma=False)
```

```python
import functools
import math

import jax
import jax.numpy as jnp
from jax import lax
from jax.experimental import pallas as pl
from jax.experimental.pallas import tpu as pltpu
from jax.sharding import PartitionSpec as P

stepsize_delta = 0.5


def tendencies(prognostic_arrays, coriolis):
    vorticity = prognostic_arrays[:, 0]
    spreading_rate_grid = prognostic_arrays[:, 1]
    thermal_state_grid = prognostic_arrays[:, 2]
    rotation = coriolis[None, :, None]
    advanced_curl_rate = vorticity - stepsize_delta * (rotation + vorticity) * spreading_rate_grid
    advanced_spreading_rate = spreading_rate_grid + stepsize_delta * (
        rotation * vorticity - spreading_rate_grid * spreading_rate_grid
    )
    advanced_thermal_state = (
        thermal_state_grid - stepsize_delta * thermal_state_grid * spreading_rate_grid
    )
    return jnp.stack(
        [advanced_curl_rate, advanced_spreading_rate, advanced_thermal_state], axis=1
    ).astype(jnp.bfloat16)


def owner_waves(owner_pairs, highest):
    return jnp.stack([owner_pairs, highest - 1 - owner_pairs], axis=1)


def phase_table(points, wavenumbers, lon_count):
    positions = jnp.arange(lon_count, dtype=jnp.int32)
    product = positions[None, :, None] * wavenumbers[None, None, :] % points[:, None, None]
    angle = (
        product.astype(jnp.float32) * (2.0 * math.pi / points.astype(jnp.float32))[:, None, None]
    )
    return jnp.stack([jnp.cos(angle), -jnp.sin(angle)], axis=2).astype(jnp.bfloat16)


def valid_points(points, lon_count):
    positions = jnp.arange(lon_count, dtype=jnp.int32)
    return positions[None, :] < points[:, None]


def half_mask(my_pairs, slot_total):
    positions = jnp.arange(slot_total, dtype=jnp.int32)
    return positions[None, :] < (slot_total - 1 - my_pairs)[:, None]


def implicit(summed, my_pairs, depth_part, diff_part):
    slot_total = summed.shape[3]
    slot_count = summed.shape[2]
    highest = slot_total - 1
    positions = jnp.arange(slot_total, dtype=jnp.int32)[None, :]
    first_half = positions < (highest - my_pairs)[:, None]
    total = jnp.where(first_half, my_pairs[:, None] + positions, positions - 1).astype(jnp.float32)
    harmonic_operator_spectrum = total * (total + 1.0) / float(highest * highest)
    bundled_prognostics = summed.reshape(-1, 3, 2, slot_count, slot_total)
    vorticity = bundled_prognostics[:, 0]
    spreading_rate_grid = bundled_prognostics[:, 1]
    thermal_state_grid = bundled_prognostics[:, 2]
    layer_stack_count = depth_part[:, None, None, None]
    diff_cols = diff_part[:, None, None, None]
    advanced_curl_rate = vorticity / (
        1.0 + diff_cols * harmonic_operator_spectrum * harmonic_operator_spectrum
    )
    advanced_spreading_rate = (
        spreading_rate_grid + harmonic_operator_spectrum * thermal_state_grid
    ) / (1.0 + layer_stack_count * harmonic_operator_spectrum)
    advanced_thermal_state = thermal_state_grid - layer_stack_count * advanced_spreading_rate
    piled_prognostics = jnp.stack(
        [advanced_curl_rate, advanced_spreading_rate, advanced_thermal_state], axis=1
    )
    return piled_prognostics.reshape(summed.shape).astype(jnp.bfloat16)


def general_body(
    prognostic_arrays, coriolis, weights, row_points, owner_pairs, legendre, depths, diffusion
):
    levels = prognostic_arrays.shape[0]
    row_count = prognostic_arrays.shape[2]
    lon_count = prognostic_arrays.shape[3]
    group_count = owner_pairs.shape[0]
    slot_count = owner_pairs.shape[1]
    local_basis = legendre[0]
    slot_total = local_basis.shape[1]
    highest = slot_total - 1
    channels = levels * 3
    packed = channels * 4 * slot_count
    wavenumbers = owner_waves(owner_pairs, highest).reshape(-1)
    valid = valid_points(row_points, lon_count)
    gridded = tendencies(prognostic_arrays, coriolis).reshape(channels, row_count, lon_count)
    gridded = jnp.where(valid[None], gridded, jnp.zeros((), gridded.dtype))
    phases = phase_table(row_points, wavenumbers, lon_count).reshape(
        row_count, lon_count, 2, group_count, 2, slot_count
    )
    row_scale = weights / row_points.astype(jnp.float32)
    fourier = jnp.einsum("crx,rxqght->grcqht", gridded, phases, preferred_element_type=jnp.float32)
    fourier = (fourier * row_scale[None, :, None, None, None, None]).astype(jnp.bfloat16)
    band_data = lax.all_to_all(
        fourier.reshape(group_count, row_count, packed),
        "lev",
        split_axis=0,
        concat_axis=0,
        tiled=True,
    )
    band_block = band_data.reshape(group_count * row_count, channels, 2, 2, slot_count)
    owner_index = lax.axis_index("lev")
    my_pairs = lax.dynamic_index_in_dim(owner_pairs, owner_index, 0, keepdims=False)
    first_half = half_mask(my_pairs, slot_total)
    half_masks = jnp.stack([first_half, jnp.logical_not(first_half)], axis=0)
    doubling = jnp.where(owner_waves(my_pairs[None], highest)[0] == 0, 1.0, 2.0).astype(jnp.float32)
    both_halves = jnp.einsum(
        "lkqht,tpl->kqhtp", band_block, local_basis, preferred_element_type=jnp.float32
    )
    summed = lax.psum(jnp.where(first_half, both_halves[:, :, 0], both_halves[:, :, 1]), "lat")
    solved = implicit(summed, my_pairs, depths, diffusion)
    masked_spec = jnp.where(half_masks[None, None], solved[:, :, None], jnp.zeros((), solved.dtype))
    inverted = jnp.einsum(
        "kqhtp,tpl->lkqht", masked_spec, local_basis, preferred_element_type=jnp.float32
    )
    inverted = (inverted * doubling[None, None, None]).astype(jnp.bfloat16)
    returned = lax.all_to_all(
        inverted.reshape(group_count, row_count, packed),
        "lev",
        split_axis=0,
        concat_axis=0,
        tiled=True,
    )
    returned = returned.reshape(group_count, row_count, channels, 2, 2, slot_count)
    outgrid = jnp.einsum("grcqht,rxqght->crx", returned, phases, preferred_element_type=jnp.float32)
    outgrid = jnp.where(valid[None], outgrid, jnp.zeros((), outgrid.dtype))
    return outgrid.reshape(levels, 3, row_count, lon_count)


lane_count = 128
piece_rows = 8


def turn_cos_sin(turns):
    scaled = turns * 4.0
    nearest = jnp.floor(scaled + 0.5)
    arc = (scaled - nearest) * (0.5 * math.pi)
    square = arc * arc
    sine = arc + arc * square * (
        -1.6666654611e-1 + square * (8.3321608736e-3 + square * -1.9515295891e-4)
    )
    cosine = (
        1.0
        - 0.5 * square
        + square
        * square
        * (4.166664568298827e-2 + square * (-1.388731625493765e-3 + square * 2.443315711809948e-5))
    )
    swapped = jnp.logical_or(nearest == 1.0, nearest == 3.0)
    cos_part = jnp.where(swapped, sine, cosine)
    sin_part = jnp.where(swapped, cosine, sine)
    cos_part = jnp.where(jnp.logical_or(nearest == 1.0, nearest == 2.0), -cos_part, cos_part)
    sin_part = jnp.where(jnp.logical_or(nearest == 2.0, nearest == 3.0), -sin_part, sin_part)
    return cos_part, sin_part


def turns_of(product, points, inverse):
    rest = product - jnp.floor(product * inverse) * points
    rest = jnp.where(rest < 0.0, rest + points, rest)
    rest = jnp.where(rest >= points, rest - points, rest)
    return rest * inverse


def wave_row(dims, pairs):
    levels, lon_count, group_count, slot_count, parts, per_part, highest = dims
    sources = parts * group_count
    tile = (piece_rows, lane_count)
    row = lax.broadcasted_iota(jnp.int32, tile, 0)
    lane = lax.broadcasted_iota(jnp.int32, tile, 1)
    lane_part = (lane >> (group_count.bit_length() - 1)) & (parts - 1)
    lane_slot = lane_part * per_part + ((lane >> (sources.bit_length() - 1)) & (per_part - 1))
    at_group = (lane & (group_count - 1)) == row
    spread = jnp.zeros(tile, jnp.float32)
    for slot in range(slot_count):
        chosen = jnp.logical_and(at_group, lane_slot == slot)
        spread = jnp.where(chosen, pairs[:, slot : slot + 1].astype(jnp.float32), spread)
    pair = jnp.sum(spread, axis=0, keepdims=True)
    lane_row = lax.broadcasted_iota(jnp.int32, (1, lane_count), 1)
    return jnp.where(lane_row >= per_part * sources, float(highest - 1) - pair, pair)


def factors(count, step, wave, points_row):
    place = lax.broadcasted_iota(jnp.int32, (count, lane_count), 0) * step
    cosine, sine = turn_cos_sin(
        turns_of(place.astype(jnp.float32) * wave, points_row, 1.0 / points_row)
    )
    return cosine, -sine


def fill_factors(wave, points_row, near_ref, far_ref, step_ref):
    span = near_ref.shape[0]
    base_real, base_imag = factors(piece_rows, 1, wave, points_row)
    step_real, step_imag = factors(span // piece_rows, piece_rows, wave, points_row)
    step_ref[:, :lane_count] = step_real
    step_ref[:, lane_count:] = step_imag
    for at in range(0, span // piece_rows, 2):
        rows = []
        for index in (at, at + 1):
            real = step_ref[index : index + 1, :lane_count]
            imag = step_ref[index : index + 1, lane_count:]
            rows.append(
                jnp.concatenate(
                    [base_real * real - base_imag * imag, base_real * imag + base_imag * real],
                    axis=1,
                )
            )
        near_ref[at * piece_rows : (at + 2) * piece_rows, :] = jnp.concatenate(
            rows, axis=0
        ).astype(jnp.bfloat16)
    far_real, far_imag = factors(far_ref.shape[0], span, wave, points_row)
    far_ref[:, :lane_count] = far_real
    far_ref[:, lane_count:] = far_imag


def fill_solve(dims, part, group, pairs, depths, diffusion, solve_ref, rows_ref):
    levels, lon_count, group_count, slot_count, parts, per_part, highest = dims
    lane_row = lax.broadcasted_iota(jnp.int32, (1, lane_count), 1)
    wide = jnp.pad(depths, ((0, 0), (0, lane_count - levels)))
    is_first = lane_row < levels
    depth_row = pltpu.roll(wide, levels, 1) + pltpu.roll(wide, 2 * levels, 1)
    coeff_row = depth_row + jnp.pad(diffusion, ((0, 0), (0, lane_count - levels)))
    rows_ref[0:1, :] = depth_row
    row = lax.broadcasted_iota(jnp.int32, pairs.shape, 0)
    column = lax.broadcasted_iota(jnp.int32, pairs.shape, 1)
    position = lax.broadcasted_iota(jnp.int32, (solve_ref.shape[1], lane_count), 0).astype(
        jnp.float32
    )
    for index in range(per_part):
        slot = jnp.minimum(part * per_part + index, slot_count - 1)
        chosen = jnp.logical_and(row == group, column == slot)
        pair = jnp.sum(jnp.where(chosen, pairs.astype(jnp.float32), 0.0), axis=0, keepdims=True)
        pair = jnp.broadcast_to(jnp.sum(pair, axis=1, keepdims=True), (1, lane_count))
        lower_half = position < float(highest) - pair
        total = jnp.where(lower_half, pair + position, position - 1.0)
        operator = total * (total + 1.0) / float(highest * highest)
        factor = jnp.where(is_first, operator * operator, operator)
        solve_ref[3 * index] = 1.0 / (1.0 + coeff_row * factor)
        solve_ref[3 * index + 1] = jnp.where(is_first, 0.0, operator)
        solve_ref[3 * index + 2] = jnp.where(lower_half, 1.0, 0.0)
        for half in range(2):
            wavenumber = pair if half == 0 else float(highest - 1) - pair
            at = 1 + half * per_part + index
            rows_ref[at : at + 1, :] = jnp.where(wavenumber == 0.0, 1.0, 2.0)


def analysis_kernel(
    dims,
    grid_hbm,
    coriolis_ref,
    weights_ref,
    points_ref,
    part_ref,
    group_ref,
    pairs_hbm,
    legendre_hbm,
    depths_hbm,
    diffusion_hbm,
    sent_ref,
    near_ref,
    far_ref,
    solve_ref,
    rows_ref,
    grid_ref,
    pairs_ref,
    legendre_ref,
    depths_ref,
    diffusion_ref,
    step_ref,
    rhs_ref,
    wave_ref,
    sems,
):
    levels, lon_count, group_count, slot_count, parts, per_part, highest = dims
    channels = 3 * levels
    blocks = lon_count // lane_count
    active = slot_count // per_part
    sources = parts * group_count
    level_rows = 3 * blocks
    chunks = levels // piece_rows
    chunk_rows = piece_rows * level_rows
    copies = [pltpu.make_async_copy(pairs_hbm, pairs_ref, sems.at[0])]
    small = (
        pltpu.make_async_copy(depths_hbm, depths_ref, sems.at[2 + chunks]),
        pltpu.make_async_copy(diffusion_hbm, diffusion_ref, sems.at[3 + chunks]),
    )
    for chunk in range(chunks):
        rows = pl.ds(chunk * chunk_rows, chunk_rows)
        copies.append(
            pltpu.make_async_copy(grid_hbm.at[rows], grid_ref.at[rows], sems.at[1 + chunk])
        )
    copies.append(pltpu.make_async_copy(legendre_hbm, legendre_ref, sems.at[1 + chunks]))
    copies[0].start()
    for copy in small:
        copy.start()
    for copy in copies[1:]:
        copy.start()
    copies[0].wait()

    points = points_ref[0]
    points_row = jnp.full((1, lane_count), points, jnp.int32).astype(jnp.float32)
    wave = wave_row(dims, pairs_ref[...])
    fill_factors(wave, points_row, near_ref, far_ref, step_ref)
    for copy in small:
        copy.wait()
    fill_solve(
        dims,
        part_ref[0],
        group_ref[0],
        pairs_ref[...],
        depths_ref[...],
        diffusion_ref[...],
        solve_ref,
        rows_ref,
    )
    tiles = near_ref.shape[0] // lane_count
    rotation = coriolis_ref[0]
    half_rotation = stepsize_delta * rotation
    lane = lax.broadcasted_iota(jnp.int32, (piece_rows, lane_count), 1)
    lane_wide = lax.broadcasted_iota(jnp.int32, (levels, lane_count), 1)
    for chunk in range(chunks):
        copies[1 + chunk].wait()
    for block in range(blocks):
        vorticity, spreading, thermal = (
            grid_ref[pl.ds(field * blocks + block, levels, stride=level_rows), :]
            for field in range(3)
        )
        inside = lane_wide < points - block * lane_count
        stepped = stepsize_delta * spreading
        advanced = (
            vorticity - (rotation + vorticity) * stepped,
            spreading + (half_rotation * vorticity - spreading * stepped),
            thermal - thermal * stepped,
        )
        lanes = slice(block % tiles * lane_count, (block % tiles + 1) * lane_count)
        for field in range(3):
            at = block // tiles * channels + field * levels
            rhs_ref[at : at + levels, lanes] = jnp.where(inside, advanced[field], 0.0).astype(
                jnp.bfloat16
            )
    partial = jnp.dot(rhs_ref[...], near_ref[...], preferred_element_type=jnp.float32)
    real, imag = None, None
    for block in range(blocks // tiles):
        part_real = partial[block * channels : (block + 1) * channels, :lane_count]
        part_imag = partial[block * channels : (block + 1) * channels, lane_count:]
        far_real = far_ref[block : block + 1, :lane_count]
        far_imag = far_ref[block : block + 1, lane_count:]
        add_real = part_real * far_real - part_imag * far_imag
        add_imag = part_real * far_imag + part_imag * far_real
        real = add_real if block == 0 else real + add_real
        imag = add_imag if block == 0 else imag + add_imag
    scale = jnp.full((1, lane_count), weights_ref[0], jnp.float32) / points_row
    half_rows = 2 * per_part
    rest = jnp.zeros((lane_count - channels, lane_count), jnp.float32)
    for phase, value in enumerate((real, imag)):
        turned = jnp.concatenate([value * scale, rest], axis=0).T
        for at in range(half_rows):
            wave_ref[pl.ds(phase * half_rows + at, sources, stride=piece_rows), :] = turned[
                at * sources : (at + 1) * sources
            ]

    copies[1 + chunks].wait()
    slot_total = highest + 1
    left = lane_count - channels
    for part in range(active):
        first, second = (
            jnp.pad(
                legendre_ref[0, part * per_part + index].astype(jnp.float32),
                ((0, 0), (0, lane_count - slot_total)),
            )
            for index in range(2)
        )
        upper_basis = pltpu.roll(first, channels, 1)
        lower = jnp.where(
            lane < slot_total, second, pltpu.roll(first, (slot_total - left) % lane_count, 1)
        )
        for group in range(group_count):
            at = part * group_count + group
            upper = jnp.where(
                lane < channels,
                wave_ref[at * piece_rows : (at + 1) * piece_rows, :],
                upper_basis,
            )
            sent_ref[at] = jnp.concatenate([upper, lower], axis=0).astype(jnp.bfloat16)
    for at in range(active * group_count, sources):
        sent_ref[at] = jnp.zeros((2 * piece_rows, lane_count), jnp.bfloat16)


def spectral_kernel(
    dims, received_ref, group_ref, solve_ref, rows_ref, sent_ref, wave_ref, back_ref
):
    levels, lon_count, group_count, slot_count, parts, per_part, highest = dims
    channels = 3 * levels
    slot_total = highest + 1
    left = lane_count - channels
    sources = parts * group_count
    group = group_ref[0]
    lane = lax.broadcasted_iota(jnp.int32, (piece_rows, lane_count), 1)
    for source in range(sources):
        wave_ref[source * piece_rows : (source + 1) * piece_rows, :] = received_ref[
            source, :piece_rows, :
        ].astype(jnp.float32)
    first, second = [], []
    for band in range(parts):
        piece = received_ref[band * group_count + group].astype(jnp.float32)
        upper, lower = piece[:piece_rows], piece[piece_rows:]
        start = pltpu.roll(upper, left, 1)
        rest = pltpu.roll(lower, (lane_count - (slot_total - left)) % lane_count, 1)
        first.append(jnp.where(lane < left, start, jnp.where(lane < slot_total, rest, 0.0)))
        second.append(jnp.where(lane < slot_total, lower, 0.0))
    bases = [jnp.concatenate(first, axis=0), jnp.concatenate(second, axis=0)]
    lane_row = lax.broadcasted_iota(jnp.int32, (1, lane_count), 1)
    is_last = lane_row >= 2 * levels
    depth_row = rows_ref[0:1, :]
    held = solve_ref.shape[1]
    basis_rows = [value.astype(jnp.bfloat16)[:, :held] for value in bases]
    every = []
    for index in range(per_part):
        basis_turned = bases[index].T[:held].astype(jnp.bfloat16)
        specs = []
        for half in range(2):
            waves = jnp.concatenate(
                [
                    wave_ref[
                        pl.ds((phase * 2 + half) * per_part + index, sources, stride=piece_rows), :
                    ]
                    for phase in range(2)
                ],
                axis=1,
            ).astype(jnp.bfloat16)
            specs.append(jnp.dot(basis_turned, waves, preferred_element_type=jnp.float32))
        every.append(specs)
    for index in range(per_part):
        specs, basis = every[index], basis_rows[index]
        lower_half = solve_ref[3 * index + 2] > 0.5
        solved = []
        for phase in range(2):
            lanes = slice(phase * lane_count, (phase + 1) * lane_count)
            spec = jnp.where(lower_half, specs[0][:, lanes], specs[1][:, lanes])
            thermal = pltpu.roll(spec, lane_count - levels, 1)
            quotient = (spec + solve_ref[3 * index + 1] * thermal) * solve_ref[3 * index]
            moved = pltpu.roll(quotient, levels, 1)
            solved.append(jnp.where(is_last, spec - depth_row * moved, quotient))
        for half in range(2):
            kept = jnp.concatenate(
                [
                    jnp.where(lower_half, value, 0.0)
                    if half == 0
                    else jnp.where(lower_half, 0.0, value)
                    for value in solved
                ],
                axis=1,
            ).astype(jnp.bfloat16)
            back = jnp.dot(basis, kept, preferred_element_type=jnp.float32)
            row = 1 + half * per_part + index
            doubling = rows_ref[row : row + 1, :]
            for phase in range(2):
                at = (phase * 2 + half) * per_part + index
                back_ref[pl.ds(at, sources, stride=piece_rows), :] = (
                    back[:, phase * lane_count : (phase + 1) * lane_count] * doubling
                )
    for source in range(sources):
        sent_ref[source] = back_ref[
            source * piece_rows : (source + 1) * piece_rows, :
        ].astype(jnp.bfloat16)


def synthesis_kernel(
    dims,
    received_ref,
    near_ref,
    far_ref,
    points_ref,
    out_hbm,
    wave_ref,
    rotated_ref,
    out_ref,
    sems,
):
    levels, lon_count, group_count, slot_count, parts, per_part, highest = dims
    channels = 3 * levels
    blocks = lon_count // lane_count
    sources = parts * group_count
    half_rows = 2 * per_part
    level_rows = 3 * blocks
    chunks = levels // piece_rows
    chunk_rows = piece_rows * level_rows
    for source in range(sources):
        wave_ref[source * piece_rows : (source + 1) * piece_rows, :] = received_ref[source].astype(
            jnp.float32
        )
    real, imag = (
        jnp.concatenate(
            [
                wave_ref[pl.ds(phase * half_rows + at, sources, stride=piece_rows), :]
                for at in range(half_rows)
            ],
            axis=0,
        ).T
        for phase in range(2)
    )
    real, imag = real[:channels], imag[:channels]
    tiles = near_ref.shape[0] // lane_count
    for block in range(blocks // tiles):
        far_real = far_ref[block : block + 1, :lane_count]
        far_imag = far_ref[block : block + 1, lane_count:]
        rotated_ref[block * channels : (block + 1) * channels, :] = jnp.concatenate(
            [real * far_real + imag * far_imag, imag * far_real - real * far_imag], axis=1
        ).astype(jnp.bfloat16)
    result = lax.dot_general(
        rotated_ref[...],
        near_ref[...],
        (((1,), (1,)), ((), ())),
        preferred_element_type=jnp.float32,
    )
    points = points_ref[0]
    lane = lax.broadcasted_iota(jnp.int32, (piece_rows, lane_count), 1)
    copies = []
    for chunk in range(chunks):
        for block in range(blocks):
            inside = lane < points - block * lane_count
            lanes = slice(block % tiles * lane_count, (block % tiles + 1) * lane_count)
            for field in range(3):
                at = block // tiles * channels + field * levels + chunk * piece_rows
                out_ref[chunk, pl.ds(field * blocks + block, piece_rows, stride=level_rows), :] = jnp.where(
                    inside, result[at : at + piece_rows, lanes], 0.0
                )
        rows = pl.ds(chunk * chunk_rows, chunk_rows)
        copies.append(pltpu.make_async_copy(out_ref.at[chunk], out_hbm.at[rows], sems.at[chunk]))
        copies[-1].start()
    for copy in copies:
        copy.wait()


def packed_body(
    dims,
    prognostic_arrays,
    coriolis,
    weights,
    row_points,
    owner_pairs,
    legendre,
    depths,
    diffusion,
):
    levels, lon_count, group_count, slot_count, parts, per_part, highest = dims
    channels = 3 * levels
    blocks = lon_count // lane_count
    sources = parts * group_count
    tiles = max(count for count in (1, 2, 3) if blocks % count == 0)
    span = tiles * lane_count
    far_rows = -(-(blocks // tiles) // piece_rows) * piece_rows
    chunks = levels // piece_rows
    slot_rows = -(-(highest + 1) // 16) * 16
    steps = pltpu.VMEM((span // piece_rows, 2 * lane_count), jnp.float32)
    in_vmem = pl.BlockSpec(memory_space=pltpu.VMEM)
    in_smem = pl.BlockSpec(memory_space=pltpu.SMEM)
    in_hbm = pl.BlockSpec(memory_space=pltpu.HBM)
    params = pltpu.CompilerParams(vmem_limit_bytes=16 << 20)
    grid = prognostic_arrays.reshape(channels * blocks, lane_count)
    basis = jnp.swapaxes(legendre, 2, 3)
    part = lax.axis_index("lat").astype(jnp.int32).reshape(1)
    group = lax.axis_index("lev").astype(jnp.int32).reshape(1)
    sent, near, far, solve, rows = pl.pallas_call(
        functools.partial(analysis_kernel, dims),
        name="analysis",
        out_shape=(
            pltpu.VMEM((sources, 2 * piece_rows, lane_count), jnp.bfloat16),
            pltpu.VMEM((span, 2 * lane_count), jnp.bfloat16),
            pltpu.VMEM((far_rows, 2 * lane_count), jnp.float32),
            pltpu.VMEM((3 * per_part, slot_rows, lane_count), jnp.float32),
            pltpu.VMEM((piece_rows, lane_count), jnp.float32),
        ),
        in_specs=[in_hbm] + [in_smem] * 5 + [in_hbm] * 4,
        out_specs=(in_vmem,) * 5,
        scratch_shapes=[
            pltpu.VMEM(grid.shape, jnp.float32),
            pltpu.VMEM(owner_pairs.shape, jnp.int32),
            pltpu.VMEM(basis.shape, jnp.bfloat16),
            pltpu.VMEM((1, levels), jnp.float32),
            pltpu.VMEM((1, levels), jnp.float32),
            steps,
            pltpu.VMEM((blocks // tiles * channels, span), jnp.bfloat16),
            pltpu.VMEM((sources * piece_rows, lane_count), jnp.float32),
            pltpu.SemaphoreType.DMA((4 + chunks,)),
        ],
        compiler_params=pltpu.CompilerParams(vmem_limit_bytes=67043328 - (2000 << 10)),
    )(
        grid,
        coriolis,
        weights,
        row_points,
        part,
        group,
        owner_pairs,
        basis,
        depths.reshape(1, levels),
        diffusion.reshape(1, levels),
    )
    received = lax.all_to_all(sent, ("lat", "lev"), split_axis=0, concat_axis=0, tiled=True)
    solved = pl.pallas_call(
        functools.partial(spectral_kernel, dims),
        name="spectral",
        out_shape=jax.ShapeDtypeStruct((sources, piece_rows, lane_count), jnp.bfloat16),
        in_specs=[in_vmem, in_smem, in_vmem, in_vmem],
        out_specs=in_vmem,
        scratch_shapes=[pltpu.VMEM((sources * piece_rows, lane_count), jnp.float32)] * 2,
        compiler_params=params,
    )(received, group, solve, rows)
    returned = lax.all_to_all(solved, ("lat", "lev"), split_axis=0, concat_axis=0, tiled=True)
    updated = pl.pallas_call(
        functools.partial(synthesis_kernel, dims),
        name="synthesis",
        out_shape=jax.ShapeDtypeStruct((channels * blocks, lane_count), jnp.float32),
        in_specs=[in_vmem, in_vmem, in_vmem, in_smem],
        out_specs=in_hbm,
        scratch_shapes=[
            pltpu.VMEM((sources * piece_rows, lane_count), jnp.float32),
            pltpu.VMEM((blocks // tiles * channels, 2 * lane_count), jnp.bfloat16),
            pltpu.VMEM((chunks, channels * blocks // chunks, lane_count), jnp.float32),
            pltpu.SemaphoreType.DMA((chunks,)),
        ],
        compiler_params=params,
    )(returned, near, far, row_points)
    return updated.reshape(prognostic_arrays.shape)


def body(prognostic_arrays, coriolis, weights, row_points, owner_pairs, legendre, depths, diffusion):
    levels, _, row_count, lon_count = prognostic_arrays.shape
    group_count, slot_count = owner_pairs.shape
    slot_total, band_rows = legendre.shape[2:]
    parts = lax.axis_size("lat")
    per_part = -(-slot_count // parts)
    channels = 3 * levels
    fits = (
        row_count == 1
        and band_rows == piece_rows == group_count
        and 4 * per_part == piece_rows
        and slot_count % per_part == 0
        and lon_count % lane_count == 0
        and 2 * per_part * parts * group_count == lane_count
        and levels % 16 == 0
        and channels < slot_total <= lane_count
        and 2 * slot_total + channels <= 2 * lane_count
        and lon_count * slot_total < 2**24
    )
    arguments = (
        prognostic_arrays, coriolis, weights, row_points, owner_pairs, legendre, depths, diffusion
    )
    if not fits:
        return general_body(*arguments)
    dims = (levels, lon_count, group_count, slot_count, parts, per_part, slot_total - 1)
    return packed_body(dims, *arguments)


def solution(mesh):
    in_specs = (
        P(None, None, ("lat", "lev"), None),
        P(("lat", "lev")),
        P(("lat", "lev")),
        P(("lat", "lev")),
        P(),
        P("lev", None, None, "lat"),
        P(),
        P(),
    )
    out_specs = P(None, None, ("lat", "lev"), None)
    return jax.shard_map(body, mesh=mesh, in_specs=in_specs, out_specs=out_specs, check_vma=False)
```
